512 devices in a mesh: elem: 32 (over x_lo, z), band: 16 (over x_hi, y, core).
Axes of the slice: x: 4 (x_hi: 2, x_lo: 2; x = x_hi * 2 + x_lo), y: 4, z: 16, core: 2. Of those that a mesh axis runs over, the one named last changes fastest.
Arguments:
- basis_sizes: int32 [512], P('elem'), may hold values from 96 to 160, as said below
- coupling_pattern: int32 [512], P('elem'), may hold values 0 or 1
- h_diag: bfloat16 [512, 160, 160], P('elem'), may hold values from -0.6708204 to 0.6708204, as said below
- h_couple: bfloat16 [512, 160, 160], P('elem'), may hold values from -0.25 to 0.25
- bands: bfloat16 [1024, 81920], P('band', 'elem'), may hold values from -1500 to 1500
Outputs:
- filtered: bfloat16 [1024, 81920], P('band', 'elem')
The draws below stay inside these ranges and needn't reach their ends.
Inputs may be any that keep to these rules, and one draw needn't show every extreme that they name: `basis_sizes`: every element has between 96 and 160 basis functions; some element has exactly 160 and some exactly 96. `h_diag`: each block is symmetric.
All inputs are finite; a program needn't handle non-finite values. No bound on the sum of `coupling_pattern` on one device may be relied on, other than what follows from the above.
Results may differ from the reference program's by a relative error of at most 0.0085.
Values may be sent and summed in bfloat16 or wider, within the bound.
A program may use at most 64 MiB of HBM per device.

```python
import math
import jax
import jax.numpy as jnp
from jax import lax

NB = 160
NB_MIN = 96
BANDS = 1024
DEGREE = 6
E = 512


def draw_basis_sizes(key, part):
    key_counts = jax.random.fold_in(key, 11)
    key_largest = jax.random.fold_in(key, 12)
    key_offset = jax.random.fold_in(key, 13)
    counts_drawn = jax.random.randint(key_counts, (E,), NB_MIN, NB + 1)
    largest = jax.random.randint(key_largest, (), 0, E)
    offset_draw = jax.random.randint(key_offset, (), 1, E)
    smallest = (largest + offset_draw) % E
    counts_drawn = counts_drawn.at[largest].set(NB)
    counts_drawn = counts_drawn.at[smallest].set(NB_MIN)
    return counts_drawn.astype(jnp.int32)


def draw_h_diag(key, part):
    noise_key = jax.random.fold_in(key, 23)
    raw_noise = jnp.clip(jax.random.normal(noise_key, (E, NB, NB), jnp.float32), -6.0, 6.0)
    scaled = raw_noise * (2.0 * NB) ** (-0.5)
    return (scaled + jnp.swapaxes(scaled, 1, 2)).astype(jnp.bfloat16)


def draw_bands(key, part):
    noise_key = jax.random.fold_in(key, 37)
    element_key = jax.random.fold_in(key, 41)
    band_key = jax.random.fold_in(key, 43)
    heavy_key = jax.random.fold_in(key, 47)
    second_key = jax.random.fold_in(key, 53)
    noise_values = jnp.clip(jax.random.normal(noise_key, (BANDS, E, NB), jnp.float32), -6.0, 6.0)
    upper_scale = 10.0
    element_scale = jnp.exp(jax.random.uniform(element_key, (E,), jnp.float32, 0.0, math.log(upper_scale)))
    first_heavy = jax.random.randint(heavy_key, (), 0, E)
    second_heavy = (first_heavy + jax.random.randint(second_key, (), 1, E)) % E
    element_ids = lax.broadcasted_iota(jnp.int32, (E,), 0)
    heavy_mask = (element_ids == first_heavy) | (element_ids == second_heavy)
    element_scale = jnp.where(heavy_mask, 60.0, element_scale)
    band_scale = jnp.exp(jax.random.uniform(band_key, (BANDS,), jnp.float32, 0.0, math.log(4.0)))
    values = noise_values * element_scale[None, :, None] * band_scale[:, None, None]
    return values.reshape(BANDS, E * NB).astype(jnp.bfloat16)


def place_ends(values, own_key, low, high):
    extent = values.shape
    index_at = [jax.random.randint(jax.random.fold_in(own_key, axis), (), 0, extent[axis]) for axis in range(len(extent))]
    values = values.at[tuple(index_at)].set(low)
    longest = extent.index(max(extent))
    index_at[longest] = (index_at[longest] + 1) % extent[longest]
    return values.at[tuple(index_at)].set(high)


def levels(rng, shape, cuts, least, top_value):
    factor_of = 1.0
    for dim, blocks in cuts:
        heights = jax.random.uniform(jax.random.fold_in(jax.random.fold_in(rng, 6), dim), (blocks,), jnp.float32, least / len(cuts), top_value / len(cuts))
        factor_of = factor_of * jnp.repeat(jnp.exp(heights), shape[dim] // blocks).reshape((-1,) + (1,) * (len(shape) - 1 - dim))
    return factor_of


def normal_values(rng, extent, deviation, limit, pieces=(), kind=jnp.bfloat16):
    entries = deviation * jax.random.normal(rng, extent, jnp.float32)
    if pieces:
        entries = entries * levels(rng, extent, pieces, -0.22, 0.18)
    return jnp.clip(entries, -limit, limit).astype(kind)


def setup_inputs(seed: int = 0) -> dict:
    key_of = jax.random.split(jax.random.key(seed), 6)
    return {
        "basis_sizes": draw_basis_sizes(jax.random.fold_in(key_of[5], 71), 0),
        "coupling_pattern": place_ends((jax.random.randint(key_of[1], (E,), 0, 4) < 3).astype(jnp.int32), jax.random.fold_in(key_of[1], 1), 0, 1),
        "h_diag": draw_h_diag(jax.random.fold_in(key_of[5], 71), 0),
        "h_couple": normal_values(key_of[3], (E, NB, NB), (4 * NB) ** -0.5, 0.25, ((0, 32),)),
        "bands": draw_bands(jax.random.fold_in(key_of[5], 71), 0),
    }


center_shift = 0.4
half_width = 2.8
epsilon_norm = 1e-06

def hamiltonian(vectors, diagonal_blocks, coupling, valid_rows):
    local_term = jnp.einsum('eij,bej->bei', diagonal_blocks, vectors)
    ahead_rows = jnp.roll(vectors, -1, axis=1)
    upper_term = jnp.einsum('eij,bej->bei', coupling, ahead_rows)
    carried = jnp.einsum('eji,bej->bei', coupling, vectors)
    lower_term = jnp.roll(carried, 1, axis=1)
    return (local_term + upper_term + lower_term) * valid_rows[None]

def reference(basis_sizes, coupling_pattern, h_diag, h_couple, bands):
    columns = lax.broadcasted_iota(jnp.int32, (E, NB), 1)
    valid_rows = (columns < basis_sizes[:, None]).astype(jnp.float32)
    diagonal_blocks = h_diag.astype(jnp.float32)
    coupling = h_couple.astype(jnp.float32) * coupling_pattern.astype(jnp.float32)[:, None, None]
    current = (bands.reshape(BANDS, E, NB).astype(jnp.float32) * valid_rows[None]).astype(jnp.bfloat16)
    previous = current
    for degree in range(DEGREE):
        current_float = current.astype(jnp.float32)
        applied = hamiltonian(current_float, diagonal_blocks, coupling, valid_rows)
        shifted = applied - center_shift * current_float
        if degree == 0:
            following = shifted / half_width
        else:
            following = 2.0 * shifted / half_width - previous.astype(jnp.float32)
        previous, current = (current, following.astype(jnp.bfloat16))
    filtered = current.reshape(BANDS, E * NB)
    gram = jnp.dot(filtered, filtered.T, preferred_element_type=jnp.float32)
    scales = lax.rsqrt(jnp.diagonal(gram) + epsilon_norm)
    normed = scales[:, None] * gram * scales[None, :]
    identity = jnp.eye(BANDS, dtype=jnp.float32)
    weights = (math.sqrt(E * NB) * scales[:, None] * (1.5 * identity - 0.5 * normed)).astype(jnp.bfloat16)
    return jnp.dot(weights.T, filtered, preferred_element_type=jnp.float32).astype(jnp.bfloat16)
```

```python
import functools
import math

import jax
import jax.numpy as jnp
from jax import lax
from jax.experimental import pallas as pl
from jax.experimental.pallas import tpu as pltpu
from jax.sharding import PartitionSpec as P

MESH = pl.DeviceIdType.MESH
DEGREE = 6
CENTER = 0.4
HALF = 2.8
EPS = 1e-06
F32 = jnp.float32
BF16 = jnp.bfloat16

NB = 160
PAD = 256
NE = 8
ROWS = 128
HALFROWS = 64
COLS = NE * NB
ZL = 4
ZN = 16
XL = 2
NY = 4
CHIPS = 8
BANDS = ROWS * CHIPS


def nt_dot(a, b):
    return lax.dot_general(a, b, (((1,), (1,)), ((), ())), preferred_element_type=F32)


def kernel(
    total_rows,
    sizes,
    pattern,
    hd,
    hc,
    bands,
    out,
    wts,
    buf,
    dbuf,
    cbuf,
    csend,
    cprev,
    raw,
    fall,
    strip,
    s1,
    r1,
    s2,
    r2,
    s3,
    r3,
    s4,
    r4,
    sqs,
    sqr,
    wfull,
    obuf,
    local_sem,
    halo_send,
    halo_recv,
    gat_send,
    gat_recv,
    red_send,
    red_recv,
    sq_send,
    sq_recv,
):
    e = lax.axis_index("elem")
    b = lax.axis_index("band")
    ne = lax.axis_size("elem")
    core = b % 2
    other = 1 - core
    chip = b // 2
    xh = chip // NY
    y = chip % NY
    xl = e // ZN
    z = e % ZN
    zh = z // ZL
    zl = z % ZL

    def at(e_, b_):
        return (e_, b_)

    partner = at(e, chip * 2 + other)
    left = at((e + ne - other) % ne, chip * 2 + other)
    right = at((e + core) % ne, chip * 2 + other)
    xpeer = at(e, ((1 - xh) * NY + y) * 2 + core)
    yup = at(e, (xh * NY + (y + 1) % NY) * 2 + core)
    ydn = at(e, (xh * NY + (y + NY - 1) % NY) * 2 + core)
    xlpeer = at((1 - xl) * ZN + z, b)
    near = [at(xl * ZN + zh * ZL + (zl + j) % ZL, b) for j in range(1, ZL)]
    far = [at(xl * ZN + ((zh + j) % ZL) * ZL + zl, b) for j in range(1, ZL)]

    barrier = pltpu.get_barrier_semaphore()
    friends = [left, right, xpeer, yup, ydn, xlpeer] + near + far
    for who in friends:
        pl.semaphore_signal(barrier, inc=1, device_id=who, device_id_type=MESH)

    def remote(src, dst, ss, rs, who):
        return pltpu.make_async_remote_copy(
            src_ref=src, dst_ref=dst, send_sem=ss, recv_sem=rs, device_id=who, device_id_type=MESH
        )

    mine = pl.ds(pl.multiple_of(core * COLS, 128), COLS)
    theirs = pl.ds(pl.multiple_of(other * COLS, 128), COLS)
    my_rows = pl.ds(pl.multiple_of(core * HALFROWS, HALFROWS), HALFROWS)
    other_rows = pl.ds(pl.multiple_of(other * HALFROWS, HALFROWS), HALFROWS)
    my_elems = pl.ds(core * NE, NE)

    load_c = pltpu.make_async_copy(hc.at[my_elems], cbuf, local_sem.at[0])
    load_d = pltpu.make_async_copy(hd.at[my_elems], dbuf, local_sem.at[1])
    load_v = pltpu.make_async_copy(bands.at[:, mine], raw.at[my_rows], local_sem.at[2])
    load_c.start()
    load_v.start()
    load_d.start()

    def size_of(i):
        return sizes[core * NE + i]

    lanes_nb = lax.broadcasted_iota(jnp.int32, (NB, NB), 1)
    eye = (lax.broadcasted_iota(jnp.int32, (NB, NB), 0) == lanes_nb).astype(BF16)

    wts[...] = jnp.zeros_like(wts)
    load_c.wait()

    def coupled(i):
        on = jnp.full((NB, NB), pattern[core * NE + i], jnp.int32) != 0
        return jnp.where(on, cbuf[i].astype(F32), 0.0)

    csend[...] = coupled(NE - 1).astype(BF16)
    load_d.wait()
    for i in range(NE):
        keep = lanes_nb < size_of(i)
        wts[i, PAD : PAD + NB, 0:NB] = jnp.where(keep, dbuf[i].astype(F32), 0.0).astype(BF16)
        pc = coupled(i)
        turned = nt_dot(eye, pc.astype(BF16))
        wts[i, 2 * PAD : 2 * PAD + NB, 0:NB] = jnp.where(keep, turned, 0.0).astype(BF16)
        if i + 1 < NE:
            keep_next = lanes_nb < size_of(i + 1)
            wts[i + 1, 0:NB, 0:NB] = jnp.where(keep_next, pc, 0.0).astype(BF16)

    pl.semaphore_wait(barrier, len(friends))

    swap = remote(bands.at[:, theirs], raw.at[my_rows], gat_send.at[9], gat_recv.at[9], partner)
    swap.start()
    pass_c = remote(csend, cprev, gat_send.at[10], gat_recv.at[10], right)
    pass_c.start()

    def slot(i):
        return slice(PAD * i, PAD * (i + 1))

    def halo(m, side):
        v = buf.at[m % 2]
        if side == 0:
            src, dst, who = v.at[:, slot(1)], v.at[:, slot(NE + 1)], left
        else:
            src, dst, who = v.at[:, slot(NE)], v.at[:, slot(0)], right
        return remote(src, dst, halo_send.at[m % 2, side], halo_recv.at[m % 2, side], who)

    load_v.wait()
    swap.wait_recv()
    lanes_pad = lax.broadcasted_iota(jnp.int32, (ROWS, PAD), 1)

    def expand(i):
        start = (NB * i) // 128 * 128
        off = NB * i - start
        x = raw[:, start : start + PAD].astype(F32)
        if off:
            x = pltpu.roll(x, PAD - off, 1)
        buf[0, :, slot(i + 1)] = jnp.where(lanes_pad < size_of(i), x, 0.0).astype(BF16)

    expand(0)
    halo(0, 0).start()
    expand(NE - 1)
    halo(0, 1).start()
    for i in range(1, NE - 1):
        expand(i)
    pass_c.wait_recv()
    wts[0, 0:NB, 0:NB] = jnp.where(lanes_nb < size_of(0), cprev[...].astype(F32), 0.0).astype(BF16)

    def element(t, i):
        now, then = t % 2, (t + 1) % 2
        acc = jnp.dot(
            buf[now, :, PAD * i : PAD * (i + 3)], wts[i], preferred_element_type=F32
        )
        shifted = acc - CENTER * buf[now, :, slot(i + 1)].astype(F32)
        if t == 0:
            nxt = shifted * (1.0 / HALF)
        else:
            nxt = shifted * (2.0 / HALF) - buf[then, :, slot(i + 1)].astype(F32)
        buf[then, :, slot(i + 1)] = nxt.astype(BF16)

    for t in range(DEGREE):
        halo(t, 1).wait_recv()
        if t >= 1:
            halo(t - 1, 0).wait_send()
        element(t, 0)
        if t + 1 < DEGREE:
            halo(t + 1, 0).start()
        halo(t, 0).wait_recv()
        if t >= 1:
            halo(t - 1, 1).wait_send()
        element(t, NE - 1)
        if t + 1 < DEGREE:
            halo(t + 1, 1).start()
        for i in range(1, NE - 1):
            element(t, i)

    final = DEGREE % 2
    chunks = {}
    for i in range(NE):
        start = (NB * i) // 128
        off = NB * i - 128 * start
        x = buf[final, :, slot(i + 1)].astype(F32)
        if off:
            x = pltpu.roll(x, off, 1)
        for k in range(2):
            part = x[:, 128 * k : 128 * (k + 1)]
            at_chunk = start + k
            chunks[at_chunk] = chunks[at_chunk] + part if at_chunk in chunks else part
        done_to = COLS // 128 if i == NE - 1 else (NB * (i + 1)) // 128
        for c in sorted(chunks):
            if c < done_to:
                fall[chip, :, 128 * c : 128 * (c + 1)] = chunks.pop(c).astype(BF16)

    def block(h_, y_):
        return h_ * NY + y_

    y_up, y_dn, y_far = (y + 1) % NY, (y + NY - 1) % NY, (y + 2) % NY
    ox = 1 - xh
    low, high = slice(0, HALFROWS), slice(HALFROWS, ROWS)

    def gather(k, src, who):
        return remote(src, src, gat_send.at[k], gat_recv.at[k], who)

    own = fall.at[chip]
    sends = [gather(0, own, xpeer), gather(1, own, yup), gather(2, own, ydn)]
    for copy in sends:
        copy.start()

    r128 = lax.broadcasted_iota(jnp.int32, (ROWS, ROWS), 0)
    c128 = lax.broadcasted_iota(jnp.int32, (ROWS, ROWS), 1)
    r8 = lax.broadcasted_iota(jnp.int32, (CHIPS, ROWS), 0)
    mine_f = fall.at[chip]
    sqs[0] = jnp.zeros((CHIPS, ROWS), F32)

    def gram(g):
        there = fall[g]
        strip[:, pl.ds(pl.multiple_of(g * ROWS, ROWS), ROWS)] = nt_dot(mine_f[...], there)
        square = nt_dot(there, there)
        diag = jnp.sum(jnp.where(r128 == c128, square, 0.0), axis=0, keepdims=True)
        sqs[0] = jnp.where(r8 == g, diag, sqs[0])

    gram(chip)
    sends[1].wait_recv()
    sends.append(gather(3, fall.at[block(xh, y_dn), low], yup))
    sends[3].start()
    gram(block(xh, y_dn))
    sends[2].wait_recv()
    sends.append(gather(4, fall.at[block(xh, y_up), high], ydn))
    sends[4].start()
    gram(block(xh, y_up))
    sends[0].wait_recv()
    sends.append(gather(5, fall.at[block(ox, y)], yup))
    sends.append(gather(6, fall.at[block(ox, y)], ydn))
    sends[5].start()
    sends[6].start()
    gram(block(ox, y))
    sends[3].wait_recv()
    sends[4].wait_recv()
    gram(block(xh, y_far))
    sends[5].wait_recv()
    sends.append(gather(7, fall.at[block(ox, y_dn), low], yup))
    sends[7].start()
    gram(block(ox, y_dn))
    sends[6].wait_recv()
    sends.append(gather(8, fall.at[block(ox, y_up), high], ydn))
    sends[8].start()
    gram(block(ox, y_up))
    sends[7].wait_recv()
    sends[8].wait_recv()
    gram(block(ox, y_far))

    def stage(k, src, dst, who):
        return remote(src, dst, red_send.at[k], red_recv.at[k], who)

    def squares(k, s, who):
        return remote(sqs.at[s], sqr.at[k], sq_send.at[k], sq_recv.at[k], who)

    s1[...] = strip[other_rows, :].astype(BF16)
    copies = [stage(0, s1, r1, partner), squares(0, 0, partner)]
    for copy in copies:
        copy.start()
    for copy in copies:
        copy.wait_recv()
    half = strip.at[my_rows]
    half[...] = half[...] + r1[...].astype(F32)
    sqs[1] = sqs[0] + sqr[0]
    sends += copies

    quarter = HALFROWS // XL
    rest = strip.at[pl.ds(pl.multiple_of(core * HALFROWS + (1 - xl) * quarter, quarter), quarter)]
    row0 = pl.multiple_of(core * HALFROWS + xl * quarter, quarter)
    piece_rows = pl.ds(row0, quarter)
    s2[...] = rest[...].astype(BF16)
    copies = [stage(1, s2, r2, xlpeer), squares(1, 1, xlpeer)]
    for copy in copies:
        copy.start()
    for copy in copies:
        copy.wait_recv()
    piece = strip.at[piece_rows]
    total = piece[...] + r2[...].astype(F32)
    piece[...] = total
    s3[...] = total.astype(BF16)
    sqs[2] = sqs[1] + sqr[1]
    sends += copies

    width = BANDS // ZL
    my_cols = pl.ds(pl.multiple_of(zl * width, width), width)
    copies = []
    for j in range(1, ZL):
        cols = pl.ds(pl.multiple_of(((zl + j) % ZL) * width, width), width)
        copies.append(stage(1 + j, s3.at[:, cols], r3.at[j - 1], near[j - 1]))
        copies.append(squares(1 + j, 2, near[j - 1]))
    for copy in copies:
        copy.start()
    for copy in copies:
        copy.wait_recv()
    total = piece[:, my_cols]
    sq = sqs[2]
    for j in range(1, ZL):
        total = total + r3[j - 1].astype(F32)
        sq = sq + sqr[1 + j]
    s4[...] = total.astype(BF16)
    sqs[3] = sq
    sends += copies

    copies = []
    for j in range(1, ZL):
        copies.append(stage(4 + j, s4, r4.at[j - 1], far[j - 1]))
        copies.append(squares(4 + j, 3, far[j - 1]))
    for copy in copies:
        copy.start()
    for copy in copies:
        copy.wait_recv()
    for j in range(1, ZL):
        total = total + r4[j - 1].astype(F32)
        sq = sq + sqr[4 + j]
    sends += copies

    scale = lax.rsqrt(sq + EPS)
    ri = lax.broadcasted_iota(jnp.int32, (quarter, ROWS), 0) + row0
    ci = lax.broadcasted_iota(jnp.int32, (quarter, ROWS), 1)
    same = ri == ci

    def row_of(table, g):
        return jnp.sum(jnp.where(r8 == g, table, 0.0), axis=0, keepdims=True)

    own_scale = jnp.sum(jnp.where(same, row_of(scale, chip), 0.0), axis=1, keepdims=True)
    for k in range(width // ROWS):
        g = zl * (width // ROWS) + k
        scale_row = row_of(scale, g)
        unit = jnp.logical_and(same, jnp.full(same.shape, g - chip, jnp.int32) == 0)
        value = total[:, ROWS * k : ROWS * (k + 1)]
        value = jnp.where(unit, row_of(sq, g), value)
        normed = own_scale * value * scale_row
        w = math.sqrt(total_rows) * scale_row * (jnp.where(unit, 1.5, 0.0) - 0.5 * normed)
        wfull[piece_rows, pl.ds(pl.multiple_of(g * ROWS, ROWS), ROWS)] = w.astype(BF16)

    mine_w = wfull.at[piece_rows, my_cols]
    copies = [stage(7 + j, mine_w, mine_w, near[j - 1]) for j in range(1, ZL)]
    for copy in copies:
        copy.start()
    for copy in copies:
        copy.wait_recv()
    sends += copies
    mine_w = wfull.at[piece_rows]
    copy = stage(11, mine_w, mine_w, xlpeer)
    copy.start()
    copy.wait_recv()
    sends.append(copy)
    mine_w = wfull.at[my_rows]
    copy = stage(12, mine_w, mine_w, partner)
    copy.start()
    copy.wait_recv()
    sends.append(copy)

    whole = fall.reshape(BANDS, COLS)
    for k in range(COLS // PAD):
        obuf[:, PAD * k : PAD * (k + 1)] = jnp.dot(
            wfull[...], whole[:, PAD * k : PAD * (k + 1)], preferred_element_type=F32
        ).astype(BF16)
    give = remote(
        obuf.at[other_rows], out.at[:, mine], gat_send.at[11], gat_recv.at[11], partner
    )
    give.start()
    keep_own = pltpu.make_async_copy(obuf.at[my_rows], out.at[:, mine], local_sem.at[3])
    keep_own.start()
    for copy in sends:
        copy.wait_send()
    swap.wait_send()
    pass_c.wait_send()
    halo(DEGREE - 1, 0).wait_send()
    halo(DEGREE - 1, 1).wait_send()
    keep_own.wait()
    give.wait()


def shards(basis_sizes, coupling_pattern, h_diag, h_couple, bands):
    total_rows = h_diag.shape[0] * lax.axis_size("elem") * h_diag.shape[1]
    smem = pl.BlockSpec(memory_space=pltpu.SMEM)
    hbm = pl.BlockSpec(memory_space=pl.ANY)
    dma = pltpu.SemaphoreType.DMA
    quarter = HALFROWS // XL
    width = BANDS // ZL
    return pl.pallas_call(
        functools.partial(kernel, total_rows),
        out_shape=jax.ShapeDtypeStruct(bands.shape, BF16),
        in_specs=[smem, smem, hbm, hbm, hbm],
        out_specs=hbm,
        scratch_shapes=[
            pltpu.VMEM((NE, 3 * PAD, PAD), BF16),
            pltpu.VMEM((2, ROWS, PAD * (NE + 2)), BF16),
            pltpu.VMEM((NE, NB, NB), BF16),
            pltpu.VMEM((NE, NB, NB), BF16),
            pltpu.VMEM((NB, NB), BF16),
            pltpu.VMEM((NB, NB), BF16),
            pltpu.VMEM((ROWS, COLS), BF16),
            pltpu.VMEM((CHIPS, ROWS, COLS), BF16),
            pltpu.VMEM((ROWS, BANDS), F32),
            pltpu.VMEM((HALFROWS, BANDS), BF16),
            pltpu.VMEM((HALFROWS, BANDS), BF16),
            pltpu.VMEM((quarter, BANDS), BF16),
            pltpu.VMEM((quarter, BANDS), BF16),
            pltpu.VMEM((quarter, BANDS), BF16),
            pltpu.VMEM((ZL - 1, quarter, width), BF16),
            pltpu.VMEM((quarter, width), BF16),
            pltpu.VMEM((ZL - 1, quarter, width), BF16),
            pltpu.VMEM((4, CHIPS, ROWS), F32),
            pltpu.VMEM((8, CHIPS, ROWS), F32),
            pltpu.VMEM((ROWS, BANDS), BF16),
            pltpu.VMEM((ROWS, COLS), BF16),
            dma((4,)),
            dma((2, 2)),
            dma((2, 2)),
            dma((12,)),
            dma((12,)),
            dma((13,)),
            dma((13,)),
            dma((8,)),
            dma((8,)),
        ],
        compiler_params=pltpu.CompilerParams(
            collective_id=0, has_side_effects=True, vmem_limit_bytes=40 * 1024 * 1024
        ),
        name="filter_step",
    )(basis_sizes, coupling_pattern, h_diag, h_couple, bands)


def solution(mesh):
    in_specs = (
        P("elem"),
        P("elem"),
        P("elem", None, None),
        P("elem", None, None),
        P("band", "elem"),
    )
    out_specs = P("band", "elem")
    return jax.shard_map(shards, mesh=mesh, in_specs=in_specs, out_specs=out_specs, check_vma=False)
```

```python
import functools
import math

import jax
import jax.numpy as jnp
from jax import lax
from jax.experimental import pallas as pl
from jax.experimental.pallas import tpu as pltpu
from jax.sharding import PartitionSpec as P

MESH = pl.DeviceIdType.MESH
DEGREE = 6
CENTER = 0.4
HALF = 2.8
EPS = 1e-06
F32 = jnp.float32
BF16 = jnp.bfloat16

NB = 160
PAD = 256
NE = 8
ROWS = 128
HALFROWS = 64
COLS = NE * NB
ZL = 4
ZN = 16
XL = 2
NY = 4
CHIPS = 8
BANDS = ROWS * CHIPS
SIDE = ROWS * NY


def nt_dot(a, b):
    return lax.dot_general(a, b, (((1,), (1,)), ((), ())), preferred_element_type=F32)


def kernel(
    total_rows,
    sizes_hbm,
    pattern_hbm,
    hd,
    hc,
    bands,
    out,
    wts,
    buf,
    dbuf,
    cbuf,
    csend,
    cprev,
    raw,
    fall,
    strip,
    s1,
    r1,
    s2,
    r2,
    s3,
    r3,
    s4,
    sqs,
    sqr,
    wfull,
    obuf,
    sizes,
    pattern,
    local_sem,
    halo_send,
    halo_recv,
    gat_send,
    gat_recv,
    red_send,
    red_recv,
    sq_send,
    sq_recv,
):
    e = lax.axis_index("elem")
    b = lax.axis_index("band")
    ne = lax.axis_size("elem")
    core = b % 2
    other = 1 - core
    chip = b // 2
    xh = chip // NY
    y = chip % NY
    xl = e // ZN
    z = e % ZN
    zh = z // ZL
    zl = z % ZL

    def at(e_, b_):
        return (e_, b_)

    partner = at(e, chip * 2 + other)
    left = at((e + ne - other) % ne, chip * 2 + other)
    right = at((e + core) % ne, chip * 2 + other)
    xpeer = at(e, ((1 - xh) * NY + y) * 2 + core)
    yup = at(e, (xh * NY + (y + 1) % NY) * 2 + core)
    ydn = at(e, (xh * NY + (y + NY - 1) % NY) * 2 + core)
    places = [((xl + j // ZL) % XL) * ZN + zh * ZL + (zl + j) % ZL for j in range(XL * ZL)]
    near = [at(p, b) for p in places[1:]]
    across = [at(p, xpeer[1]) for p in places]
    far = [at(xl * ZN + ((zh + j) % ZL) * ZL + zl, b) for j in range(1, ZL)]

    barrier = pltpu.get_barrier_semaphore()
    friends = [left, right, yup, ydn] + near + across + far
    for who in friends:
        pl.semaphore_signal(barrier, inc=1, device_id=who, device_id_type=MESH)

    def remote(src, dst, ss, rs, who):
        return pltpu.make_async_remote_copy(
            src_ref=src, dst_ref=dst, send_sem=ss, recv_sem=rs, device_id=who, device_id_type=MESH
        )

    mine = pl.ds(pl.multiple_of(core * COLS, 128), COLS)
    theirs = pl.ds(pl.multiple_of(other * COLS, 128), COLS)
    my_rows = pl.ds(pl.multiple_of(core * HALFROWS, HALFROWS), HALFROWS)
    other_rows = pl.ds(pl.multiple_of(other * HALFROWS, HALFROWS), HALFROWS)
    my_elems = pl.ds(core * NE, NE)

    load_c = pltpu.make_async_copy(hc.at[my_elems], cbuf, local_sem.at[0])
    load_d = pltpu.make_async_copy(hd.at[my_elems], dbuf, local_sem.at[1])
    load_v = pltpu.make_async_copy(bands.at[:, mine], raw.at[my_rows], local_sem.at[2])
    load_s = pltpu.make_async_copy(sizes_hbm, sizes, local_sem.at[5])
    load_p = pltpu.make_async_copy(pattern_hbm, pattern, local_sem.at[6])
    for load in (load_s, load_p, load_c, load_d, load_v):
        load.start()

    def size_of(i):
        return sizes[core * NE + i]

    lanes_nb = lax.broadcasted_iota(jnp.int32, (NB, NB), 1)
    eye = (lax.broadcasted_iota(jnp.int32, (NB, NB), 0) == lanes_nb).astype(BF16)

    wts[...] = jnp.zeros_like(wts)
    load_s.wait()
    load_p.wait()
    load_c.wait()

    def coupled(i):
        on = jnp.full((NB, NB), pattern[core * NE + i], jnp.int32) != 0
        return jnp.where(on, cbuf[i].astype(F32), 0.0)

    csend[...] = coupled(NE - 1).astype(BF16)
    load_d.wait()
    for i in range(NE):
        keep = lanes_nb < size_of(i)
        wts[i, PAD : PAD + NB, 0:NB] = jnp.where(keep, dbuf[i].astype(F32), 0.0).astype(BF16)
        pc = coupled(i)
        turned = nt_dot(eye, pc.astype(BF16))
        wts[i, 2 * PAD : 2 * PAD + NB, 0:NB] = jnp.where(keep, turned, 0.0).astype(BF16)
        if i + 1 < NE:
            keep_next = lanes_nb < size_of(i + 1)
            wts[i + 1, 0:NB, 0:NB] = jnp.where(keep_next, pc, 0.0).astype(BF16)

    pl.semaphore_wait(barrier, len(friends))

    swap = remote(bands.at[:, theirs], raw.at[my_rows], gat_send.at[9], gat_recv.at[9], partner)
    swap.start()
    pass_c = remote(csend, cprev, gat_send.at[10], gat_recv.at[10], right)
    pass_c.start()

    def slot(i):
        return slice(PAD * i, PAD * (i + 1))

    def halo(m, side):
        v = buf.at[m % 2]
        if side == 0:
            src, dst, who = v.at[:, slot(1)], v.at[:, slot(NE + 1)], left
        else:
            src, dst, who = v.at[:, slot(NE)], v.at[:, slot(0)], right
        return remote(src, dst, halo_send.at[m % 2, side], halo_recv.at[m % 2, side], who)

    load_v.wait()
    swap.wait_recv()
    lanes_pad = lax.broadcasted_iota(jnp.int32, (ROWS, PAD), 1)

    def expand(i):
        start = (NB * i) // 128 * 128
        off = NB * i - start
        x = raw[:, start : start + PAD].astype(F32)
        if off:
            x = pltpu.roll(x, PAD - off, 1)
        buf[0, :, slot(i + 1)] = jnp.where(lanes_pad < size_of(i), x, 0.0).astype(BF16)

    expand(0)
    halo(0, 0).start()
    expand(NE - 1)
    halo(0, 1).start()
    for i in range(1, NE - 1):
        expand(i)
    pass_c.wait_recv()
    wts[0, 0:NB, 0:NB] = jnp.where(lanes_nb < size_of(0), cprev[...].astype(F32), 0.0).astype(BF16)

    def element(t, i):
        now, then = t % 2, (t + 1) % 2
        acc = jnp.dot(
            buf[now, :, PAD * i : PAD * (i + 3)], wts[i], preferred_element_type=F32
        )
        shifted = acc - CENTER * buf[now, :, slot(i + 1)].astype(F32)
        if t == 0:
            nxt = shifted * (1.0 / HALF)
        else:
            nxt = shifted * (2.0 / HALF) - buf[then, :, slot(i + 1)].astype(F32)
        buf[then, :, slot(i + 1)] = nxt.astype(BF16)

    for t in range(DEGREE):
        halo(t, 1).wait_recv()
        if t >= 1:
            halo(t - 1, 0).wait_send()
        element(t, 0)
        if t + 1 < DEGREE:
            halo(t + 1, 0).start()
        halo(t, 0).wait_recv()
        if t >= 1:
            halo(t - 1, 1).wait_send()
        element(t, NE - 1)
        if t + 1 < DEGREE:
            halo(t + 1, 1).start()
        for i in range(1, NE - 1):
            element(t, i)

    final = DEGREE % 2
    chunks = {}
    for i in range(NE):
        start = (NB * i) // 128
        off = NB * i - 128 * start
        x = buf[final, :, slot(i + 1)].astype(F32)
        if off:
            x = pltpu.roll(x, off, 1)
        for k in range(2):
            part = x[:, 128 * k : 128 * (k + 1)]
            at_chunk = start + k
            chunks[at_chunk] = chunks[at_chunk] + part if at_chunk in chunks else part
        done_to = COLS // 128 if i == NE - 1 else (NB * (i + 1)) // 128
        for c in sorted(chunks):
            if c < done_to:
                fall[chip, :, 128 * c : 128 * (c + 1)] = chunks.pop(c).astype(BF16)

    y_up, y_dn, y_far = (y + 1) % NY, (y + NY - 1) % NY, (y + 2) % NY
    peer_chip = (1 - xh) * NY + y
    side, far_side = xh * NY, (1 - xh) * NY
    low, high = slice(0, HALFROWS), slice(HALFROWS, ROWS)

    def gather(k, src, who):
        return remote(src, src, gat_send.at[k], gat_recv.at[k], who)

    own = fall.at[chip]
    sends = [gather(0, own, xpeer), gather(1, own, yup), gather(2, own, ydn)]
    for copy in sends:
        copy.start()

    r128 = lax.broadcasted_iota(jnp.int32, (ROWS, ROWS), 0)
    c128 = lax.broadcasted_iota(jnp.int32, (ROWS, ROWS), 1)
    r8 = lax.broadcasted_iota(jnp.int32, (CHIPS, ROWS), 0)
    sqs[0] = jnp.zeros((CHIPS, ROWS), F32)

    def cols_of(y_):
        return pl.ds(pl.multiple_of(y_ * ROWS, ROWS), ROWS)

    def norms(g):
        there = fall[g]
        square = nt_dot(there, there)
        diag = jnp.sum(jnp.where(r128 == c128, square, 0.0), axis=0, keepdims=True)
        sqs[0] = jnp.where(r8 == g, diag, sqs[0])

    def gram(part, g, y_):
        strip[part, :, cols_of(y_)] = nt_dot(fall[g], fall[side + y_])

    gram(0, chip, y)
    norms(chip)
    sends[1].wait_recv()
    sends.append(gather(3, fall.at[side + y_dn, low], yup))
    sends[3].start()
    gram(0, chip, y_dn)
    norms(side + y_dn)
    sends[2].wait_recv()
    sends.append(gather(4, fall.at[side + y_up, high], ydn))
    sends[4].start()
    gram(0, chip, y_up)
    norms(side + y_up)
    sends[3].wait_recv()
    sends[4].wait_recv()
    gram(0, chip, y_far)
    norms(side + y_far)
    sends[0].wait_recv()
    sends.append(gather(5, fall.at[peer_chip], yup))
    sends.append(gather(6, fall.at[peer_chip], ydn))
    sends[5].start()
    sends[6].start()
    for y_ in range(NY):
        gram(1, peer_chip, y_)
    norms(peer_chip)

    def stage(k, src, dst, who):
        return remote(src, dst, red_send.at[k], red_recv.at[k], who)

    def squares(k, s, who):
        return remote(sqs.at[s], sqr.at[k], sq_send.at[k], sq_recv.at[k], who)

    s1[...] = strip[:, other_rows, :].astype(BF16)
    copies = [stage(0, s1, r1, partner), squares(0, 0, partner)]
    for copy in copies:
        copy.start()
    for copy in copies:
        copy.wait_recv()
    half = strip[:, my_rows, :] + r1[...].astype(F32)
    strip[:, my_rows, :] = half
    s2[...] = half.astype(BF16)
    sqs[1] = sqs[0] + sqr[0]
    sends += copies

    quarter = HALFROWS // XL
    copies = []
    for j in range(1, XL * ZL):
        xl_, zl_ = (xl + j // ZL) % XL, (zl + j) % ZL
        rows = pl.ds(pl.multiple_of(xl_ * quarter, quarter), quarter)
        copies.append(stage(j, s2.at[:, rows, cols_of(zl_)], r2.at[j - 1], near[j - 1]))
        copies.append(squares(j, 1, near[j - 1]))
    for copy in copies:
        copy.start()
    row0 = pl.multiple_of(core * HALFROWS + xl * quarter, quarter)
    piece_rows = pl.ds(row0, quarter)
    total = strip[:, piece_rows, cols_of(zl)]
    sq = sqs[1]
    for copy in copies:
        copy.wait_recv()
    for j in range(1, XL * ZL):
        total = total + r2[j - 1].astype(F32)
        sq = sq + sqr[j]
    s3[...] = total.astype(BF16)
    sqs[2] = sq
    sends += copies

    copies = []
    for j in range(1, ZL):
        copies.append(stage(7 + j, s3, r3.at[j - 1], far[j - 1]))
        copies.append(squares(7 + j, 2, far[j - 1]))
    for copy in copies:
        copy.start()
    sends[5].wait_recv()
    late = [gather(7, fall.at[far_side + y_dn, low], yup)]
    late[0].start()
    sends[6].wait_recv()
    late.append(gather(8, fall.at[far_side + y_up, high], ydn))
    late[1].start()
    for copy in copies:
        copy.wait_recv()
    for j in range(1, ZL):
        total = total + r3[j - 1].astype(F32)
        sq = sq + sqr[7 + j]
    sends += copies + late

    scale = lax.rsqrt(sq + EPS)
    ri = lax.broadcasted_iota(jnp.int32, (quarter, ROWS), 0) + row0
    ci = lax.broadcasted_iota(jnp.int32, (quarter, ROWS), 1)
    same = ri == ci
    g = side + zl
    scale_row = jnp.sum(jnp.where(r8 == g, scale, 0.0), axis=0, keepdims=True)
    sq_row = jnp.sum(jnp.where(r8 == g, sq, 0.0), axis=0, keepdims=True)
    for part in range(2):
        of = chip if part == 0 else peer_chip
        lanes = jnp.sum(jnp.where(r8 == of, scale, 0.0), axis=0, keepdims=True)
        row_scale = jnp.sum(jnp.where(same, lanes, 0.0), axis=1, keepdims=True)
        value = total[part]
        ident = jnp.zeros_like(value)
        if part == 0:
            unit = jnp.logical_and(same, jnp.full(same.shape, zl - y, jnp.int32) == 0)
            value = jnp.where(unit, sq_row, value)
            ident = jnp.where(unit, 1.5, 0.0)
        normed = row_scale * value * scale_row
        w = math.sqrt(total_rows) * scale_row * (ident - 0.5 * normed)
        s4[part] = w.astype(BF16)

    g_cols = pl.ds(pl.multiple_of(g * ROWS, ROWS), ROWS)
    place = wfull.at[piece_rows, g_cols]
    put = pltpu.make_async_copy(s4.at[0], place, local_sem.at[4])
    put.start()
    copies = [stage(10 + j, s4.at[0], place, near[j - 1]) for j in range(1, XL * ZL)]
    copies += [stage(18 + j, s4.at[1], place, across[j]) for j in range(XL * ZL)]
    for copy in copies:
        copy.start()
    for copy in copies:
        copy.wait_recv()
    put.wait()
    sends += copies
    mine_w = wfull.at[my_rows]
    copy = stage(26, mine_w, mine_w, partner)
    copy.start()
    for waiting in late:
        waiting.wait_recv()
    copy.wait_recv()
    sends.append(copy)

    whole = fall.reshape(BANDS, COLS)
    for k in range(COLS // PAD):
        obuf[:, PAD * k : PAD * (k + 1)] = jnp.dot(
            wfull[...], whole[:, PAD * k : PAD * (k + 1)], preferred_element_type=F32
        ).astype(BF16)
    give = remote(
        obuf.at[other_rows], out.at[:, mine], gat_send.at[11], gat_recv.at[11], partner
    )
    give.start()
    keep_own = pltpu.make_async_copy(obuf.at[my_rows], out.at[:, mine], local_sem.at[3])
    keep_own.start()
    for copy in sends:
        copy.wait_send()
    swap.wait_send()
    pass_c.wait_send()
    halo(DEGREE - 1, 0).wait_send()
    halo(DEGREE - 1, 1).wait_send()
    keep_own.wait()
    give.wait()


def shards(basis_sizes, coupling_pattern, h_diag, h_couple, bands):
    total_rows = h_diag.shape[0] * lax.axis_size("elem") * h_diag.shape[1]
    hbm = pl.BlockSpec(memory_space=pltpu.HBM)
    dma = pltpu.SemaphoreType.DMA
    quarter = HALFROWS // XL
    return pl.pallas_call(
        functools.partial(kernel, total_rows),
        out_shape=jax.ShapeDtypeStruct(bands.shape, BF16),
        in_specs=[hbm] * 5,
        out_specs=hbm,
        scratch_shapes=[
            pltpu.VMEM((NE, 3 * PAD, PAD), BF16),
            pltpu.VMEM((2, ROWS, PAD * (NE + 2)), BF16),
            pltpu.VMEM((NE, NB, NB), BF16),
            pltpu.VMEM((NE, NB, NB), BF16),
            pltpu.VMEM((NB, NB), BF16),
            pltpu.VMEM((NB, NB), BF16),
            pltpu.VMEM((ROWS, COLS), BF16),
            pltpu.VMEM((CHIPS, ROWS, COLS), BF16),
            pltpu.VMEM((2, ROWS, SIDE), F32),
            pltpu.VMEM((2, HALFROWS, SIDE), BF16),
            pltpu.VMEM((2, HALFROWS, SIDE), BF16),
            pltpu.VMEM((2, HALFROWS, SIDE), BF16),
            pltpu.VMEM((XL * ZL - 1, 2, quarter, ROWS), BF16),
            pltpu.VMEM((2, quarter, ROWS), BF16),
            pltpu.VMEM((ZL - 1, 2, quarter, ROWS), BF16),
            pltpu.VMEM((2, quarter, ROWS), BF16),
            pltpu.VMEM((3, CHIPS, ROWS), F32),
            pltpu.VMEM((11, CHIPS, ROWS), F32),
            pltpu.VMEM((ROWS, BANDS), BF16),
            pltpu.VMEM((ROWS, COLS), BF16),
            pltpu.SMEM((2 * NE,), jnp.int32),
            pltpu.SMEM((2 * NE,), jnp.int32),
            dma((7,)),
            dma((2, 2)),
            dma((2, 2)),
            dma((12,)),
            dma((12,)),
            dma((27,)),
            dma((27,)),
            dma((11,)),
            dma((11,)),
        ],
        compiler_params=pltpu.CompilerParams(
            collective_id=0, has_side_effects=True, vmem_limit_bytes=67043328
        ),
        name="filter_step",
    )(basis_sizes, coupling_pattern, h_diag, h_couple, bands)


def solution(mesh):
    in_specs = (
        P("elem"),
        P("elem"),
        P("elem", None, None),
        P("elem", None, None),
        P("band", "elem"),
    )
    out_specs = P("band", "elem")
    return jax.shard_map(shards, mesh=mesh, in_specs=in_specs, out_specs=out_specs, check_vma=False)
```

```python
import functools
import math

import jax
import jax.numpy as jnp
from jax import lax
from jax.experimental import pallas as pl
from jax.experimental.pallas import tpu as pltpu
from jax.sharding import PartitionSpec as P

MESH = pl.DeviceIdType.MESH
DEGREE = 6
CENTER = 0.4
HALF = 2.8
EPS = 1e-06
F32 = jnp.float32
BF16 = jnp.bfloat16

NB = 160
PAD = 256
NE = 8
ROWS = 128
HALFROWS = 64
COLS = NE * NB
DEEP = 3
EDGE = 512
ZL = 4
ZN = 16
XL = 2
NY = 4
CHIPS = 8
BANDS = ROWS * CHIPS
SIDE = ROWS * NY


def nt_dot(a, b):
    return lax.dot_general(a, b, (((1,), (1,)), ((), ())), preferred_element_type=F32)


def kernel(
    total_rows,
    sizes_hbm,
    pattern_hbm,
    hd,
    hc,
    bands,
    out,
    wts,
    buf,
    dbuf,
    cbuf,
    raw,
    edges,
    fall,
    strip,
    s1,
    r1,
    s2,
    r2,
    s3,
    r3,
    s4,
    sqs,
    sqr,
    wfull,
    obuf,
    sizes,
    pattern,
    sizes_left,
    pattern_left,
    sizes_right,
    pattern_right,
    local_sem,
    ext_send,
    ext_recv,
    gat_send,
    gat_recv,
    red_send,
    red_recv,
    sq_send,
    sq_recv,
):
    e = lax.axis_index("elem")
    b = lax.axis_index("band")
    ne = lax.axis_size("elem")
    core = b % 2
    other = 1 - core
    chip = b // 2
    xh = chip // NY
    y = chip % NY
    xl = e // ZN
    z = e % ZN
    zh = z // ZL
    zl = z % ZL

    def at(e_, b_):
        return (e_, b_)

    partner = at(e, chip * 2 + other)
    left = at((e + ne - other) % ne, chip * 2 + other)
    right = at((e + core) % ne, chip * 2 + other)
    xpeer = at(e, ((1 - xh) * NY + y) * 2 + core)
    yup = at(e, (xh * NY + (y + 1) % NY) * 2 + core)
    ydn = at(e, (xh * NY + (y + NY - 1) % NY) * 2 + core)
    places = [((xl + j // ZL) % XL) * ZN + zh * ZL + (zl + j) % ZL for j in range(XL * ZL)]
    near = [at(p, b) for p in places[1:]]
    across = [at(p, xpeer[1]) for p in places]
    far = [at(xl * ZN + ((zh + j) % ZL) * ZL + zl, b) for j in range(1, ZL)]

    barrier = pltpu.get_barrier_semaphore()
    friends = [left, right, yup, ydn] + near + across + far
    for who in friends:
        pl.semaphore_signal(barrier, inc=1, device_id=who, device_id_type=MESH)

    def remote(src, dst, ss, rs, who):
        return pltpu.make_async_remote_copy(
            src_ref=src, dst_ref=dst, send_sem=ss, recv_sem=rs, device_id=who, device_id_type=MESH
        )

    mine = pl.ds(pl.multiple_of(core * COLS, 128), COLS)
    theirs = pl.ds(pl.multiple_of(other * COLS, 128), COLS)
    my_rows = pl.ds(pl.multiple_of(core * HALFROWS, HALFROWS), HALFROWS)
    other_rows = pl.ds(pl.multiple_of(other * HALFROWS, HALFROWS), HALFROWS)
    my_elems = pl.ds(core * NE, NE)

    own_c, own_d = slice(DEEP, DEEP + NE), slice(DEEP - 1, DEEP - 1 + NE)
    load_c = pltpu.make_async_copy(hc.at[my_elems], cbuf.at[own_c], local_sem.at[0])
    load_d = pltpu.make_async_copy(hd.at[my_elems], dbuf.at[own_d], local_sem.at[1])
    load_v = pltpu.make_async_copy(bands.at[:, mine], raw.at[my_rows], local_sem.at[2])
    load_s = pltpu.make_async_copy(sizes_hbm, sizes, local_sem.at[5])
    load_p = pltpu.make_async_copy(pattern_hbm, pattern, local_sem.at[6])
    for load in (load_s, load_p, load_c, load_d, load_v):
        load.start()

    def number(own_table, left_table, right_table, i):
        if i < 0:
            return left_table[other * NE + NE + i]
        if i >= NE:
            return right_table[other * NE + i - NE]
        return own_table[core * NE + i]

    def size_of(i):
        return number(sizes, sizes_left, sizes_right, i)

    def slot(i, n=1):
        return slice(PAD * (i + DEEP), PAD * (i + DEEP + n))

    lanes_nb = lax.broadcasted_iota(jnp.int32, (NB, NB), 1)
    eye = (lax.broadcasted_iota(jnp.int32, (NB, NB), 0) == lanes_nb).astype(BF16)

    def coupled(i):
        on = jnp.full((NB, NB), number(pattern, pattern_left, pattern_right, i), jnp.int32) != 0
        return jnp.where(on, cbuf[i + DEEP].astype(F32), 0.0)

    def put_weights(i, row, value):
        keep = lanes_nb < size_of(i)
        at_row = slice(row * PAD, row * PAD + NB)
        wts[i + DEEP - 1, at_row, 0:NB] = jnp.where(keep, value, 0.0).astype(BF16)

    def use_coupling(i):
        pc = coupled(i)
        if -DEEP + 1 <= i:
            put_weights(i, 2, nt_dot(eye, pc.astype(BF16)))
        if i + 1 < NE + DEEP - 1:
            put_weights(i + 1, 0, pc)

    def use_diagonal(i):
        put_weights(i, 1, dbuf[i + DEEP - 1].astype(F32))

    wts[...] = jnp.zeros_like(wts)
    for load in (load_s, load_p, load_c, load_d):
        load.wait()
    for i in range(NE):
        use_diagonal(i)
        if i + 1 < NE:
            use_coupling(i)

    pl.semaphore_wait(barrier, len(friends))

    def outer(k, src, dst, who):
        return remote(src, dst, ext_send.at[k], ext_recv.at[k], who)

    first, last = core * NE, core * NE + NE
    swap = remote(bands.at[:, theirs], raw.at[my_rows], gat_send.at[9], gat_recv.at[9], partner)
    swap.start()
    n_c, n_d = DEEP - 1, DEEP - 1
    blocks = [
        outer(0, sizes_hbm, sizes_left, right),
        outer(1, pattern_hbm, pattern_left, right),
        outer(2, hc.at[pl.ds(last - DEEP, DEEP)], cbuf.at[0:DEEP], right),
        outer(3, hd.at[pl.ds(last - n_d, n_d)], dbuf.at[0:n_d], right),
        outer(4, sizes_hbm, sizes_right, left),
        outer(5, pattern_hbm, pattern_right, left),
        outer(6, hc.at[pl.ds(first, n_c)], cbuf.at[DEEP + NE : DEEP + NE + n_c], left),
        outer(7, hd.at[pl.ds(first, n_d)], dbuf.at[n_d + NE : n_d + NE + n_d], left),
    ]
    for copy in blocks:
        copy.start()

    load_v.wait()
    swap.wait_recv()
    vectors = [
        outer(8, raw.at[:, COLS - EDGE : COLS], edges.at[0], right),
        outer(9, raw.at[:, 0:EDGE], edges.at[1], left),
    ]
    for copy in vectors:
        copy.start()

    lanes_pad = lax.broadcasted_iota(jnp.int32, (ROWS, PAD), 1)

    def expand(i, ref, column):
        start = column // 128 * 128
        off = column - start
        x = ref[:, start : start + PAD].astype(F32)
        if off:
            x = pltpu.roll(x, PAD - off, 1)
        buf[0, :, slot(i)] = jnp.where(lanes_pad < size_of(i), x, 0.0).astype(BF16)

    for i in range(NE):
        expand(i, raw, NB * i)

    def element(t, i):
        now, prior, targets = [
            (0, None, [1]),
            (1, 0, [0, 2]),
            (0, 1, [1, 3]),
            (3, 2, [2]),
            (2, 3, [3]),
            (3, 2, [2]),
        ][t]
        acc = jnp.dot(
            buf[now, :, slot(i - 1, 3)], wts[i + DEEP - 1], preferred_element_type=F32
        )
        shifted = acc - CENTER * buf[now, :, slot(i)].astype(F32)
        if t == 0:
            nxt = shifted * (1.0 / HALF)
        else:
            nxt = shifted * (2.0 / HALF) - buf[prior, :, slot(i)].astype(F32)
        nxt = nxt.astype(BF16)
        for target in targets:
            if target >= 2 and t < DEEP and not 0 <= i < NE:
                continue
            buf[target, :, slot(i)] = nxt

    def inside(t0):
        for k in range(DEEP):
            for i in range(k + 1, NE - k - 1):
                element(t0 + k, i)

    def left_side(t0, k):
        for i in range(k + 1 - DEEP, k + 1):
            element(t0 + k, i)

    def right_side(t0, k):
        for i in range(NE - k - 1, NE + DEEP - k - 1):
            element(t0 + k, i)

    inside(0)
    for copy in blocks:
        copy.wait_recv()
    use_coupling(NE - 1)
    for i in range(1, DEEP):
        use_coupling(-i)
        use_coupling(NE + i - 1)
        use_diagonal(-i)
        use_diagonal(NE + i - 1)
    use_coupling(-DEEP)
    for copy in vectors:
        copy.wait_recv()
    for i in range(DEEP):
        expand(i - DEEP, edges.at[0], EDGE - NB * (DEEP - i))
        expand(NE + i, edges.at[1], NB * i)

    def pass_on(k, source, target, n):
        v, w = buf.at[source], buf.at[target]
        return [
            outer(k, v.at[:, slot(NE - n, n)], w.at[:, slot(-n, n)], right),
            outer(k + 1, v.at[:, slot(0, n)], w.at[:, slot(NE, n)], left),
        ]

    second = pass_on(10, 0, 2, DEEP - 1)
    third = pass_on(12, 1, 3, DEEP)
    for k in range(DEEP):
        left_side(0, k)
        if k == 1:
            second[1].start()
        if k == 2:
            third[1].start()
        right_side(0, k)
        if k == 1:
            second[0].start()
        if k == 2:
            third[0].start()
    inside(DEEP)
    for copy in second + third:
        copy.wait_recv()
    for k in range(DEEP):
        left_side(DEEP, k)
        right_side(DEEP, k)

    final = 2
    chunks = {}
    for i in range(NE):
        start = (NB * i) // 128
        off = NB * i - 128 * start
        x = buf[final, :, slot(i)].astype(F32)
        if off:
            x = pltpu.roll(x, off, 1)
        for k in range(2):
            part = x[:, 128 * k : 128 * (k + 1)]
            at_chunk = start + k
            chunks[at_chunk] = chunks[at_chunk] + part if at_chunk in chunks else part
        done_to = COLS // 128 if i == NE - 1 else (NB * (i + 1)) // 128
        for c in sorted(chunks):
            if c < done_to:
                fall[chip, :, 128 * c : 128 * (c + 1)] = chunks.pop(c).astype(BF16)

    y_up, y_dn, y_far = (y + 1) % NY, (y + NY - 1) % NY, (y + 2) % NY
    peer_chip = (1 - xh) * NY + y
    side, far_side = xh * NY, (1 - xh) * NY
    low, high = slice(0, HALFROWS), slice(HALFROWS, ROWS)

    def gather(k, src, who):
        return remote(src, src, gat_send.at[k], gat_recv.at[k], who)

    own = fall.at[chip]
    sends = [gather(0, own, xpeer), gather(1, own, yup), gather(2, own, ydn)]
    for copy in sends:
        copy.start()

    r128 = lax.broadcasted_iota(jnp.int32, (ROWS, ROWS), 0)
    c128 = lax.broadcasted_iota(jnp.int32, (ROWS, ROWS), 1)
    r8 = lax.broadcasted_iota(jnp.int32, (CHIPS, ROWS), 0)
    sqs[0] = jnp.zeros((CHIPS, ROWS), F32)

    def cols_of(y_):
        return pl.ds(pl.multiple_of(y_ * ROWS, ROWS), ROWS)

    def norms(g):
        there = fall[g]
        square = nt_dot(there, there)
        diag = jnp.sum(jnp.where(r128 == c128, square, 0.0), axis=0, keepdims=True)
        sqs[0] = jnp.where(r8 == g, diag, sqs[0])

    def gram(part, g, y_):
        strip[part, :, cols_of(y_)] = nt_dot(fall[g], fall[side + y_])

    gram(0, chip, y)
    norms(chip)
    sends[1].wait_recv()
    sends.append(gather(3, fall.at[side + y_dn, low], yup))
    sends[3].start()
    gram(0, chip, y_dn)
    norms(side + y_dn)
    sends[2].wait_recv()
    sends.append(gather(4, fall.at[side + y_up, high], ydn))
    sends[4].start()
    gram(0, chip, y_up)
    norms(side + y_up)
    sends[3].wait_recv()
    sends[4].wait_recv()
    gram(0, chip, y_far)
    norms(side + y_far)
    sends[0].wait_recv()
    sends.append(gather(5, fall.at[peer_chip], yup))
    sends.append(gather(6, fall.at[peer_chip], ydn))
    sends[5].start()
    sends[6].start()
    for y_ in range(NY):
        gram(1, peer_chip, y_)
    norms(peer_chip)

    def stage(k, src, dst, who):
        return remote(src, dst, red_send.at[k], red_recv.at[k], who)

    def squares(k, s, who):
        return remote(sqs.at[s], sqr.at[k], sq_send.at[k], sq_recv.at[k], who)

    s1[...] = strip[:, other_rows, :].astype(BF16)
    copies = [stage(0, s1, r1, partner), squares(0, 0, partner)]
    for copy in copies:
        copy.start()
    for copy in copies:
        copy.wait_recv()
    half = strip[:, my_rows, :] + r1[...].astype(F32)
    strip[:, my_rows, :] = half
    s2[...] = half.astype(BF16)
    sqs[1] = sqs[0] + sqr[0]
    sends += copies

    quarter = HALFROWS // XL
    copies = []
    for j in range(1, XL * ZL):
        xl_, zl_ = (xl + j // ZL) % XL, (zl + j) % ZL
        rows = pl.ds(pl.multiple_of(xl_ * quarter, quarter), quarter)
        copies.append(stage(j, s2.at[:, rows, cols_of(zl_)], r2.at[j - 1], near[j - 1]))
        copies.append(squares(j, 1, near[j - 1]))
    for copy in copies:
        copy.start()
    row0 = pl.multiple_of(core * HALFROWS + xl * quarter, quarter)
    piece_rows = pl.ds(row0, quarter)
    total = strip[:, piece_rows, cols_of(zl)]
    sq = sqs[1]
    for copy in copies:
        copy.wait_recv()
    for j in range(1, XL * ZL):
        total = total + r2[j - 1].astype(F32)
        sq = sq + sqr[j]
    s3[...] = total.astype(BF16)
    sqs[2] = sq
    sends += copies

    copies = []
    for j in range(1, ZL):
        copies.append(stage(7 + j, s3, r3.at[j - 1], far[j - 1]))
        copies.append(squares(7 + j, 2, far[j - 1]))
    for copy in copies:
        copy.start()
    sends[5].wait_recv()
    late = [gather(7, fall.at[far_side + y_dn, low], yup)]
    late[0].start()
    sends[6].wait_recv()
    late.append(gather(8, fall.at[far_side + y_up, high], ydn))
    late[1].start()
    for copy in copies:
        copy.wait_recv()
    for j in range(1, ZL):
        total = total + r3[j - 1].astype(F32)
        sq = sq + sqr[7 + j]
    sends += copies + late

    scale = lax.rsqrt(sq + EPS)
    ri = lax.broadcasted_iota(jnp.int32, (quarter, ROWS), 0) + row0
    ci = lax.broadcasted_iota(jnp.int32, (quarter, ROWS), 1)
    same = ri == ci
    g = side + zl
    scale_row = jnp.sum(jnp.where(r8 == g, scale, 0.0), axis=0, keepdims=True)
    sq_row = jnp.sum(jnp.where(r8 == g, sq, 0.0), axis=0, keepdims=True)
    for part in range(2):
        of = chip if part == 0 else peer_chip
        lanes = jnp.sum(jnp.where(r8 == of, scale, 0.0), axis=0, keepdims=True)
        row_scale = jnp.sum(jnp.where(same, lanes, 0.0), axis=1, keepdims=True)
        value = total[part]
        ident = jnp.zeros_like(value)
        if part == 0:
            unit = jnp.logical_and(same, jnp.full(same.shape, zl - y, jnp.int32) == 0)
            value = jnp.where(unit, sq_row, value)
            ident = jnp.where(unit, 1.5, 0.0)
        normed = row_scale * value * scale_row
        w = math.sqrt(total_rows) * scale_row * (ident - 0.5 * normed)
        s4[part] = w.astype(BF16)

    g_cols = pl.ds(pl.multiple_of(g * ROWS, ROWS), ROWS)
    place = wfull.at[piece_rows, g_cols]
    put = pltpu.make_async_copy(s4.at[0], place, local_sem.at[4])
    put.start()
    copies = [stage(10 + j, s4.at[0], place, near[j - 1]) for j in range(1, XL * ZL)]
    copies += [stage(18 + j, s4.at[1], place, across[j]) for j in range(XL * ZL)]
    for copy in copies:
        copy.start()
    for copy in copies:
        copy.wait_recv()
    put.wait()
    sends += copies
    mine_w = wfull.at[my_rows]
    copy = stage(26, mine_w, mine_w, partner)
    copy.start()
    for waiting in late:
        waiting.wait_recv()
    copy.wait_recv()
    sends.append(copy)

    whole = fall.reshape(BANDS, COLS)
    for k in range(COLS // PAD):
        obuf[:, PAD * k : PAD * (k + 1)] = jnp.dot(
            wfull[...], whole[:, PAD * k : PAD * (k + 1)], preferred_element_type=F32
        ).astype(BF16)
    give = remote(
        obuf.at[other_rows], out.at[:, mine], gat_send.at[11], gat_recv.at[11], partner
    )
    give.start()
    keep_own = pltpu.make_async_copy(obuf.at[my_rows], out.at[:, mine], local_sem.at[3])
    keep_own.start()
    for copy in sends:
        copy.wait_send()
    swap.wait_send()
    for copy in blocks + vectors + second + third:
        copy.wait_send()
    keep_own.wait()
    give.wait()


def shards(basis_sizes, coupling_pattern, h_diag, h_couple, bands):
    total_rows = h_diag.shape[0] * lax.axis_size("elem") * h_diag.shape[1]
    hbm = pl.BlockSpec(memory_space=pltpu.HBM)
    dma = pltpu.SemaphoreType.DMA
    quarter = HALFROWS // XL
    return pl.pallas_call(
        functools.partial(kernel, total_rows),
        out_shape=jax.ShapeDtypeStruct(bands.shape, BF16),
        in_specs=[hbm] * 5,
        out_specs=hbm,
        scratch_shapes=[
            pltpu.VMEM((NE + 2 * DEEP - 2, 3 * PAD, PAD), BF16),
            pltpu.VMEM((4, ROWS, PAD * (NE + 2 * DEEP)), BF16),
            pltpu.VMEM((NE + 2 * DEEP - 2, NB, NB), BF16),
            pltpu.VMEM((NE + 2 * DEEP - 1, NB, NB), BF16),
            pltpu.VMEM((ROWS, COLS), BF16),
            pltpu.VMEM((2, ROWS, EDGE), BF16),
            pltpu.VMEM((CHIPS, ROWS, COLS), BF16),
            pltpu.VMEM((2, ROWS, SIDE), F32),
            pltpu.VMEM((2, HALFROWS, SIDE), BF16),
            pltpu.VMEM((2, HALFROWS, SIDE), BF16),
            pltpu.VMEM((2, HALFROWS, SIDE), BF16),
            pltpu.VMEM((XL * ZL - 1, 2, quarter, ROWS), BF16),
            pltpu.VMEM((2, quarter, ROWS), BF16),
            pltpu.VMEM((ZL - 1, 2, quarter, ROWS), BF16),
            pltpu.VMEM((2, quarter, ROWS), BF16),
            pltpu.VMEM((3, CHIPS, ROWS), F32),
            pltpu.VMEM((11, CHIPS, ROWS), F32),
            pltpu.VMEM((ROWS, BANDS), BF16),
            pltpu.VMEM((ROWS, COLS), BF16),
            *[pltpu.SMEM((2 * NE,), jnp.int32)] * 6,
            dma((7,)),
            dma((14,)),
            dma((14,)),
            dma((12,)),
            dma((12,)),
            dma((27,)),
            dma((27,)),
            dma((11,)),
            dma((11,)),
        ],
        compiler_params=pltpu.CompilerParams(
            collective_id=0, has_side_effects=True, vmem_limit_bytes=67043328
        ),
        name="filter_step",
    )(basis_sizes, coupling_pattern, h_diag, h_couple, bands)


def solution(mesh):
    in_specs = (
        P("elem"),
        P("elem"),
        P("elem", None, None),
        P("elem", None, None),
        P("band", "elem"),
    )
    out_specs = P("band", "elem")
    return jax.shard_map(shards, mesh=mesh, in_specs=in_specs, out_specs=out_specs, check_vma=False)
```

```python
import functools
import math

import jax
import jax.numpy as jnp
from jax import lax
from jax.experimental import pallas as pl
from jax.experimental.pallas import tpu as pltpu
from jax.sharding import PartitionSpec as P

MESH = pl.DeviceIdType.MESH
DEGREE = 6
CENTER = 0.4
HALF = 2.8
EPS = 1e-06
F32 = jnp.float32
BF16 = jnp.bfloat16

NB = 160
PAD = 256
NE = 8
ROWS = 128
HALFROWS = 64
COLS = NE * NB
DEEP = 3
EDGE = 512
ZL = 4
ZN = 16
XL = 2
NY = 4
CHIPS = 8
BANDS = ROWS * CHIPS
SIDE = ROWS * NY


def nt_dot(a, b):
    return lax.dot_general(a, b, (((1,), (1,)), ((), ())), preferred_element_type=F32)


def kernel(
    total_rows,
    sizes_hbm,
    pattern_hbm,
    hd,
    hc,
    bands,
    out_low,
    out_high,
    wts,
    buf,
    dbuf,
    cbuf,
    raw,
    edges,
    fall,
    strip,
    s1,
    r1,
    s2,
    r2,
    s3,
    r3,
    s4,
    sqs,
    sqr,
    wfull,
    obuf,
    sizes,
    pattern,
    sizes_out,
    pattern_out,
    local_sem,
    ext_send,
    ext_recv,
    gat_send,
    gat_recv,
    red_send,
    red_recv,
    sq_send,
    sq_recv,
):
    e = lax.axis_index("elem")
    b = lax.axis_index("band")
    ne = lax.axis_size("elem")
    core = b % 2
    other = 1 - core
    chip = b // 2
    xh = chip // NY
    y = chip % NY
    xl = e // ZN
    z = e % ZN
    zh = z // ZL
    zl = z % ZL

    def at(e_, b_):
        return (e_, b_)

    partner = at(e, chip * 2 + other)
    first = core == 0
    across_chip = at((e + jnp.where(first, ne - 1, 1)) % ne, chip * 2 + other)
    xpeer = at(e, ((1 - xh) * NY + y) * 2 + core)
    yup = at(e, (xh * NY + (y + 1) % NY) * 2 + core)
    ydn = at(e, (xh * NY + (y + NY - 1) % NY) * 2 + core)
    places = [((xl + j // ZL) % XL) * ZN + zh * ZL + (zl + j) % ZL for j in range(XL * ZL)]
    near = [at(p, b) for p in places[1:]]
    across = [at(p, xpeer[1]) for p in places]
    far = [at(xl * ZN + ((zh + j) % ZL) * ZL + zl, b) for j in range(1, ZL)]

    barrier = pltpu.get_barrier_semaphore()
    friends = [partner, across_chip, yup, ydn] + near + across + far
    for who in friends:
        pl.semaphore_signal(barrier, inc=1, device_id=who, device_id_type=MESH)

    def remote(src, dst, ss, rs, who):
        return pltpu.make_async_remote_copy(
            src_ref=src, dst_ref=dst, send_sem=ss, recv_sem=rs, device_id=who, device_id_type=MESH
        )

    def aligned(x, n):
        return pl.multiple_of(x, n)

    my_rows = pl.ds(aligned(core * HALFROWS, HALFROWS), HALFROWS)
    other_rows = pl.ds(aligned(other * HALFROWS, HALFROWS), HALFROWS)

    n_c, n_d = NE + DEEP, NE + DEEP - 1
    c_at, d_at = jnp.where(first, DEEP, 0), jnp.where(first, DEEP - 1, 0)
    load_c = pltpu.make_async_copy(
        hc.at[pl.ds(core * (NE - DEEP), n_c)], cbuf.at[pl.ds(c_at, n_c)], local_sem.at[0]
    )
    load_d = pltpu.make_async_copy(
        hd.at[pl.ds(core * (NE - DEEP + 1), n_d)], dbuf.at[pl.ds(d_at, n_d)], local_sem.at[1]
    )
    wide = COLS + EDGE
    base = aligned(core * EDGE, 128)
    mine = pl.ds(aligned(core * (COLS - EDGE), 128), wide)
    theirs = pl.ds(aligned(other * (COLS - EDGE), 128), wide)
    load_v = pltpu.make_async_copy(bands.at[:, mine], raw.at[my_rows], local_sem.at[2])
    load_s = pltpu.make_async_copy(sizes_hbm, sizes, local_sem.at[5])
    load_p = pltpu.make_async_copy(pattern_hbm, pattern, local_sem.at[6])
    for load in (load_s, load_p, load_c, load_d, load_v):
        load.start()

    pl.semaphore_wait(barrier, len(friends))

    def outer(k, src, dst, who):
        return remote(src, dst, ext_send.at[k], ext_recv.at[k], who)

    swap = remote(bands.at[:, theirs], raw.at[my_rows], gat_send.at[13], gat_recv.at[13], partner)
    swap.start()
    c_out = jnp.where(first, 0, 2 * NE - DEEP)
    d_out = jnp.where(first, 0, 2 * NE - DEEP + 1)
    c_in, d_in = jnp.where(first, DEEP + NE, 0), jnp.where(first, DEEP - 1 + NE, 0)
    blocks = [
        outer(0, sizes_hbm, sizes_out, across_chip),
        outer(1, pattern_hbm, pattern_out, across_chip),
        outer(2, hc.at[pl.ds(c_out, DEEP)], cbuf.at[pl.ds(c_in, DEEP)], across_chip),
        outer(3, hd.at[pl.ds(d_out, DEEP - 1)], dbuf.at[pl.ds(d_in, DEEP - 1)], across_chip),
    ]
    for copy in blocks:
        copy.start()

    wts[...] = jnp.zeros_like(wts)
    load_v.wait()
    swap.wait_recv()
    edge_out = pl.ds(aligned(core * COLS, 128), EDGE)
    vectors = outer(4, raw.at[:, edge_out], edges, across_chip)
    vectors.start()

    ICI, CHIP = 0, 1

    def on_side(side, j):
        return jnp.where(first, j, NE - 1 - j) if side == ICI else jnp.where(first, NE - 1 - j, j)

    def number(table, table_out, side, j):
        if side == ICI and j < 0:
            return table_out[jnp.where(first, 2 * NE + j, -1 - j)]
        if side == ICI:
            return table[jnp.where(first, j, 2 * NE - 1 - j)]
        return table[jnp.where(first, NE - 1 - j, NE + j)]

    lanes_nb = lax.broadcasted_iota(jnp.int32, (NB, NB), 1)
    eye = (lax.broadcasted_iota(jnp.int32, (NB, NB), 0) == lanes_nb).astype(BF16)

    def coupled(i, on):
        gate = jnp.full((NB, NB), on, jnp.int32) != 0
        return jnp.where(gate, cbuf[i + DEEP].astype(F32), 0.0)

    def put_weights(i, row, value, size):
        at_row = slice(row * PAD, row * PAD + NB)
        keep = lanes_nb < size
        wts[i + DEEP - 1, at_row, 0:NB] = jnp.where(keep, value, 0.0).astype(BF16)

    for load in (load_s, load_p, load_c, load_d):
        load.wait()
    own_size = [sizes[core * NE + i] for i in range(NE)]
    for i in range(NE):
        put_weights(i, 1, dbuf[i + DEEP - 1].astype(F32), own_size[i])
        if i + 1 < NE:
            pc = coupled(i, pattern[core * NE + i])
            put_weights(i, 2, nt_dot(eye, pc.astype(BF16)), own_size[i])
            put_weights(i + 1, 0, pc, own_size[i + 1])

    def side_weights(side):
        left_side = first if side == ICI else jnp.logical_not(first)
        count = number

        for j in range(-1, -DEEP, -1):
            i = on_side(side, j)
            size = count(sizes, sizes_out, side, j)
            put_weights(i, 1, dbuf[i + DEEP - 1].astype(F32), size)
        for j in range(0, -DEEP, -1):
            low = jnp.where(left_side, on_side(side, j - 1), on_side(side, j))
            on = jnp.where(
                left_side,
                count(pattern, pattern_out, side, j - 1),
                count(pattern, pattern_out, side, j),
            )
            pc = coupled(low, on)
            turned = nt_dot(eye, pc.astype(BF16))
            inner, outer_ = on_side(side, j), on_side(side, j - 1)
            size = count(sizes, sizes_out, side, j)
            value = jnp.where(left_side, pc, turned)
            put_weights_at(inner, jnp.where(left_side, 0, 2), value, size)
            if j > 1 - DEEP:
                size = count(sizes, sizes_out, side, j - 1)
                value = jnp.where(left_side, turned, pc)
                put_weights_at(outer_, jnp.where(left_side, 2, 0), value, size)

    def put_weights_at(i, row, value, size):
        keep = lanes_nb < size
        rows = pl.ds(aligned(row * PAD, PAD), NB)
        wts[i + DEEP - 1, rows, 0:NB] = jnp.where(keep, value, 0.0).astype(BF16)

    def slot(i, n=1):
        if isinstance(i, int):
            return slice(PAD * (i + DEEP), PAD * (i + DEEP + n))
        return pl.ds(aligned(PAD * (i + DEEP), PAD), PAD * n)

    lanes_pad = lax.broadcasted_iota(jnp.int32, (ROWS, PAD), 1)

    def expand(i, size, ref, column):
        off = column % 128
        x = ref[:, pl.ds(aligned(column - off, 128), PAD)].astype(F32)
        x = pltpu.roll(x, (PAD - off) % PAD, 1)
        buf[0, :, slot(i)] = jnp.where(lanes_pad < size, x, 0.0).astype(BF16)

    for i in range(NE):
        start = NB * i // 128 * 128
        x = raw[:, pl.ds(aligned(base + start, 128), PAD)].astype(F32)
        if NB * i > start:
            x = pltpu.roll(x, PAD - (NB * i - start), 1)
        buf[0, :, slot(i)] = jnp.where(lanes_pad < own_size[i], x, 0.0).astype(BF16)
    for j in range(-1, -DEEP - 1, -1):
        column = jnp.where(first, COLS + NB * (-1 - j), EDGE + NB * j)
        expand(on_side(CHIP, j), number(sizes, sizes_out, CHIP, j), raw, column)

    def element(t, i, own):
        now, prior, targets = [
            (0, None, [1]),
            (1, 0, [0, 2]),
            (0, 1, [1, 3]),
            (3, 2, [2]),
            (2, 3, [3]),
            (3, 2, [2]),
        ][t]
        acc = jnp.dot(
            buf[now, :, slot(i - 1, 3)], wts[i + DEEP - 1], preferred_element_type=F32
        )
        shifted = acc - CENTER * buf[now, :, slot(i)].astype(F32)
        if t == 0:
            nxt = shifted * (1.0 / HALF)
        else:
            nxt = shifted * (2.0 / HALF) - buf[prior, :, slot(i)].astype(F32)
        nxt = nxt.astype(BF16)
        for target in targets:
            if own or target < 2 or t >= DEEP:
                buf[target, :, slot(i)] = nxt

    def inside(t0):
        for k in range(DEEP):
            for i in range(k + 1, NE - k - 1):
                element(t0 + k, i, True)

    def side_steps(t0, side, k):
        for j in range(k + 1 - DEEP, k + 1):
            element(t0 + k, on_side(side, j), j >= 0)

    def pass_on(k, side, source, target, n):
        v, w = buf.at[source], buf.at[target]
        left_side = first if side == ICI else jnp.logical_not(first)
        src = slot(jnp.where(left_side, 0, NE - n), n)
        dst = slot(jnp.where(left_side, NE, -n), n)
        return outer(k, v.at[:, src], w.at[:, dst], across_chip if side == ICI else partner)

    second = [pass_on(5 + side, side, 0, 2, DEEP - 1) for side in (ICI, CHIP)]
    third = [pass_on(7 + side, side, 1, 3, DEEP) for side in (ICI, CHIP)]

    def first_steps(side):
        for k in range(DEEP):
            side_steps(0, side, k)
            if k == DEEP - 2:
                second[side].start()
        third[side].start()

    side_weights(CHIP)
    inside(0)
    first_steps(CHIP)
    for copy in blocks:
        copy.wait_recv()
    side_weights(ICI)
    vectors.wait_recv()
    for j in range(-1, -DEEP - 1, -1):
        column = jnp.where(first, EDGE + NB * j, NB * (-1 - j))
        expand(on_side(ICI, j), number(sizes, sizes_out, ICI, j), edges, column)
    first_steps(ICI)
    inside(DEEP)
    for side in (CHIP, ICI):
        second[side].wait_recv()
        third[side].wait_recv()
        for k in range(DEEP):
            side_steps(DEEP, side, k)

    final = 2
    chunks = {}
    for i in range(NE):
        start = (NB * i) // 128
        off = NB * i - 128 * start
        x = buf[final, :, slot(i)].astype(F32)
        if off:
            x = pltpu.roll(x, off, 1)
        for k in range(2):
            part = x[:, 128 * k : 128 * (k + 1)]
            at_chunk = start + k
            chunks[at_chunk] = chunks[at_chunk] + part if at_chunk in chunks else part
        done_to = COLS // 128 if i == NE - 1 else (NB * (i + 1)) // 128
        for c in sorted(chunks):
            if c < done_to:
                fall[core, chip, :, 128 * c : 128 * (c + 1)] = chunks.pop(c).astype(BF16)

    y_up, y_dn, y_far = (y + 1) % NY, (y + NY - 1) % NY, (y + 2) % NY
    peer_chip = (1 - xh) * NY + y
    side, far_side = xh * NY, (1 - xh) * NY
    low, high = slice(0, HALFROWS), slice(HALFROWS, ROWS)

    held = fall.at[core]

    def gather(k, g, rows, who):
        part = held.at[g] if rows is None else held.at[g, rows]
        copy = remote(part, part, gat_send.at[k], gat_recv.at[k], who)
        copy.start()
        sends.append(copy)
        return copy

    def share(k, g):
        copy = gather(14 + k, g, None, partner)
        shared.append(copy)

    sends, shared = [], []
    from_dn = [gather(1, chip, low, yup)]
    from_up = [gather(3, chip, high, ydn)]
    from_x = gather(0, chip, None, xpeer)
    from_dn.append(gather(2, chip, high, yup))
    from_up.append(gather(4, chip, low, ydn))
    share(0, chip)

    r128 = lax.broadcasted_iota(jnp.int32, (ROWS, ROWS), 0)
    c128 = lax.broadcasted_iota(jnp.int32, (ROWS, ROWS), 1)
    r8 = lax.broadcasted_iota(jnp.int32, (CHIPS, ROWS), 0)
    sqs[0] = jnp.zeros((CHIPS, ROWS), F32)

    def cols_of(y_):
        return pl.ds(pl.multiple_of(y_ * ROWS, ROWS), ROWS)

    def norms(g):
        there = held[g]
        square = nt_dot(there, there)
        diag = jnp.sum(jnp.where(r128 == c128, square, 0.0), axis=0, keepdims=True)
        sqs[0] = jnp.where(r8 == g, diag, sqs[0])

    def gram(part, g, y_):
        strip[part, :, cols_of(y_)] = nt_dot(held[g], held[side + y_])

    gram(0, chip, y)
    norms(chip)
    from_dn[0].wait_recv()
    on_up = gather(5, side + y_dn, low, yup)
    from_up[0].wait_recv()
    on_dn = gather(6, side + y_up, high, ydn)
    from_dn[1].wait_recv()
    share(1, side + y_dn)
    gram(0, chip, y_dn)
    norms(side + y_dn)
    from_up[1].wait_recv()
    share(2, side + y_up)
    gram(0, chip, y_up)
    norms(side + y_up)
    from_x.wait_recv()
    late_dn = [gather(7, peer_chip, low, yup)]
    late_up = [gather(9, peer_chip, high, ydn)]
    late_dn.append(gather(8, peer_chip, high, yup))
    late_up.append(gather(10, peer_chip, low, ydn))
    norms(peer_chip)
    gram(1, peer_chip, y)
    gram(1, peer_chip, y_dn)
    gram(1, peer_chip, y_up)
    on_up.wait_recv()
    on_dn.wait_recv()
    gram(0, chip, y_far)
    gram(1, peer_chip, y_far)
    norms(side + y_far)

    def stage(k, src, dst, who):
        return remote(src, dst, red_send.at[k], red_recv.at[k], who)

    def squares(k, s, who):
        return remote(sqs.at[s], sqr.at[k], sq_send.at[k], sq_recv.at[k], who)

    s1[...] = strip[:, other_rows, :].astype(BF16)
    copies = [stage(0, s1, r1, partner), squares(0, 0, partner)]
    for copy in copies:
        copy.start()
    for copy in copies:
        copy.wait_recv()
    half = strip[:, my_rows, :] + r1[...].astype(F32)
    strip[:, my_rows, :] = half
    s2[...] = half.astype(BF16)
    sqs[1] = sqs[0] + sqr[0]
    sends += copies
    share(3, side + y_far)
    share(4, peer_chip)

    quarter = HALFROWS // XL
    copies = []
    for j in range(1, XL * ZL):
        xl_, zl_ = (xl + j // ZL) % XL, (zl + j) % ZL
        rows = pl.ds(pl.multiple_of(xl_ * quarter, quarter), quarter)
        copies.append(stage(j, s2.at[:, rows, cols_of(zl_)], r2.at[j - 1], near[j - 1]))
        copies.append(squares(j, 1, near[j - 1]))
    for copy in copies:
        copy.start()
    row0 = pl.multiple_of(core * HALFROWS + xl * quarter, quarter)
    piece_rows = pl.ds(row0, quarter)
    total = strip[:, piece_rows, cols_of(zl)]
    sq = sqs[1]
    for copy in copies:
        copy.wait_recv()
    for j in range(1, XL * ZL):
        total = total + r2[j - 1].astype(F32)
        sq = sq + sqr[j]
    s3[...] = total.astype(BF16)
    sqs[2] = sq
    sends += copies

    copies = []
    for j in range(1, ZL):
        copies.append(stage(7 + j, s3, r3.at[j - 1], far[j - 1]))
        copies.append(squares(7 + j, 2, far[j - 1]))
    for copy in copies:
        copy.start()
    late_dn[0].wait_recv()
    late_on_up = gather(11, far_side + y_dn, low, yup)
    late_up[0].wait_recv()
    late_on_dn = gather(12, far_side + y_up, high, ydn)
    late_dn[1].wait_recv()
    share(5, far_side + y_dn)
    late_up[1].wait_recv()
    share(6, far_side + y_up)
    for copy in copies:
        copy.wait_recv()
    for j in range(1, ZL):
        total = total + r3[j - 1].astype(F32)
        sq = sq + sqr[7 + j]
    sends += copies

    scale = lax.rsqrt(sq + EPS)
    ri = lax.broadcasted_iota(jnp.int32, (quarter, ROWS), 0) + row0
    ci = lax.broadcasted_iota(jnp.int32, (quarter, ROWS), 1)
    same = ri == ci
    g = side + zl
    scale_row = jnp.sum(jnp.where(r8 == g, scale, 0.0), axis=0, keepdims=True)
    sq_row = jnp.sum(jnp.where(r8 == g, sq, 0.0), axis=0, keepdims=True)
    for part in range(2):
        of = chip if part == 0 else peer_chip
        lanes = jnp.sum(jnp.where(r8 == of, scale, 0.0), axis=0, keepdims=True)
        row_scale = jnp.sum(jnp.where(same, lanes, 0.0), axis=1, keepdims=True)
        value = total[part]
        ident = jnp.zeros_like(value)
        if part == 0:
            unit = jnp.logical_and(same, jnp.full(same.shape, zl - y, jnp.int32) == 0)
            value = jnp.where(unit, sq_row, value)
            ident = jnp.where(unit, 1.5, 0.0)
        normed = row_scale * value * scale_row
        w = math.sqrt(total_rows) * scale_row * (ident - 0.5 * normed)
        s4[part] = w.astype(BF16)

    g_cols = pl.ds(pl.multiple_of(g * ROWS, ROWS), ROWS)
    place = wfull.at[pl.ds(pl.multiple_of(xl * quarter, quarter), quarter), g_cols]
    put = pltpu.make_async_copy(s4.at[0], place, local_sem.at[4])
    put.start()
    copies = [stage(10 + j, s4.at[0], place, near[j - 1]) for j in range(1, XL * ZL)]
    copies += [stage(18 + j, s4.at[1], place, across[j]) for j in range(XL * ZL)]
    for copy in copies:
        copy.start()
    late_on_up.wait_recv()
    late_on_dn.wait_recv()
    share(7, far_side + y_far)
    for copy in shared:
        copy.wait_recv()
    for copy in copies:
        copy.wait_recv()
    put.wait()
    sends += copies

    writes = []
    for h in range(2):
        whole = fall.at[h].reshape(BANDS, COLS)
        for k in range(COLS // PAD):
            obuf[h, :, PAD * k : PAD * (k + 1)] = jnp.dot(
                wfull[...], whole[:, PAD * k : PAD * (k + 1)], preferred_element_type=F32
            ).astype(BF16)
        write = pltpu.make_async_copy(obuf.at[h], (out_low, out_high)[h], local_sem.at[3 + 4 * h])
        write.start()
        writes.append(write)
    for copy in sends + blocks + [vectors, swap] + second + third:
        copy.wait_send()
    for write in writes:
        write.wait()


def shards(basis_sizes, coupling_pattern, h_diag, h_couple, bands):
    total_rows = h_diag.shape[0] * lax.axis_size("elem") * h_diag.shape[1]
    hbm = pl.BlockSpec(memory_space=pltpu.HBM)
    dma = pltpu.SemaphoreType.DMA
    quarter = HALFROWS // XL
    halves = pl.pallas_call(
        functools.partial(kernel, total_rows),
        out_shape=[jax.ShapeDtypeStruct((HALFROWS, COLS), BF16)] * 2,
        in_specs=[hbm] * 5,
        out_specs=[hbm, hbm],
        scratch_shapes=[
            pltpu.VMEM((NE + 2 * DEEP - 2, 3 * PAD, PAD), BF16),
            pltpu.VMEM((4, ROWS, PAD * (NE + 2 * DEEP)), BF16),
            pltpu.VMEM((NE + 2 * DEEP - 2, NB, NB), BF16),
            pltpu.VMEM((NE + 2 * DEEP, NB, NB), BF16),
            pltpu.VMEM((ROWS, COLS + EDGE), BF16),
            pltpu.VMEM((ROWS, EDGE), BF16),
            pltpu.VMEM((2, CHIPS, ROWS, COLS), BF16),
            pltpu.VMEM((2, ROWS, SIDE), F32),
            pltpu.VMEM((2, HALFROWS, SIDE), BF16),
            pltpu.VMEM((2, HALFROWS, SIDE), BF16),
            pltpu.VMEM((2, HALFROWS, SIDE), BF16),
            pltpu.VMEM((XL * ZL - 1, 2, quarter, ROWS), BF16),
            pltpu.VMEM((2, quarter, ROWS), BF16),
            pltpu.VMEM((ZL - 1, 2, quarter, ROWS), BF16),
            pltpu.VMEM((2, quarter, ROWS), BF16),
            pltpu.VMEM((3, CHIPS, ROWS), F32),
            pltpu.VMEM((11, CHIPS, ROWS), F32),
            pltpu.VMEM((HALFROWS, BANDS), BF16),
            pltpu.VMEM((2, HALFROWS, COLS), BF16),
            *[pltpu.SMEM((2 * NE,), jnp.int32)] * 4,
            dma((8,)),
            dma((9,)),
            dma((9,)),
            dma((22,)),
            dma((22,)),
            dma((26,)),
            dma((26,)),
            dma((11,)),
            dma((11,)),
        ],
        compiler_params=pltpu.CompilerParams(
            collective_id=0, has_side_effects=True, vmem_limit_bytes=67043328
        ),
        name="filter_step",
    )(basis_sizes, coupling_pattern, h_diag, h_couple, bands)
    return jnp.concatenate(halves, axis=1)


def solution(mesh):
    in_specs = (
        P("elem"),
        P("elem"),
        P("elem", None, None),
        P("elem", None, None),
        P("band", "elem"),
    )
    out_specs = P("band", "elem")
    return jax.shard_map(shards, mesh=mesh, in_specs=in_specs, out_specs=out_specs, check_vma=False)
```

```python
import functools
import math

import jax
import jax.numpy as jnp
from jax import lax
from jax.experimental import pallas as pl
from jax.experimental.pallas import tpu as pltpu
from jax.sharding import PartitionSpec as P

MESH = pl.DeviceIdType.MESH
DEGREE = 6
CENTER = 0.4
HALF = 2.8
EPS = 1e-06
F32 = jnp.float32
BF16 = jnp.bfloat16

NB = 160
PAD = 256
NE = 8
ROWS = 128
HALFROWS = 64
COLS = NE * NB
DEEP = 3
EDGE = 512
ZL = 4
ZN = 16
XL = 2
NY = 4
CHIPS = 8
BANDS = ROWS * CHIPS


def nt_dot(a, b):
    return lax.dot_general(a, b, (((1,), (1,)), ((), ())), preferred_element_type=F32)


def kernel(
    total_rows,
    sizes_hbm,
    pattern_hbm,
    hd,
    hc,
    bands,
    out_low,
    out_high,
    wts,
    buf,
    dbuf,
    cbuf,
    raw,
    edges,
    fall,
    strip,
    s1,
    r1,
    s2,
    r2,
    s3,
    r3,
    s4,
    sqs,
    sqr,
    wfull,
    obuf,
    sizes,
    pattern,
    sizes_out,
    pattern_out,
    round1,
    round2,
    round3,
    local_sem,
    ext_send,
    ext_recv,
    gat_send,
    gat_recv,
    red_send,
    red_recv,
    sq_send,
    sq_recv,
):
    e = lax.axis_index("elem")
    b = lax.axis_index("band")
    ne = lax.axis_size("elem")
    core = b % 2
    other = 1 - core
    chip = b // 2
    xh = chip // NY
    y = chip % NY
    xl = e // ZN
    z = e % ZN
    zh = z // ZL
    zl = z % ZL

    def at(e_, b_):
        return (e_, b_)

    partner = at(e, chip * 2 + other)
    first = core == 0
    across_chip = at((e + jnp.where(first, ne - 1, 1)) % ne, chip * 2 + other)
    xpeer = at(e, ((1 - xh) * NY + y) * 2 + core)
    yup = at(e, (xh * NY + (y + 1) % NY) * 2 + core)
    ydn = at(e, (xh * NY + (y + NY - 1) % NY) * 2 + core)
    places = [((xl + j // ZL) % XL) * ZN + zh * ZL + (zl + j) % ZL for j in range(XL * ZL)]
    near = [at(p, b) for p in places[1:]]
    across = [at(p, xpeer[1]) for p in places]
    far = [at(xl * ZN + ((zh + j) % ZL) * ZL + zl, b) for j in range(1, ZL)]

    barrier = pltpu.get_barrier_semaphore()
    zs = [at(xl * ZN + (z + d) % ZN, b) for d in (1, ZN - 1, 2, ZN - 2)]
    links = zs + [xpeer, at((1 - xl) * ZN + z, b), yup, ydn]
    friends = [partner, across_chip] + links
    yfar = at(e, (xh * NY + (y + 2) % NY) * 2 + core)

    def tell(sem, whom):
        for who in whom:
            pl.semaphore_signal(sem, inc=1, device_id=who, device_id_type=MESH)

    tell(barrier, friends)

    def remote(src, dst, ss, rs, who):
        return pltpu.make_async_remote_copy(
            src_ref=src, dst_ref=dst, send_sem=ss, recv_sem=rs, device_id=who, device_id_type=MESH
        )

    def aligned(x, n):
        return pl.multiple_of(x, n)

    my_rows = pl.ds(aligned(core * HALFROWS, HALFROWS), HALFROWS)
    other_rows = pl.ds(aligned(other * HALFROWS, HALFROWS), HALFROWS)

    n_c, n_d = NE + DEEP, NE + DEEP - 1
    c_at, d_at = jnp.where(first, DEEP, 0), jnp.where(first, DEEP - 1, 0)
    load_c = pltpu.make_async_copy(
        hc.at[pl.ds(core * (NE - DEEP), n_c)], cbuf.at[pl.ds(c_at, n_c)], local_sem.at[0]
    )
    load_d = pltpu.make_async_copy(
        hd.at[pl.ds(core * (NE - DEEP + 1), n_d)], dbuf.at[pl.ds(d_at, n_d)], local_sem.at[1]
    )
    wide = COLS + EDGE
    base = aligned(core * EDGE, 128)
    mine = pl.ds(aligned(core * (COLS - EDGE), 128), wide)
    theirs = pl.ds(aligned(other * (COLS - EDGE), 128), wide)
    load_v = pltpu.make_async_copy(bands.at[:, mine], raw.at[my_rows], local_sem.at[2])
    load_s = pltpu.make_async_copy(sizes_hbm, sizes, local_sem.at[5])
    load_p = pltpu.make_async_copy(pattern_hbm, pattern, local_sem.at[6])
    for load in (load_s, load_p, load_c, load_d, load_v):
        load.start()

    pl.semaphore_wait(barrier, len(friends))

    tell(round1, links)

    def outer(k, src, dst, who):
        return remote(src, dst, ext_send.at[k], ext_recv.at[k], who)

    swap = remote(bands.at[:, theirs], raw.at[my_rows], gat_send.at[13], gat_recv.at[13], partner)
    swap.start()
    c_out = jnp.where(first, 0, 2 * NE - DEEP)
    d_out = jnp.where(first, 0, 2 * NE - DEEP + 1)
    c_in, d_in = jnp.where(first, DEEP + NE, 0), jnp.where(first, DEEP - 1 + NE, 0)
    blocks = [
        outer(0, sizes_hbm, sizes_out, across_chip),
        outer(1, pattern_hbm, pattern_out, across_chip),
        outer(2, hc.at[pl.ds(c_out, DEEP)], cbuf.at[pl.ds(c_in, DEEP)], across_chip),
        outer(3, hd.at[pl.ds(d_out, DEEP - 1)], dbuf.at[pl.ds(d_in, DEEP - 1)], across_chip),
    ]
    for copy in blocks:
        copy.start()

    wts[...] = jnp.zeros_like(wts)
    load_v.wait()
    swap.wait_recv()
    edge_out = pl.ds(aligned(core * COLS, 128), EDGE)
    vectors = outer(4, raw.at[:, edge_out], edges, across_chip)
    vectors.start()

    pl.semaphore_wait(round1, len(links))
    tell(round2, links + [far[0], far[ZL - 2]])

    ICI, CHIP = 0, 1

    def on_side(side, j):
        return jnp.where(first, j, NE - 1 - j) if side == ICI else jnp.where(first, NE - 1 - j, j)

    def number(table, table_out, side, j):
        if side == ICI and j < 0:
            return table_out[jnp.where(first, 2 * NE + j, -1 - j)]
        if side == ICI:
            return table[jnp.where(first, j, 2 * NE - 1 - j)]
        return table[jnp.where(first, NE - 1 - j, NE + j)]

    lanes_nb = lax.broadcasted_iota(jnp.int32, (NB, NB), 1)
    eye = (lax.broadcasted_iota(jnp.int32, (NB, NB), 0) == lanes_nb).astype(BF16)

    def coupled(i, on):
        gate = jnp.full((NB, NB), on, jnp.int32) != 0
        return jnp.where(gate, cbuf[i + DEEP].astype(F32), 0.0)

    def put_weights(i, row, value, size):
        at_row = slice(row * PAD, row * PAD + NB)
        keep = lanes_nb < size
        wts[i + DEEP - 1, at_row, 0:NB] = jnp.where(keep, value, 0.0).astype(BF16)

    for load in (load_s, load_p, load_c, load_d):
        load.wait()
    own_size = [sizes[core * NE + i] for i in range(NE)]
    for i in range(NE):
        put_weights(i, 1, dbuf[i + DEEP - 1].astype(F32), own_size[i])
        if i + 1 < NE:
            pc = coupled(i, pattern[core * NE + i])
            put_weights(i, 2, nt_dot(eye, pc.astype(BF16)), own_size[i])
            put_weights(i + 1, 0, pc, own_size[i + 1])

    def side_weights(side):
        left_side = first if side == ICI else jnp.logical_not(first)
        count = number

        for j in range(-1, -DEEP, -1):
            i = on_side(side, j)
            size = count(sizes, sizes_out, side, j)
            put_weights(i, 1, dbuf[i + DEEP - 1].astype(F32), size)
        for j in range(0, -DEEP, -1):
            low = jnp.where(left_side, on_side(side, j - 1), on_side(side, j))
            on = jnp.where(
                left_side,
                count(pattern, pattern_out, side, j - 1),
                count(pattern, pattern_out, side, j),
            )
            pc = coupled(low, on)
            turned = nt_dot(eye, pc.astype(BF16))
            inner, outer_ = on_side(side, j), on_side(side, j - 1)
            size = count(sizes, sizes_out, side, j)
            value = jnp.where(left_side, pc, turned)
            put_weights_at(inner, jnp.where(left_side, 0, 2), value, size)
            if j > 1 - DEEP:
                size = count(sizes, sizes_out, side, j - 1)
                value = jnp.where(left_side, turned, pc)
                put_weights_at(outer_, jnp.where(left_side, 2, 0), value, size)

    def put_weights_at(i, row, value, size):
        keep = lanes_nb < size
        rows = pl.ds(aligned(row * PAD, PAD), NB)
        wts[i + DEEP - 1, rows, 0:NB] = jnp.where(keep, value, 0.0).astype(BF16)

    def slot(i, n=1):
        if isinstance(i, int):
            return slice(PAD * (i + DEEP), PAD * (i + DEEP + n))
        return pl.ds(aligned(PAD * (i + DEEP), PAD), PAD * n)

    lanes_pad = lax.broadcasted_iota(jnp.int32, (ROWS, PAD), 1)

    def expand(i, size, ref, column):
        off = column % 128
        x = ref[:, pl.ds(aligned(column - off, 128), PAD)].astype(F32)
        x = pltpu.roll(x, (PAD - off) % PAD, 1)
        buf[0, :, slot(i)] = jnp.where(lanes_pad < size, x, 0.0).astype(BF16)

    for i in range(NE):
        start = NB * i // 128 * 128
        x = raw[:, pl.ds(aligned(base + start, 128), PAD)].astype(F32)
        if NB * i > start:
            x = pltpu.roll(x, PAD - (NB * i - start), 1)
        buf[0, :, slot(i)] = jnp.where(lanes_pad < own_size[i], x, 0.0).astype(BF16)
    for j in range(-1, -DEEP - 1, -1):
        column = jnp.where(first, COLS + NB * (-1 - j), EDGE + NB * j)
        expand(on_side(CHIP, j), number(sizes, sizes_out, CHIP, j), raw, column)

    def element(t, i, own):
        now, prior, targets = [
            (0, None, [1]),
            (1, 0, [0, 2]),
            (0, 1, [1, 3]),
            (3, 2, [2]),
            (2, 3, [3]),
            (3, 2, [2]),
        ][t]
        acc = jnp.dot(
            buf[now, :, slot(i - 1, 3)], wts[i + DEEP - 1], preferred_element_type=F32
        )
        shifted = acc - CENTER * buf[now, :, slot(i)].astype(F32)
        if t == 0:
            nxt = shifted * (1.0 / HALF)
        else:
            nxt = shifted * (2.0 / HALF) - buf[prior, :, slot(i)].astype(F32)
        nxt = nxt.astype(BF16)
        for target in targets:
            if own or target < 2 or t >= DEEP:
                buf[target, :, slot(i)] = nxt

    def inside(t0):
        for k in range(DEEP):
            for i in range(k + 1, NE - k - 1):
                element(t0 + k, i, True)

    def side_steps(t0, side, k):
        for j in range(k + 1 - DEEP, k + 1):
            element(t0 + k, on_side(side, j), j >= 0 or k == DEEP - 2)

    def pass_on(k, side, source, target, skip, n):
        v, w = buf.at[source], buf.at[target]
        left_side = first if side == ICI else jnp.logical_not(first)
        src = slot(jnp.where(left_side, skip, NE - n - skip), n)
        dst = slot(jnp.where(left_side, NE + skip, -n - skip), n)
        return outer(k, v.at[:, src], w.at[:, dst], across_chip if side == ICI else partner)

    second = [pass_on(5 + side, side, 0, 2, DEEP - 2, 1) for side in (ICI, CHIP)]
    third = [pass_on(7 + side, side, 1, 3, 0, DEEP) for side in (ICI, CHIP)]

    def first_steps(side):
        for k in range(DEEP):
            side_steps(0, side, k)
            if k == DEEP - 2:
                second[side].start()
        third[side].start()

    side_weights(CHIP)
    inside(0)
    first_steps(CHIP)
    pl.semaphore_wait(round2, len(links) + 2)
    tell(round3, links)
    for copy in blocks:
        copy.wait_recv()
    side_weights(ICI)
    vectors.wait_recv()
    for j in range(-1, -DEEP - 1, -1):
        column = jnp.where(first, EDGE + NB * j, NB * (-1 - j))
        expand(on_side(ICI, j), number(sizes, sizes_out, ICI, j), edges, column)
    first_steps(ICI)
    inside(DEEP)
    for side in (CHIP, ICI):
        second[side].wait_recv()
        third[side].wait_recv()
        for k in range(DEEP):
            side_steps(DEEP, side, k)

    pl.semaphore_wait(round3, len(links))

    final = 2
    chunks = {}
    for i in range(NE):
        start = (NB * i) // 128
        off = NB * i - 128 * start
        x = buf[final, :, slot(i)].astype(F32)
        if off:
            x = pltpu.roll(x, off, 1)
        for k in range(2):
            part = x[:, 128 * k : 128 * (k + 1)]
            at_chunk = start + k
            chunks[at_chunk] = chunks[at_chunk] + part if at_chunk in chunks else part
        done_to = COLS // 128 if i == NE - 1 else (NB * (i + 1)) // 128
        for c in sorted(chunks):
            if c < done_to:
                fall[core, chip, :, 128 * c : 128 * (c + 1)] = chunks.pop(c).astype(BF16)

    y_up, y_dn, y_far = (y + 1) % NY, (y + NY - 1) % NY, (y + 2) % NY
    peer_chip = (1 - xh) * NY + y
    side, far_side = xh * NY, (1 - xh) * NY
    low, high = slice(0, HALFROWS), slice(HALFROWS, ROWS)

    held = fall.at[core]

    def gather(k, g, rows, who):
        part = held.at[g] if rows is None else held.at[g, rows]
        copy = remote(part, part, gat_send.at[k], gat_recv.at[k], who)
        copy.start()
        sends.append(copy)
        return copy

    def share(k, g):
        copy = gather(14 + k, g, None, partner)
        shared.append(copy)

    sends, shared = [], []
    from_dn = [gather(1, chip, low, yup)]
    from_up = [gather(3, chip, high, ydn)]
    from_x = gather(0, chip, None, xpeer)
    from_dn.append(gather(2, chip, high, yup))
    from_up.append(gather(4, chip, low, ydn))
    share(0, chip)

    r128 = lax.broadcasted_iota(jnp.int32, (ROWS, ROWS), 0)
    c128 = lax.broadcasted_iota(jnp.int32, (ROWS, ROWS), 1)

    def gram(part, g, o):
        strip[o, part] = nt_dot(held[g], held[side + (y + o) % NY])

    def squares(k, s, who):
        copy = remote(sqs.at[s], sqr.at[k], sq_send.at[k], sq_recv.at[k], who)
        copy.start()
        sends.append(copy)
        return copy

    def stage(k, src, dst, who):
        return remote(src, dst, red_send.at[k], red_recv.at[k], who)

    quarter = HALFROWS // XL
    row0 = pl.multiple_of(core * HALFROWS + xl * quarter, quarter)
    piece_rows = pl.ds(row0, quarter)

    def over_cores(offsets):
        copies = []
        for o in offsets:
            s1[o] = strip[o, :, other_rows, :].astype(BF16)
            copies.append(stage(o, s1.at[o], r1.at[o], partner))
            copies[-1].start()
        sends.extend(copies)
        return copies

    def to_owner(o, dx):
        col = (y + o) % NY
        j = dx * ZL + (col + ZL - zl) % ZL
        xl_ = (xl + dx) % XL
        rows = pl.ds(pl.multiple_of(xl_ * quarter, quarter), quarter)
        who = at(xl_ * ZN + zh * ZL + col, b)
        copy = remote(
            s2.at[o, :, rows], r2.at[j - 1], red_send.at[j + 4], red_recv.at[j + 4], who
        )
        return copy, col != zl

    def to_owners(offsets, copies):
        for o, copy in zip(offsets, copies):
            copy.wait_recv()
            half = strip[o, :, my_rows, :] + r1[o].astype(F32)
            strip[o, :, my_rows, :] = half
            s2[o] = half.astype(BF16)
            crossing, _ = to_owner(o, 1)
            crossing.start()
            along, away = to_owner(o, 0)

            @pl.when(away)
            def _():
                along.start()

    gram(0, chip, 0)
    norm = jnp.sum(jnp.where(r128 == c128, strip[0, 0], 0.0), axis=0, keepdims=True)
    sqs[0] = jnp.broadcast_to(norm, (CHIPS, ROWS))
    of_core = squares(0, 0, partner)
    from_dn[0].wait_recv()
    on_up = gather(5, side + y_dn, low, yup)
    from_up[0].wait_recv()
    on_dn = gather(6, side + y_up, high, ydn)
    of_core.wait_recv()
    sqs[1] = sqs[0] + sqr[0]
    of_near = [squares(j, 1, near[j - 1]) for j in range(1, XL * ZL)]
    from_dn[1].wait_recv()
    gram(0, chip, 3)
    from_up[1].wait_recv()
    gram(0, chip, 1)
    from_x.wait_recv()
    late_dn = [gather(7, peer_chip, low, yup)]
    late_up = [gather(9, peer_chip, high, ydn)]
    late_dn.append(gather(8, peer_chip, high, yup))
    late_up.append(gather(10, peer_chip, low, ydn))
    early, last = (0, 3, 1), (2,)
    for o in early:
        gram(1, peer_chip, o)
    first_sums = over_cores(early)
    to_owners(early, first_sums)
    for copy in of_near:
        copy.wait_recv()
    norm = sqs[1]
    for j in range(1, XL * ZL):
        norm = norm + sqr[j]
    sqs[2] = norm
    of_far = [squares(7 + j, 2, far[j - 1]) for j in range(1, ZL)]
    on_up.wait_recv()
    on_dn.wait_recv()
    gram(0, chip, 2)
    gram(1, peer_chip, 2)
    last_sums = over_cores(last)
    to_owners(last, last_sums)
    share(1, side + y_dn)
    share(2, side + y_up)
    share(3, side + y_far)
    share(4, peer_chip)

    copies = [stage(4 + j, r2.at[j - 1], r2.at[j - 1], near[j - 1]) for j in range(1, XL * ZL)]
    for copy in copies:
        copy.wait_recv()
    total = strip[(zl + NY - y) % NY, :, piece_rows, :]
    for j in range(1, XL * ZL):
        total = total + r2[j - 1].astype(F32)
    s3[...] = total.astype(BF16)
    copies = [stage(11 + j, s3, r3.at[j - 1], far[j - 1]) for j in range(1, ZL)]
    for copy in copies:
        copy.start()
    sends.extend(copies)

    for copy in of_far:
        copy.wait_recv()
    norm = sqs[2]
    for j in range(1, ZL):
        norm = norm + sqr[7 + j]
    sqs[3] = norm
    norms = [squares(11 + k, 3, who) for k, who in enumerate((yup, ydn, yfar, xpeer))]
    late_dn[0].wait_recv()
    late_on_up = gather(11, far_side + y_dn, low, yup)
    late_up[0].wait_recv()
    late_on_dn = gather(12, far_side + y_up, high, ydn)
    late_dn[1].wait_recv()
    share(5, far_side + y_dn)
    late_up[1].wait_recv()
    share(6, far_side + y_up)
    for copy in norms:
        copy.wait_recv()
    for copy in copies:
        copy.wait_recv()
    for j in range(1, ZL):
        total = total + r3[j - 1].astype(F32)

    ri = lax.broadcasted_iota(jnp.int32, (quarter, ROWS), 0) + row0
    ci = lax.broadcasted_iota(jnp.int32, (quarter, ROWS), 1)
    same = ri == ci
    g = side + zl
    by_offset = [sqs[3, 0:1], sqr[12, 0:1], sqr[13, 0:1], sqr[11, 0:1]]
    sq_row = by_offset[0]
    for o in range(1, NY):
        here = jnp.full((1, ROWS), (zl + NY - y) % NY, jnp.int32) == o
        sq_row = jnp.where(here, by_offset[o], sq_row)
    scale_row = lax.rsqrt(sq_row + EPS)
    for part in range(2):
        lanes = lax.rsqrt((sqs[3, 0:1] if part == 0 else sqr[14, 0:1]) + EPS)
        row_scale = jnp.sum(jnp.where(same, lanes, 0.0), axis=1, keepdims=True)
        value = total[part]
        ident = jnp.zeros_like(value)
        if part == 0:
            unit = jnp.logical_and(same, jnp.full(same.shape, zl - y, jnp.int32) == 0)
            value = jnp.where(unit, sq_row, value)
            ident = jnp.where(unit, 1.5, 0.0)
        normed = row_scale * value * scale_row
        w = math.sqrt(total_rows) * scale_row * (ident - 0.5 * normed)
        s4[part] = w.astype(BF16)

    g_cols = pl.ds(pl.multiple_of(g * ROWS, ROWS), ROWS)
    place = wfull.at[pl.ds(pl.multiple_of(xl * quarter, quarter), quarter), g_cols]
    put = pltpu.make_async_copy(s4.at[0], place, local_sem.at[4])
    put.start()
    copies = [stage(14 + j, s4.at[0], place, near[j - 1]) for j in range(1, XL * ZL)]
    copies += [stage(22 + j, s4.at[1], place, across[j]) for j in range(XL * ZL)]
    for copy in copies:
        copy.start()
    late_on_up.wait_recv()
    late_on_dn.wait_recv()
    share(7, far_side + y_far)
    for copy in shared:
        copy.wait_recv()
    for copy in copies:
        copy.wait_recv()
    put.wait()
    sends += copies

    writes = []
    for h in range(2):
        whole = fall.at[h].reshape(BANDS, COLS)
        for k in range(COLS // PAD):
            obuf[h, :, PAD * k : PAD * (k + 1)] = jnp.dot(
                wfull[...], whole[:, PAD * k : PAD * (k + 1)], preferred_element_type=F32
            ).astype(BF16)
        write = pltpu.make_async_copy(obuf.at[h], (out_low, out_high)[h], local_sem.at[3 + 4 * h])
        write.start()
        writes.append(write)
    for o in range(NY):
        crossing, _ = to_owner(o, 1)
        crossing.wait_send()
        along, away = to_owner(o, 0)

        @pl.when(away)
        def _():
            along.wait_send()

    for copy in sends + blocks + [vectors, swap] + second + third:
        copy.wait_send()
    for write in writes:
        write.wait()


def shards(basis_sizes, coupling_pattern, h_diag, h_couple, bands):
    total_rows = h_diag.shape[0] * lax.axis_size("elem") * h_diag.shape[1]
    hbm = pl.BlockSpec(memory_space=pltpu.HBM)
    dma = pltpu.SemaphoreType.DMA
    quarter = HALFROWS // XL
    halves = pl.pallas_call(
        functools.partial(kernel, total_rows),
        out_shape=[jax.ShapeDtypeStruct((HALFROWS, COLS), BF16)] * 2,
        in_specs=[hbm] * 5,
        out_specs=[hbm, hbm],
        scratch_shapes=[
            pltpu.VMEM((NE + 2 * DEEP - 2, 3 * PAD, PAD), BF16),
            pltpu.VMEM((4, ROWS, PAD * (NE + 2 * DEEP)), BF16),
            pltpu.VMEM((NE + 2 * DEEP - 2, NB, NB), BF16),
            pltpu.VMEM((NE + 2 * DEEP, NB, NB), BF16),
            pltpu.VMEM((ROWS, COLS + EDGE), BF16),
            pltpu.VMEM((ROWS, EDGE), BF16),
            pltpu.VMEM((2, CHIPS, ROWS, COLS), BF16),
            pltpu.VMEM((NY, 2, ROWS, ROWS), F32),
            pltpu.VMEM((NY, 2, HALFROWS, ROWS), BF16),
            pltpu.VMEM((NY, 2, HALFROWS, ROWS), BF16),
            pltpu.VMEM((NY, 2, HALFROWS, ROWS), BF16),
            pltpu.VMEM((XL * ZL - 1, 2, quarter, ROWS), BF16),
            pltpu.VMEM((2, quarter, ROWS), BF16),
            pltpu.VMEM((ZL - 1, 2, quarter, ROWS), BF16),
            pltpu.VMEM((2, quarter, ROWS), BF16),
            pltpu.VMEM((4, CHIPS, ROWS), F32),
            pltpu.VMEM((15, CHIPS, ROWS), F32),
            pltpu.VMEM((HALFROWS, BANDS), BF16),
            pltpu.VMEM((2, HALFROWS, COLS), BF16),
            *[pltpu.SMEM((2 * NE,), jnp.int32)] * 4,
            *[pltpu.SemaphoreType.REGULAR] * 3,
            dma((8,)),
            dma((9,)),
            dma((9,)),
            dma((22,)),
            dma((22,)),
            dma((30,)),
            dma((30,)),
            dma((15,)),
            dma((15,)),
        ],
        compiler_params=pltpu.CompilerParams(
            collective_id=0, has_side_effects=True, vmem_limit_bytes=67043328
        ),
        name="filter_step",
    )(basis_sizes, coupling_pattern, h_diag, h_couple, bands)
    return jnp.concatenate(halves, axis=1)


def solution(mesh):
    in_specs = (
        P("elem"),
        P("elem"),
        P("elem", None, None),
        P("elem", None, None),
        P("band", "elem"),
    )
    out_specs = P("band", "elem")
    return jax.shard_map(shards, mesh=mesh, in_specs=in_specs, out_specs=out_specs, check_vma=False)
```

```python
import functools
import math

import jax
import jax.numpy as jnp
from jax import lax
from jax.experimental import pallas as pl
from jax.experimental.pallas import tpu as pltpu
from jax.sharding import PartitionSpec as P

MESH = pl.DeviceIdType.MESH
DEGREE = 6
CENTER = 0.4
HALF = 2.8
EPS = 1e-06
F32 = jnp.float32
BF16 = jnp.bfloat16

NB = 160
PAD = 256
NE = 8
ROWS = 128
HALFROWS = 64
COLS = NE * NB
DEEP = 3
EDGE = 512
REST = NB - 128
ZL = 4
ZN = 16
XL = 2
NY = 4
CHIPS = 8
BANDS = ROWS * CHIPS


def nt_dot(a, b):
    return lax.dot_general(a, b, (((1,), (1,)), ((), ())), preferred_element_type=F32)


def kernel(
    total_rows,
    sizes_hbm,
    pattern_hbm,
    hd,
    hc,
    bands,
    out_low,
    out_high,
    wts,
    buf,
    dbuf,
    cbuf,
    raw,
    edges,
    tails,
    packed,
    fall,
    strip,
    s1,
    r1,
    s2,
    r2,
    s3,
    r3,
    s4,
    sqs,
    sqr,
    wfull,
    obuf,
    sizes,
    pattern,
    sizes_out,
    pattern_out,
    round1,
    round2,
    round3,
    local_sem,
    ext_send,
    ext_recv,
    gat_send,
    gat_recv,
    red_send,
    red_recv,
    sq_send,
    sq_recv,
):
    e = lax.axis_index("elem")
    b = lax.axis_index("band")
    ne = lax.axis_size("elem")
    core = b % 2
    other = 1 - core
    chip = b // 2
    xh = chip // NY
    y = chip % NY
    xl = e // ZN
    z = e % ZN
    zh = z // ZL
    zl = z % ZL

    def at(e_, b_):
        return (e_, b_)

    partner = at(e, chip * 2 + other)
    first = core == 0
    across_chip = at((e + jnp.where(first, ne - 1, 1)) % ne, chip * 2 + other)
    xpeer = at(e, ((1 - xh) * NY + y) * 2 + core)
    yup = at(e, (xh * NY + (y + 1) % NY) * 2 + core)
    ydn = at(e, (xh * NY + (y + NY - 1) % NY) * 2 + core)
    places = [((xl + j // ZL) % XL) * ZN + zh * ZL + (zl + j) % ZL for j in range(XL * ZL)]
    near = [at(p, b) for p in places[1:]]
    across = [at(p, xpeer[1]) for p in places]
    far = [at(xl * ZN + ((zh + j) % ZL) * ZL + zl, b) for j in range(1, ZL)]

    barrier = pltpu.get_barrier_semaphore()
    zs = [at(xl * ZN + (z + d) % ZN, b) for d in (1, ZN - 1, 2, ZN - 2)]
    links = zs + [xpeer, at((1 - xl) * ZN + z, b), yup, ydn]
    friends = [partner, across_chip] + links
    yfar = at(e, (xh * NY + (y + 2) % NY) * 2 + core)

    def tell(sem, whom):
        for who in whom:
            pl.semaphore_signal(sem, inc=1, device_id=who, device_id_type=MESH)

    tell(barrier, friends)

    def remote(src, dst, ss, rs, who):
        return pltpu.make_async_remote_copy(
            src_ref=src, dst_ref=dst, send_sem=ss, recv_sem=rs, device_id=who, device_id_type=MESH
        )

    def aligned(x, n):
        return pl.multiple_of(x, n)

    my_rows = pl.ds(aligned(core * HALFROWS, HALFROWS), HALFROWS)
    other_rows = pl.ds(aligned(other * HALFROWS, HALFROWS), HALFROWS)

    n_c, n_d = NE + DEEP, NE + DEEP - 1
    c_at, d_at = jnp.where(first, DEEP, 0), jnp.where(first, DEEP - 1, 0)
    load_c = pltpu.make_async_copy(
        hc.at[pl.ds(core * (NE - DEEP), n_c)], cbuf.at[pl.ds(c_at, n_c)], local_sem.at[0]
    )
    load_d = pltpu.make_async_copy(
        hd.at[pl.ds(core * (NE - DEEP + 1), n_d)], dbuf.at[pl.ds(d_at, n_d)], local_sem.at[1]
    )
    wide = COLS + EDGE
    base = aligned(core * EDGE, 128)
    mine = pl.ds(aligned(core * (COLS - EDGE), 128), wide)
    theirs = pl.ds(aligned(other * (COLS - EDGE), 128), wide)
    load_v = pltpu.make_async_copy(bands.at[:, mine], raw.at[my_rows], local_sem.at[2])
    load_s = pltpu.make_async_copy(sizes_hbm, sizes, local_sem.at[5])
    load_p = pltpu.make_async_copy(pattern_hbm, pattern, local_sem.at[6])
    for load in (load_s, load_p, load_c, load_d, load_v):
        load.start()

    pl.semaphore_wait(barrier, len(friends))

    tell(round1, links)

    def outer(k, src, dst, who):
        return remote(src, dst, ext_send.at[k], ext_recv.at[k], who)

    swap = remote(bands.at[:, theirs], raw.at[my_rows], gat_send.at[13], gat_recv.at[13], partner)
    swap.start()
    head, n_e = slice(0, 128), DEEP - 1
    c_out = jnp.where(first, 0, 2 * NE - DEEP)
    d_out = jnp.where(first, 0, 2 * NE - DEEP + 1)
    c_in, d_in = jnp.where(first, DEEP + NE, 0), jnp.where(first, DEEP - 1 + NE, 0)
    blocks = [
        outer(0, sizes_hbm, sizes_out, across_chip),
        outer(1, pattern_hbm, pattern_out, across_chip),
        outer(2, hc.at[pl.ds(c_out, DEEP), :, head], cbuf.at[pl.ds(c_in, DEEP), :, head], across_chip),
        outer(3, hd.at[pl.ds(d_out, n_e), :, head], dbuf.at[pl.ds(d_in, n_e), :, head], across_chip),
    ]
    for copy in blocks:
        copy.start()
    for load in (load_s, load_p, load_c, load_d):
        load.wait()
    c_from = jnp.where(first, DEEP, NE)
    d_from = jnp.where(first, DEEP - 1, NE)
    for k in range(DEEP):
        tails[0, :, REST * k : REST * (k + 1)] = cbuf[c_from + k, :, 128:NB]
    for k in range(n_e):
        tails[0, REST * k : REST * (k + 1), REST * DEEP : 128] = dbuf[d_from + k, 128:NB, 128:NB]
    blocks.append(outer(5, tails.at[0], tails.at[1], across_chip))
    blocks[-1].start()

    wts[...] = jnp.zeros_like(wts)
    load_v.wait()
    swap.wait_recv()
    edge_out = pl.ds(aligned(core * COLS, 128), EDGE)
    vectors = outer(4, raw.at[:, edge_out], edges, across_chip)
    vectors.start()

    ICI, CHIP = 0, 1

    def on_side(side, j):
        return jnp.where(first, j, NE - 1 - j) if side == ICI else jnp.where(first, NE - 1 - j, j)

    def number(table, table_out, side, j):
        if side == ICI and j < 0:
            return table_out[jnp.where(first, 2 * NE + j, -1 - j)]
        if side == ICI:
            return table[jnp.where(first, j, 2 * NE - 1 - j)]
        return table[jnp.where(first, NE - 1 - j, NE + j)]

    lanes_nb = lax.broadcasted_iota(jnp.int32, (NB, NB), 1)
    eye = (lax.broadcasted_iota(jnp.int32, (NB, NB), 0) == lanes_nb).astype(BF16)

    def coupled(i, on):
        gate = jnp.full((NB, NB), on, jnp.int32) != 0
        return jnp.where(gate, cbuf[i + DEEP].astype(F32), 0.0)

    def put_weights(i, row, value, size):
        at_row = slice(row * PAD, row * PAD + NB)
        keep = lanes_nb < size
        wts[i + DEEP - 1, at_row, 0:NB] = jnp.where(keep, value, 0.0).astype(BF16)

    own_size = [sizes[core * NE + i] for i in range(NE)]
    for i in range(NE):
        put_weights(i, 1, dbuf[i + DEEP - 1].astype(F32), own_size[i])
        if i + 1 < NE:
            pc = coupled(i, pattern[core * NE + i])
            put_weights(i, 2, nt_dot(eye, pc.astype(BF16)), own_size[i])
            put_weights(i + 1, 0, pc, own_size[i + 1])

    def side_weights(side):
        left_side = first if side == ICI else jnp.logical_not(first)
        count = number

        for j in range(-1, -DEEP, -1):
            i = on_side(side, j)
            size = count(sizes, sizes_out, side, j)
            put_weights(i, 1, dbuf[i + DEEP - 1].astype(F32), size)
        for j in range(0, -DEEP, -1):
            low = jnp.where(left_side, on_side(side, j - 1), on_side(side, j))
            on = jnp.where(
                left_side,
                count(pattern, pattern_out, side, j - 1),
                count(pattern, pattern_out, side, j),
            )
            pc = coupled(low, on)
            turned = nt_dot(eye, pc.astype(BF16))
            inner, outer_ = on_side(side, j), on_side(side, j - 1)
            size = count(sizes, sizes_out, side, j)
            value = jnp.where(left_side, pc, turned)
            put_weights_at(inner, jnp.where(left_side, 0, 2), value, size)
            if j > 1 - DEEP:
                size = count(sizes, sizes_out, side, j - 1)
                value = jnp.where(left_side, turned, pc)
                put_weights_at(outer_, jnp.where(left_side, 2, 0), value, size)

    def put_weights_at(i, row, value, size):
        keep = lanes_nb < size
        rows = pl.ds(aligned(row * PAD, PAD), NB)
        wts[i + DEEP - 1, rows, 0:NB] = jnp.where(keep, value, 0.0).astype(BF16)

    def slot(i, n=1):
        if isinstance(i, int):
            return slice(PAD * (i + DEEP), PAD * (i + DEEP + n))
        return pl.ds(aligned(PAD * (i + DEEP), PAD), PAD * n)

    lanes_pad = lax.broadcasted_iota(jnp.int32, (ROWS, PAD), 1)

    def expand(i, size, ref, column):
        off = column % 128
        x = ref[:, pl.ds(aligned(column - off, 128), PAD)].astype(F32)
        x = pltpu.roll(x, (PAD - off) % PAD, 1)
        buf[0, :, slot(i)] = jnp.where(lanes_pad < size, x, 0.0).astype(BF16)

    for i in range(NE):
        start = NB * i // 128 * 128
        x = raw[:, pl.ds(aligned(base + start, 128), PAD)].astype(F32)
        if NB * i > start:
            x = pltpu.roll(x, PAD - (NB * i - start), 1)
        buf[0, :, slot(i)] = jnp.where(lanes_pad < own_size[i], x, 0.0).astype(BF16)
    for j in range(-1, -DEEP - 1, -1):
        column = jnp.where(first, COLS + NB * (-1 - j), EDGE + NB * j)
        expand(on_side(CHIP, j), number(sizes, sizes_out, CHIP, j), raw, column)

    def element(t, i, own):
        now, prior, targets = [
            (0, None, [1]),
            (1, 0, [0, 2]),
            (0, 1, [1, 3]),
            (3, 2, [2]),
            (2, 3, [3]),
            (3, 2, [2]),
        ][t]
        acc = jnp.dot(
            buf[now, :, slot(i - 1, 3)], wts[i + DEEP - 1], preferred_element_type=F32
        )
        shifted = acc - CENTER * buf[now, :, slot(i)].astype(F32)
        if t == 0:
            nxt = shifted * (1.0 / HALF)
        else:
            nxt = shifted * (2.0 / HALF) - buf[prior, :, slot(i)].astype(F32)
        nxt = nxt.astype(BF16)
        for target in targets:
            if own or target < 2 or t >= DEEP:
                buf[target, :, slot(i)] = nxt

    def inside(t0):
        for k in range(DEEP):
            for i in range(k + 1, NE - k - 1):
                element(t0 + k, i, True)

    def side_steps(t0, side, k):
        for j in range(k + 1 - DEEP, k + 1):
            element(t0 + k, on_side(side, j), j >= 0 or k == DEEP - 2)

    def pass_on(k, source, target, skip, n):
        v, w = buf.at[source], buf.at[target]
        src = slot(jnp.where(first, NE - n - skip, skip), n)
        dst = slot(jnp.where(first, -n - skip, NE + skip), n)
        return outer(k, v.at[:, src], w.at[:, dst], partner)

    second = pass_on(6, 0, 2, DEEP - 2, 1)
    third = pass_on(7, 1, 3, 0, DEEP)
    packed_copy = outer(8, packed.at[0], packed.at[1], across_chip)
    sent = [(1, j) for j in range(DEEP)] + [(0, DEEP - 2)]

    def pack():
        for k, (source, j) in enumerate(sent):
            at_slot = on_side(ICI, j)
            start = aligned(PAD * (at_slot + DEEP), PAD)
            packed[0, :, 128 * k : 128 * (k + 1)] = buf[source, :, pl.ds(start, 128)]
            x = buf[source, :, pl.ds(aligned(start + 128, 128), 128)].astype(F32)
            if k:
                x = pltpu.roll(x, REST * k, 1)
            rest = x if k == 0 else rest + x
        packed[0, :, 512:640] = rest.astype(BF16)

    def unpack():
        rest = packed[1, :, 512:640].astype(F32)
        for k, (source, j) in enumerate(sent):
            start = aligned(PAD * (on_side(ICI, -1 - j) + DEEP), PAD)
            buf[source + 2, :, pl.ds(start, 128)] = packed[1, :, 128 * k : 128 * (k + 1)]
            x = pltpu.roll(rest, 128 - REST * k, 1) if k else rest
            x = jnp.where(lanes_pad[:, 0:128] < REST, x, 0.0).astype(BF16)
            buf[source + 2, :, pl.ds(aligned(start + 128, 128), 128)] = x

    def first_steps(side):
        for k in range(DEEP):
            side_steps(0, side, k)
        if side == CHIP:
            second.start()
            third.start()
        else:
            pack()
            packed_copy.start()

    pl.semaphore_wait(round1, len(links))
    tell(round2, links + [far[0], far[ZL - 2]])
    side_weights(CHIP)
    inside(0)
    first_steps(CHIP)
    pl.semaphore_wait(round2, len(links) + 2)
    tell(round3, links)
    for copy in blocks:
        copy.wait_recv()
    c_got, d_got = jnp.where(first, 0, DEEP + NE), jnp.where(first, 0, DEEP - 1 + NE)
    for k in range(DEEP):
        cbuf[c_got + k, :, 128:NB] = tails[1, :, REST * k : REST * (k + 1)]
    for k in range(n_e):
        turned = nt_dot(eye[0:128, 0:128], dbuf[d_got + k, 128:NB, 0:128])
        dbuf[d_got + k, 0:128, 128:NB] = turned.astype(BF16)
        corner = tails[1, REST * k : REST * (k + 1), REST * DEEP : 128]
        dbuf[d_got + k, 128:NB, 128:NB] = corner
    side_weights(ICI)
    vectors.wait_recv()
    for j in range(-1, -DEEP - 1, -1):
        column = jnp.where(first, EDGE + NB * j, NB * (-1 - j))
        expand(on_side(ICI, j), number(sizes, sizes_out, ICI, j), edges, column)
    first_steps(ICI)
    inside(DEEP)
    second.wait_recv()
    third.wait_recv()
    for k in range(DEEP):
        side_steps(DEEP, CHIP, k)
    packed_copy.wait_recv()
    unpack()
    for k in range(DEEP):
        side_steps(DEEP, ICI, k)

    pl.semaphore_wait(round3, len(links))

    final = 2
    chunks = {}
    for i in range(NE):
        start = (NB * i) // 128
        off = NB * i - 128 * start
        x = buf[final, :, slot(i)].astype(F32)
        if off:
            x = pltpu.roll(x, off, 1)
        for k in range(2):
            part = x[:, 128 * k : 128 * (k + 1)]
            at_chunk = start + k
            chunks[at_chunk] = chunks[at_chunk] + part if at_chunk in chunks else part
        done_to = COLS // 128 if i == NE - 1 else (NB * (i + 1)) // 128
        for c in sorted(chunks):
            if c < done_to:
                fall[core, chip, :, 128 * c : 128 * (c + 1)] = chunks.pop(c).astype(BF16)

    y_up, y_dn, y_far = (y + 1) % NY, (y + NY - 1) % NY, (y + 2) % NY
    peer_chip = (1 - xh) * NY + y
    side, far_side = xh * NY, (1 - xh) * NY
    low, high = slice(0, HALFROWS), slice(HALFROWS, ROWS)

    held = fall.at[core]

    def gather(k, g, rows, who):
        part = held.at[g] if rows is None else held.at[g, rows]
        copy = remote(part, part, gat_send.at[k], gat_recv.at[k], who)
        copy.start()
        sends.append(copy)
        return copy

    def share(k, g):
        copy = gather(14 + k, g, None, partner)
        shared.append(copy)

    sends, shared = [], []
    from_dn = [gather(1, chip, low, yup)]
    from_up = [gather(3, chip, high, ydn)]
    from_x = gather(0, chip, None, xpeer)
    from_dn.append(gather(2, chip, high, yup))
    from_up.append(gather(4, chip, low, ydn))
    share(0, chip)

    r128 = lax.broadcasted_iota(jnp.int32, (ROWS, ROWS), 0)
    c128 = lax.broadcasted_iota(jnp.int32, (ROWS, ROWS), 1)

    def gram(part, g, o):
        strip[o, part] = nt_dot(held[g], held[side + (y + o) % NY])

    def squares(k, s, who):
        copy = remote(sqs.at[s], sqr.at[k], sq_send.at[k], sq_recv.at[k], who)
        copy.start()
        sends.append(copy)
        return copy

    def stage(k, src, dst, who):
        return remote(src, dst, red_send.at[k], red_recv.at[k], who)

    quarter = HALFROWS // XL
    row0 = pl.multiple_of(core * HALFROWS + xl * quarter, quarter)
    piece_rows = pl.ds(row0, quarter)

    def over_cores(offsets):
        copies = []
        for o in offsets:
            s1[o] = strip[o, :, other_rows, :].astype(BF16)
            copies.append(stage(o, s1.at[o], r1.at[o], partner))
            copies[-1].start()
        sends.extend(copies)
        return copies

    def to_owner(o, dx):
        col = (y + o) % NY
        j = dx * ZL + (col + ZL - zl) % ZL
        xl_ = (xl + dx) % XL
        rows = pl.ds(pl.multiple_of(xl_ * quarter, quarter), quarter)
        who = at(xl_ * ZN + zh * ZL + col, b)
        copy = remote(
            s2.at[o, :, rows], r2.at[j - 1], red_send.at[j + 4], red_recv.at[j + 4], who
        )
        return copy, col != zl

    def to_owners(offsets, copies):
        for o, copy in zip(offsets, copies):
            copy.wait_recv()
            half = strip[o, :, my_rows, :] + r1[o].astype(F32)
            strip[o, :, my_rows, :] = half
            s2[o] = half.astype(BF16)
            crossing, _ = to_owner(o, 1)
            crossing.start()
            along, away = to_owner(o, 0)

            @pl.when(away)
            def _():
                along.start()

    gram(0, chip, 0)
    norm = jnp.sum(jnp.where(r128 == c128, strip[0, 0], 0.0), axis=0, keepdims=True)
    sqs[0] = jnp.broadcast_to(norm, (CHIPS, ROWS))
    of_core = squares(0, 0, partner)
    from_dn[0].wait_recv()
    on_up = gather(5, side + y_dn, low, yup)
    from_up[0].wait_recv()
    on_dn = gather(6, side + y_up, high, ydn)
    of_core.wait_recv()
    sqs[1] = sqs[0] + sqr[0]
    of_near = [squares(j, 1, near[j - 1]) for j in range(1, XL * ZL)]
    from_dn[1].wait_recv()
    gram(0, chip, 3)
    from_up[1].wait_recv()
    gram(0, chip, 1)
    from_x.wait_recv()
    late_dn = [gather(7, peer_chip, low, yup)]
    late_up = [gather(9, peer_chip, high, ydn)]
    late_dn.append(gather(8, peer_chip, high, yup))
    late_up.append(gather(10, peer_chip, low, ydn))
    early, last = (0, 3, 1), (2,)
    for o in early:
        gram(1, peer_chip, o)
    first_sums = over_cores(early)
    to_owners(early, first_sums)
    for copy in of_near:
        copy.wait_recv()
    norm = sqs[1]
    for j in range(1, XL * ZL):
        norm = norm + sqr[j]
    sqs[2] = norm
    of_far = [squares(7 + j, 2, far[j - 1]) for j in range(1, ZL)]
    on_up.wait_recv()
    on_dn.wait_recv()
    gram(0, chip, 2)
    gram(1, peer_chip, 2)
    last_sums = over_cores(last)
    to_owners(last, last_sums)
    share(1, side + y_dn)
    share(2, side + y_up)
    share(3, side + y_far)
    share(4, peer_chip)

    copies = [stage(4 + j, r2.at[j - 1], r2.at[j - 1], near[j - 1]) for j in range(1, XL * ZL)]
    for copy in copies:
        copy.wait_recv()
    total = strip[(zl + NY - y) % NY, :, piece_rows, :]
    for j in range(1, XL * ZL):
        total = total + r2[j - 1].astype(F32)
    s3[...] = total.astype(BF16)
    copies = [stage(11 + j, s3, r3.at[j - 1], far[j - 1]) for j in range(1, ZL)]
    for copy in copies:
        copy.start()
    sends.extend(copies)

    for copy in of_far:
        copy.wait_recv()
    norm = sqs[2]
    for j in range(1, ZL):
        norm = norm + sqr[7 + j]
    sqs[3] = norm
    norms = [squares(11 + k, 3, who) for k, who in enumerate((yup, ydn, yfar, xpeer))]
    late_dn[0].wait_recv()
    late_on_up = gather(11, far_side + y_dn, low, yup)
    late_up[0].wait_recv()
    late_on_dn = gather(12, far_side + y_up, high, ydn)
    late_dn[1].wait_recv()
    share(5, far_side + y_dn)
    late_up[1].wait_recv()
    share(6, far_side + y_up)
    for copy in norms:
        copy.wait_recv()
    for copy in copies:
        copy.wait_recv()
    for j in range(1, ZL):
        total = total + r3[j - 1].astype(F32)

    ri = lax.broadcasted_iota(jnp.int32, (quarter, ROWS), 0) + row0
    ci = lax.broadcasted_iota(jnp.int32, (quarter, ROWS), 1)
    same = ri == ci
    g = side + zl
    by_offset = [sqs[3, 0:1], sqr[12, 0:1], sqr[13, 0:1], sqr[11, 0:1]]
    sq_row = by_offset[0]
    for o in range(1, NY):
        here = jnp.full((1, ROWS), (zl + NY - y) % NY, jnp.int32) == o
        sq_row = jnp.where(here, by_offset[o], sq_row)
    scale_row = lax.rsqrt(sq_row + EPS)
    for part in range(2):
        lanes = lax.rsqrt((sqs[3, 0:1] if part == 0 else sqr[14, 0:1]) + EPS)
        row_scale = jnp.sum(jnp.where(same, lanes, 0.0), axis=1, keepdims=True)
        value = total[part]
        ident = jnp.zeros_like(value)
        if part == 0:
            unit = jnp.logical_and(same, jnp.full(same.shape, zl - y, jnp.int32) == 0)
            value = jnp.where(unit, sq_row, value)
            ident = jnp.where(unit, 1.5, 0.0)
        normed = row_scale * value * scale_row
        w = math.sqrt(total_rows) * scale_row * (ident - 0.5 * normed)
        s4[part] = w.astype(BF16)

    g_cols = pl.ds(pl.multiple_of(g * ROWS, ROWS), ROWS)
    place = wfull.at[pl.ds(pl.multiple_of(xl * quarter, quarter), quarter), g_cols]
    put = pltpu.make_async_copy(s4.at[0], place, local_sem.at[4])
    put.start()
    copies = [stage(14 + j, s4.at[0], place, near[j - 1]) for j in range(1, XL * ZL)]
    copies += [stage(22 + j, s4.at[1], place, across[j]) for j in range(XL * ZL)]
    for copy in copies:
        copy.start()
    late_on_up.wait_recv()
    late_on_dn.wait_recv()
    share(7, far_side + y_far)
    for copy in shared:
        copy.wait_recv()
    for copy in copies:
        copy.wait_recv()
    put.wait()
    sends += copies

    writes = []
    for h in range(2):
        whole = fall.at[h].reshape(BANDS, COLS)
        for k in range(COLS // PAD):
            obuf[h, :, PAD * k : PAD * (k + 1)] = jnp.dot(
                wfull[...], whole[:, PAD * k : PAD * (k + 1)], preferred_element_type=F32
            ).astype(BF16)
        write = pltpu.make_async_copy(obuf.at[h], (out_low, out_high)[h], local_sem.at[3 + 4 * h])
        write.start()
        writes.append(write)
    for o in range(NY):
        crossing, _ = to_owner(o, 1)
        crossing.wait_send()
        along, away = to_owner(o, 0)

        @pl.when(away)
        def _():
            along.wait_send()

    for copy in sends + blocks + [vectors, swap, second, third, packed_copy]:
        copy.wait_send()
    for write in writes:
        write.wait()


def shards(basis_sizes, coupling_pattern, h_diag, h_couple, bands):
    total_rows = h_diag.shape[0] * lax.axis_size("elem") * h_diag.shape[1]
    hbm = pl.BlockSpec(memory_space=pltpu.HBM)
    dma = pltpu.SemaphoreType.DMA
    quarter = HALFROWS // XL
    halves = pl.pallas_call(
        functools.partial(kernel, total_rows),
        out_shape=[jax.ShapeDtypeStruct((HALFROWS, COLS), BF16)] * 2,
        in_specs=[hbm] * 5,
        out_specs=[hbm, hbm],
        scratch_shapes=[
            pltpu.VMEM((NE + 2 * DEEP - 2, 3 * PAD, PAD), BF16),
            pltpu.VMEM((4, ROWS, PAD * (NE + 2 * DEEP)), BF16),
            pltpu.VMEM((NE + 2 * DEEP - 2, NB, NB), BF16),
            pltpu.VMEM((NE + 2 * DEEP, NB, NB), BF16),
            pltpu.VMEM((ROWS, COLS + EDGE), BF16),
            pltpu.VMEM((ROWS, EDGE), BF16),
            pltpu.VMEM((2, NB, 128), BF16),
            pltpu.VMEM((2, ROWS, 640), BF16),
            pltpu.VMEM((2, CHIPS, ROWS, COLS), BF16),
            pltpu.VMEM((NY, 2, ROWS, ROWS), F32),
            pltpu.VMEM((NY, 2, HALFROWS, ROWS), BF16),
            pltpu.VMEM((NY, 2, HALFROWS, ROWS), BF16),
            pltpu.VMEM((NY, 2, HALFROWS, ROWS), BF16),
            pltpu.VMEM((XL * ZL - 1, 2, quarter, ROWS), BF16),
            pltpu.VMEM((2, quarter, ROWS), BF16),
            pltpu.VMEM((ZL - 1, 2, quarter, ROWS), BF16),
            pltpu.VMEM((2, quarter, ROWS), BF16),
            pltpu.VMEM((4, CHIPS, ROWS), F32),
            pltpu.VMEM((15, CHIPS, ROWS), F32),
            pltpu.VMEM((HALFROWS, BANDS), BF16),
            pltpu.VMEM((2, HALFROWS, COLS), BF16),
            *[pltpu.SMEM((2 * NE,), jnp.int32)] * 4,
            *[pltpu.SemaphoreType.REGULAR] * 3,
            dma((8,)),
            dma((9,)),
            dma((9,)),
            dma((22,)),
            dma((22,)),
            dma((30,)),
            dma((30,)),
            dma((15,)),
            dma((15,)),
        ],
        compiler_params=pltpu.CompilerParams(
            collective_id=0, has_side_effects=True, vmem_limit_bytes=67043328
        ),
        name="filter_step",
    )(basis_sizes, coupling_pattern, h_diag, h_couple, bands)
    return jnp.concatenate(halves, axis=1)


def solution(mesh):
    in_specs = (
        P("elem"),
        P("elem"),
        P("elem", None, None),
        P("elem", None, None),
        P("band", "elem"),
    )
    out_specs = P("band", "elem")
    return jax.shard_map(shards, mesh=mesh, in_specs=in_specs, out_specs=out_specs, check_vma=False)
```

```python
import functools
import math

import jax
import jax.numpy as jnp
from jax import lax
from jax.experimental import pallas as pl
from jax.experimental.pallas import tpu as pltpu
from jax.sharding import PartitionSpec as P

MESH = pl.DeviceIdType.MESH
DEGREE = 6
CENTER = 0.4
HALF = 2.8
EPS = 1e-06
F32 = jnp.float32
BF16 = jnp.bfloat16

NB = 160
PAD = 256
NE = 8
ROWS = 128
HALFROWS = 64
COLS = NE * NB
DEEP = 3
EDGE = 512
REST = NB - 128
ZL = 4
ZN = 16
XL = 2
NY = 4
CHIPS = 8
BANDS = ROWS * CHIPS


def nt_dot(a, b):
    return lax.dot_general(a, b, (((1,), (1,)), ((), ())), preferred_element_type=F32)


def kernel(
    total_rows,
    sizes_hbm,
    pattern_hbm,
    hd,
    hc,
    bands,
    out_low,
    out_high,
    wts,
    buf,
    dbuf,
    cbuf,
    raw,
    edges,
    tails,
    packed,
    fall,
    strip,
    s1,
    r1,
    s2,
    r2,
    s3,
    r3,
    s4,
    sqs,
    sqr,
    wfull,
    halfsum,
    obuf,
    sizes,
    pattern,
    sizes_out,
    pattern_out,
    round1,
    round2,
    round3,
    local_sem,
    ext_send,
    ext_recv,
    gat_send,
    gat_recv,
    red_send,
    red_recv,
    sq_send,
    sq_recv,
):
    e = lax.axis_index("elem")
    b = lax.axis_index("band")
    ne = lax.axis_size("elem")
    core = b % 2
    other = 1 - core
    chip = b // 2
    xh = chip // NY
    y = chip % NY
    xl = e // ZN
    z = e % ZN
    zh = z // ZL
    zl = z % ZL

    def at(e_, b_):
        return (e_, b_)

    partner = at(e, chip * 2 + other)
    first = core == 0
    across_chip = at((e + jnp.where(first, ne - 1, 1)) % ne, chip * 2 + other)
    xpeer = at(e, ((1 - xh) * NY + y) * 2 + core)
    yup = at(e, (xh * NY + (y + 1) % NY) * 2 + core)
    ydn = at(e, (xh * NY + (y + NY - 1) % NY) * 2 + core)
    places = [((xl + j // ZL) % XL) * ZN + zh * ZL + (zl + j) % ZL for j in range(XL * ZL)]
    near = [at(p, b) for p in places[1:]]
    across = [at(p, xpeer[1]) for p in places]
    far = [at(xl * ZN + ((zh + j) % ZL) * ZL + zl, b) for j in range(1, ZL)]

    barrier = pltpu.get_barrier_semaphore()
    zs = [at(xl * ZN + (z + d) % ZN, b) for d in (1, ZN - 1, 2, ZN - 2)]
    links = zs + [xpeer, at((1 - xl) * ZN + z, b), yup, ydn]
    friends = [partner, across_chip] + links
    yfar = at(e, (xh * NY + (y + 2) % NY) * 2 + core)

    def tell(sem, whom):
        for who in whom:
            pl.semaphore_signal(sem, inc=1, device_id=who, device_id_type=MESH)

    tell(barrier, friends)

    def remote(src, dst, ss, rs, who):
        return pltpu.make_async_remote_copy(
            src_ref=src, dst_ref=dst, send_sem=ss, recv_sem=rs, device_id=who, device_id_type=MESH
        )

    def aligned(x, n):
        return pl.multiple_of(x, n)

    my_rows = pl.ds(aligned(core * HALFROWS, HALFROWS), HALFROWS)
    other_rows = pl.ds(aligned(other * HALFROWS, HALFROWS), HALFROWS)

    n_c, n_d = NE + DEEP, NE + DEEP - 1
    c_at, d_at = jnp.where(first, DEEP, 0), jnp.where(first, DEEP - 1, 0)
    load_c = pltpu.make_async_copy(
        hc.at[pl.ds(core * (NE - DEEP), n_c)], cbuf.at[pl.ds(c_at, n_c)], local_sem.at[0]
    )
    load_d = pltpu.make_async_copy(
        hd.at[pl.ds(core * (NE - DEEP + 1), n_d)], dbuf.at[pl.ds(d_at, n_d)], local_sem.at[1]
    )
    wide = COLS + EDGE
    base = aligned(core * EDGE, 128)
    mine = pl.ds(aligned(core * (COLS - EDGE), 128), wide)
    theirs = pl.ds(aligned(other * (COLS - EDGE), 128), wide)
    load_v = pltpu.make_async_copy(bands.at[:, mine], raw.at[my_rows], local_sem.at[2])
    load_s = pltpu.make_async_copy(sizes_hbm, sizes, local_sem.at[5])
    load_p = pltpu.make_async_copy(pattern_hbm, pattern, local_sem.at[6])
    for load in (load_s, load_p, load_c, load_d, load_v):
        load.start()

    pl.semaphore_wait(barrier, len(friends))

    tell(round1, links)

    def outer(k, src, dst, who):
        return remote(src, dst, ext_send.at[k], ext_recv.at[k], who)

    swap = remote(bands.at[:, theirs], raw.at[my_rows], gat_send.at[13], gat_recv.at[13], partner)
    swap.start()
    head, n_e = slice(0, 128), DEEP - 1
    c_out = jnp.where(first, 0, 2 * NE - DEEP)
    d_out = jnp.where(first, 0, 2 * NE - DEEP + 1)
    c_in, d_in = jnp.where(first, DEEP + NE, 0), jnp.where(first, DEEP - 1 + NE, 0)
    blocks = [
        outer(0, sizes_hbm, sizes_out, across_chip),
        outer(1, pattern_hbm, pattern_out, across_chip),
        outer(2, hc.at[pl.ds(c_out, DEEP), :, head], cbuf.at[pl.ds(c_in, DEEP), :, head], across_chip),
        outer(3, hd.at[pl.ds(d_out, n_e), :, head], dbuf.at[pl.ds(d_in, n_e), :, head], across_chip),
    ]
    for copy in blocks:
        copy.start()
    for load in (load_s, load_p, load_c, load_d):
        load.wait()
    c_from = jnp.where(first, DEEP, NE)
    d_from = jnp.where(first, DEEP - 1, NE)
    for k in range(DEEP):
        tails[0, :, REST * k : REST * (k + 1)] = cbuf[c_from + k, :, 128:NB]
    for k in range(n_e):
        tails[0, REST * k : REST * (k + 1), REST * DEEP : 128] = dbuf[d_from + k, 128:NB, 128:NB]
    blocks.append(outer(5, tails.at[0], tails.at[1], across_chip))
    blocks[-1].start()

    wts[...] = jnp.zeros_like(wts)
    load_v.wait()
    swap.wait_recv()
    edge_out = pl.ds(aligned(core * COLS, 128), EDGE)
    vectors = outer(4, raw.at[:, edge_out], edges, across_chip)
    vectors.start()

    ICI, CHIP = 0, 1

    def on_side(side, j):
        return jnp.where(first, j, NE - 1 - j) if side == ICI else jnp.where(first, NE - 1 - j, j)

    def number(table, table_out, side, j):
        if side == ICI and j < 0:
            return table_out[jnp.where(first, 2 * NE + j, -1 - j)]
        if side == ICI:
            return table[jnp.where(first, j, 2 * NE - 1 - j)]
        return table[jnp.where(first, NE - 1 - j, NE + j)]

    lanes_nb = lax.broadcasted_iota(jnp.int32, (NB, NB), 1)
    eye = (lax.broadcasted_iota(jnp.int32, (NB, NB), 0) == lanes_nb).astype(BF16)

    def coupled(i, on):
        gate = jnp.full((NB, NB), on, jnp.int32) != 0
        return jnp.where(gate, cbuf[i + DEEP].astype(F32), 0.0)

    def put_weights(i, row, value, size):
        at_row = slice(row * PAD, row * PAD + NB)
        keep = lanes_nb < size
        wts[i + DEEP - 1, at_row, 0:NB] = jnp.where(keep, value, 0.0).astype(BF16)

    own_size = [sizes[core * NE + i] for i in range(NE)]
    for i in range(NE):
        put_weights(i, 1, dbuf[i + DEEP - 1].astype(F32), own_size[i])
        if i + 1 < NE:
            pc = coupled(i, pattern[core * NE + i])
            put_weights(i, 2, nt_dot(eye, pc.astype(BF16)), own_size[i])
            put_weights(i + 1, 0, pc, own_size[i + 1])

    def side_weights(side):
        left_side = first if side == ICI else jnp.logical_not(first)
        count = number

        for j in range(-1, -DEEP, -1):
            i = on_side(side, j)
            size = count(sizes, sizes_out, side, j)
            put_weights(i, 1, dbuf[i + DEEP - 1].astype(F32), size)
        for j in range(0, -DEEP, -1):
            low = jnp.where(left_side, on_side(side, j - 1), on_side(side, j))
            on = jnp.where(
                left_side,
                count(pattern, pattern_out, side, j - 1),
                count(pattern, pattern_out, side, j),
            )
            pc = coupled(low, on)
            turned = nt_dot(eye, pc.astype(BF16))
            inner, outer_ = on_side(side, j), on_side(side, j - 1)
            size = count(sizes, sizes_out, side, j)
            value = jnp.where(left_side, pc, turned)
            put_weights_at(inner, jnp.where(left_side, 0, 2), value, size)
            if j > 1 - DEEP:
                size = count(sizes, sizes_out, side, j - 1)
                value = jnp.where(left_side, turned, pc)
                put_weights_at(outer_, jnp.where(left_side, 2, 0), value, size)

    def put_weights_at(i, row, value, size):
        keep = lanes_nb < size
        rows = pl.ds(aligned(row * PAD, PAD), NB)
        wts[i + DEEP - 1, rows, 0:NB] = jnp.where(keep, value, 0.0).astype(BF16)

    def slot(i, n=1):
        if isinstance(i, int):
            return slice(PAD * (i + DEEP), PAD * (i + DEEP + n))
        return pl.ds(aligned(PAD * (i + DEEP), PAD), PAD * n)

    lanes_pad = lax.broadcasted_iota(jnp.int32, (ROWS, PAD), 1)

    def expand(i, size, ref, column):
        off = column % 128
        x = ref[:, pl.ds(aligned(column - off, 128), PAD)].astype(F32)
        x = pltpu.roll(x, (PAD - off) % PAD, 1)
        buf[0, :, slot(i)] = jnp.where(lanes_pad < size, x, 0.0).astype(BF16)

    for i in range(NE):
        start = NB * i // 128 * 128
        x = raw[:, pl.ds(aligned(base + start, 128), PAD)].astype(F32)
        if NB * i > start:
            x = pltpu.roll(x, PAD - (NB * i - start), 1)
        buf[0, :, slot(i)] = jnp.where(lanes_pad < own_size[i], x, 0.0).astype(BF16)
    for j in range(-1, -DEEP - 1, -1):
        column = jnp.where(first, COLS + NB * (-1 - j), EDGE + NB * j)
        expand(on_side(CHIP, j), number(sizes, sizes_out, CHIP, j), raw, column)

    plan = [
        (0, None, [1]),
        (1, 0, [0, 2]),
        (0, 1, [1, 3]),
        (3, 2, [2]),
        (2, 3, [3]),
        (3, 2, [2]),
    ]

    def element(t, i, own):
        store(t, i, own, stepped(t, i))

    def stepped(t, i):
        now, prior, _ = plan[t]
        acc = jnp.dot(
            buf[now, :, slot(i - 1, 3)], wts[i + DEEP - 1], preferred_element_type=F32
        )
        shifted = acc - CENTER * buf[now, :, slot(i)].astype(F32)
        if t == 0:
            nxt = shifted * (1.0 / HALF)
        else:
            nxt = shifted * (2.0 / HALF) - buf[prior, :, slot(i)].astype(F32)
        return nxt.astype(BF16)

    def store(t, i, own, nxt):
        for target in plan[t][2]:
            if own or target < 2 or t >= DEEP:
                buf[target, :, slot(i)] = nxt

    def inside(t0):
        for k in range(DEEP):
            for i in range(k + 1, NE - k - 1):
                element(t0 + k, i, True)

    def side_steps(t0, side, k):
        level = range(k + 1 - DEEP, k + 1)
        made = [stepped(t0 + k, on_side(side, j)) for j in level]
        for j, nxt in zip(level, made):
            store(t0 + k, on_side(side, j), j >= 0 or k == DEEP - 2, nxt)

    def pass_on(k, source, target, skip, n):
        v, w = buf.at[source], buf.at[target]
        src = slot(jnp.where(first, NE - n - skip, skip), n)
        dst = slot(jnp.where(first, -n - skip, NE + skip), n)
        return outer(k, v.at[:, src], w.at[:, dst], partner)

    second = pass_on(6, 0, 2, DEEP - 2, 1)
    third = pass_on(7, 1, 3, 0, DEEP)
    packed_copy = outer(8, packed.at[0], packed.at[1], across_chip)
    sent = [(1, j) for j in range(DEEP)] + [(0, DEEP - 2)]

    def pack():
        for k, (source, j) in enumerate(sent):
            at_slot = on_side(ICI, j)
            start = aligned(PAD * (at_slot + DEEP), PAD)
            packed[0, :, 128 * k : 128 * (k + 1)] = buf[source, :, pl.ds(start, 128)]
            x = buf[source, :, pl.ds(aligned(start + 128, 128), 128)].astype(F32)
            if k:
                x = pltpu.roll(x, REST * k, 1)
            rest = x if k == 0 else rest + x
        packed[0, :, 512:640] = rest.astype(BF16)

    def unpack():
        rest = packed[1, :, 512:640].astype(F32)
        for k, (source, j) in enumerate(sent):
            start = aligned(PAD * (on_side(ICI, -1 - j) + DEEP), PAD)
            buf[source + 2, :, pl.ds(start, 128)] = packed[1, :, 128 * k : 128 * (k + 1)]
            x = pltpu.roll(rest, 128 - REST * k, 1) if k else rest
            x = jnp.where(lanes_pad[:, 0:128] < REST, x, 0.0).astype(BF16)
            buf[source + 2, :, pl.ds(aligned(start + 128, 128), 128)] = x

    def first_steps(side):
        for k in range(DEEP):
            side_steps(0, side, k)
        if side == CHIP:
            second.start()
            third.start()
        else:
            pack()
            packed_copy.start()

    pl.semaphore_wait(round1, len(links))
    tell(round2, links + [far[0], far[ZL - 2]])
    side_weights(CHIP)
    inside(0)
    first_steps(CHIP)
    pl.semaphore_wait(round2, len(links) + 2)
    tell(round3, links)
    for copy in blocks:
        copy.wait_recv()
    c_got, d_got = jnp.where(first, 0, DEEP + NE), jnp.where(first, 0, DEEP - 1 + NE)
    for k in range(DEEP):
        cbuf[c_got + k, :, 128:NB] = tails[1, :, REST * k : REST * (k + 1)]
    for k in range(n_e):
        turned = nt_dot(eye[0:128, 0:128], dbuf[d_got + k, 128:NB, 0:128])
        dbuf[d_got + k, 0:128, 128:NB] = turned.astype(BF16)
        corner = tails[1, REST * k : REST * (k + 1), REST * DEEP : 128]
        dbuf[d_got + k, 128:NB, 128:NB] = corner
    side_weights(ICI)
    vectors.wait_recv()
    for j in range(-1, -DEEP - 1, -1):
        column = jnp.where(first, EDGE + NB * j, NB * (-1 - j))
        expand(on_side(ICI, j), number(sizes, sizes_out, ICI, j), edges, column)
    first_steps(ICI)
    inside(DEEP)
    second.wait_recv()
    third.wait_recv()
    for k in range(DEEP):
        side_steps(DEEP, CHIP, k)
    packed_copy.wait_recv()
    unpack()
    for k in range(DEEP):
        side_steps(DEEP, ICI, k)

    pl.semaphore_wait(round3, len(links))

    final = 2
    chunks = {}
    for i in range(NE):
        start = (NB * i) // 128
        off = NB * i - 128 * start
        x = buf[final, :, slot(i)].astype(F32)
        if off:
            x = pltpu.roll(x, off, 1)
        for k in range(2):
            part = x[:, 128 * k : 128 * (k + 1)]
            at_chunk = start + k
            chunks[at_chunk] = chunks[at_chunk] + part if at_chunk in chunks else part
        done_to = COLS // 128 if i == NE - 1 else (NB * (i + 1)) // 128
        for c in sorted(chunks):
            if c < done_to:
                fall[core, chip, :, 128 * c : 128 * (c + 1)] = chunks.pop(c).astype(BF16)

    y_up, y_dn, y_far = (y + 1) % NY, (y + NY - 1) % NY, (y + 2) % NY
    peer_chip = (1 - xh) * NY + y
    side, far_side = xh * NY, (1 - xh) * NY
    low, high = slice(0, HALFROWS), slice(HALFROWS, ROWS)

    held = fall.at[core]

    def gather(k, g, rows, who):
        part = held.at[g] if rows is None else held.at[g, rows]
        copy = remote(part, part, gat_send.at[k], gat_recv.at[k], who)
        copy.start()
        sends.append(copy)
        return copy

    def share(k, g):
        copy = gather(14 + k, g, None, partner)
        shared.append(copy)

    sends, shared = [], []
    from_dn = [gather(1, chip, low, yup)]
    from_up = [gather(3, chip, high, ydn)]
    from_x = gather(0, chip, None, xpeer)
    from_dn.append(gather(2, chip, high, yup))
    from_up.append(gather(4, chip, low, ydn))

    r128 = lax.broadcasted_iota(jnp.int32, (ROWS, ROWS), 0)
    c128 = lax.broadcasted_iota(jnp.int32, (ROWS, ROWS), 1)

    def gram(which, g, o):
        strip[o, which] = nt_dot(held[g], held[side + (y + o) % NY])

    def squares(k, s, who):
        copy = remote(sqs.at[s], sqr.at[k], sq_send.at[k], sq_recv.at[k], who)
        copy.start()
        sends.append(copy)
        return copy

    def stage(k, src, dst, who):
        return remote(src, dst, red_send.at[k], red_recv.at[k], who)

    quarter = HALFROWS // XL
    row0 = pl.multiple_of(core * HALFROWS + xl * quarter, quarter)
    piece_rows = pl.ds(row0, quarter)

    def over_cores(offsets):
        copies = []
        for o in offsets:
            s1[o] = strip[o, :, other_rows, :].astype(BF16)
            copies.append(stage(o, s1.at[o], r1.at[o], partner))
            copies[-1].start()
        sends.extend(copies)
        return copies

    def to_owner(o, dx):
        col = (y + o) % NY
        j = dx * ZL + (col + ZL - zl) % ZL
        xl_ = (xl + dx) % XL
        rows = pl.ds(pl.multiple_of(xl_ * quarter, quarter), quarter)
        who = at(xl_ * ZN + zh * ZL + col, b)
        copy = remote(
            s2.at[o, :, rows], r2.at[j - 1], red_send.at[j + 4], red_recv.at[j + 4], who
        )
        return copy, col != zl

    def to_owners(offsets, copies):
        for o, copy in zip(offsets, copies):
            copy.wait_recv()
            half = strip[o, :, my_rows, :] + r1[o].astype(F32)
            strip[o, :, my_rows, :] = half
            s2[o] = half.astype(BF16)
            crossing, _ = to_owner(o, 1)
            crossing.start()
            along, away = to_owner(o, 0)

            @pl.when(away)
            def _():
                along.start()

    gram(0, chip, 0)
    norm = jnp.sum(jnp.where(r128 == c128, strip[0, 0], 0.0), axis=0, keepdims=True)
    sqs[0] = jnp.broadcast_to(norm, (CHIPS, ROWS))
    of_core = squares(0, 0, partner)
    from_dn[0].wait_recv()
    on_up = gather(5, side + y_dn, low, yup)
    from_up[0].wait_recv()
    on_dn = gather(6, side + y_up, high, ydn)
    of_core.wait_recv()
    sqs[1] = sqs[0] + sqr[0]
    of_near = [squares(j, 1, near[j - 1]) for j in range(1, XL * ZL)]
    from_dn[1].wait_recv()
    gram(0, chip, 3)
    from_up[1].wait_recv()
    gram(0, chip, 1)
    from_x.wait_recv()
    late_dn = [gather(7, peer_chip, low, yup)]
    late_up = [gather(9, peer_chip, high, ydn)]
    late_dn.append(gather(8, peer_chip, high, yup))
    late_up.append(gather(10, peer_chip, low, ydn))
    early, last = (0, 3, 1), (2,)
    for o in early:
        gram(1, peer_chip, o)
    first_sums = over_cores(early)
    to_owners(early, first_sums)
    for copy in of_near:
        copy.wait_recv()
    norm = sqs[1]
    for j in range(1, XL * ZL):
        norm = norm + sqr[j]
    sqs[2] = norm
    of_far = [squares(7 + j, 2, far[j - 1]) for j in range(1, ZL)]
    on_up.wait_recv()
    on_dn.wait_recv()
    gram(0, chip, 2)
    gram(1, peer_chip, 2)
    last_sums = over_cores(last)
    to_owners(last, last_sums)
    share(0, chip)
    share(1, side + y_dn)
    share(2, side + y_up)
    share(3, side + y_far)
    share(4, peer_chip)

    copies = [stage(4 + j, r2.at[j - 1], r2.at[j - 1], near[j - 1]) for j in range(1, XL * ZL)]
    for copy in copies:
        copy.wait_recv()
    total = strip[(zl + NY - y) % NY, :, piece_rows, :]
    for j in range(1, XL * ZL):
        total = total + r2[j - 1].astype(F32)
    s3[...] = total.astype(BF16)
    copies = [stage(11 + j, s3, r3.at[j - 1], far[j - 1]) for j in range(1, ZL)]
    for copy in copies:
        copy.start()
    sends.extend(copies)

    for copy in of_far:
        copy.wait_recv()
    norm = sqs[2]
    for j in range(1, ZL):
        norm = norm + sqr[7 + j]
    sqs[3] = norm
    norms = [squares(11 + k, 3, who) for k, who in enumerate((yup, ydn, yfar, xpeer))]
    late_dn[0].wait_recv()
    late_on_up = gather(11, far_side + y_dn, low, yup)
    late_up[0].wait_recv()
    late_on_dn = gather(12, far_side + y_up, high, ydn)
    late_dn[1].wait_recv()
    share(5, far_side + y_dn)
    late_up[1].wait_recv()
    share(6, far_side + y_up)
    for copy in norms:
        copy.wait_recv()
    for copy in copies:
        copy.wait_recv()
    for j in range(1, ZL):
        total = total + r3[j - 1].astype(F32)

    ri = lax.broadcasted_iota(jnp.int32, (quarter, ROWS), 0) + row0
    ci = lax.broadcasted_iota(jnp.int32, (quarter, ROWS), 1)
    same = ri == ci
    g = side + zl
    by_offset = [sqs[3, 0:1], sqr[12, 0:1], sqr[13, 0:1], sqr[11, 0:1]]
    sq_row = by_offset[0]
    for o in range(1, NY):
        here = jnp.full((1, ROWS), (zl + NY - y) % NY, jnp.int32) == o
        sq_row = jnp.where(here, by_offset[o], sq_row)
    scale_row = lax.rsqrt(sq_row + EPS)
    for rows_of in range(2):
        lanes = lax.rsqrt((sqs[3, 0:1] if rows_of == 0 else sqr[14, 0:1]) + EPS)
        row_scale = jnp.sum(jnp.where(same, lanes, 0.0), axis=1, keepdims=True)
        value = total[rows_of]
        ident = jnp.zeros_like(value)
        if rows_of == 0:
            unit = jnp.logical_and(same, jnp.full(same.shape, zl - y, jnp.int32) == 0)
            value = jnp.where(unit, sq_row, value)
            ident = jnp.where(unit, 1.5, 0.0)
        normed = row_scale * value * scale_row
        w = math.sqrt(total_rows) * scale_row * (ident - 0.5 * normed)
        s4[rows_of] = w.astype(BF16)

    g_cols = pl.ds(pl.multiple_of(g * ROWS, ROWS), ROWS)
    place = wfull.at[pl.ds(pl.multiple_of(xl * quarter, quarter), quarter), g_cols]
    put = pltpu.make_async_copy(s4.at[0], place, local_sem.at[4])
    put.start()
    copies = [stage(14 + j, s4.at[0], place, near[j - 1]) for j in range(1, XL * ZL)]
    copies += [stage(22 + j, s4.at[1], place, across[j]) for j in range(XL * ZL)]
    for copy in copies:
        copy.start()
    late_on_up.wait_recv()
    late_on_dn.wait_recv()
    share(7, far_side + y_far)
    for copy in shared:
        copy.wait_recv()
    near_cols = pl.ds(pl.multiple_of(side * ROWS, 128), NY * ROWS)
    far_cols = pl.ds(pl.multiple_of(far_side * ROWS, 128), NY * ROWS)
    for copy in copies[: XL * ZL - 1]:
        copy.wait_recv()
    put.wait()
    for h in range(2):
        whole = fall.at[h].reshape(BANDS, COLS)
        for k in range(COLS // PAD):
            halfsum[h, :, PAD * k : PAD * (k + 1)] = jnp.dot(
                wfull[:, near_cols],
                whole[near_cols, PAD * k : PAD * (k + 1)],
                preferred_element_type=F32,
            )
    for copy in copies[XL * ZL - 1 :]:
        copy.wait_recv()
    sends += copies

    writes = []
    for h in range(2):
        whole = fall.at[h].reshape(BANDS, COLS)
        for k in range(COLS // PAD):
            more = jnp.dot(
                wfull[:, far_cols],
                whole[far_cols, PAD * k : PAD * (k + 1)],
                preferred_element_type=F32,
            )
            obuf[h, :, PAD * k : PAD * (k + 1)] = (
                halfsum[h, :, PAD * k : PAD * (k + 1)] + more
            ).astype(BF16)
        write = pltpu.make_async_copy(obuf.at[h], (out_low, out_high)[h], local_sem.at[3 + 4 * h])
        write.start()
        writes.append(write)
    for o in range(NY):
        crossing, _ = to_owner(o, 1)
        crossing.wait_send()
        along, away = to_owner(o, 0)

        @pl.when(away)
        def _():
            along.wait_send()

    for copy in sends + blocks + [vectors, swap, second, third, packed_copy]:
        copy.wait_send()
    for write in writes:
        write.wait()


def shards(basis_sizes, coupling_pattern, h_diag, h_couple, bands):
    total_rows = h_diag.shape[0] * lax.axis_size("elem") * h_diag.shape[1]
    hbm = pl.BlockSpec(memory_space=pltpu.HBM)
    dma = pltpu.SemaphoreType.DMA
    quarter = HALFROWS // XL
    halves = pl.pallas_call(
        functools.partial(kernel, total_rows),
        out_shape=[jax.ShapeDtypeStruct((HALFROWS, COLS), BF16)] * 2,
        in_specs=[hbm] * 5,
        out_specs=[hbm, hbm],
        scratch_shapes=[
            pltpu.VMEM((NE + 2 * DEEP - 2, 3 * PAD, PAD), BF16),
            pltpu.VMEM((4, ROWS, PAD * (NE + 2 * DEEP)), BF16),
            pltpu.VMEM((NE + 2 * DEEP - 2, NB, NB), BF16),
            pltpu.VMEM((NE + 2 * DEEP, NB, NB), BF16),
            pltpu.VMEM((ROWS, COLS + EDGE), BF16),
            pltpu.VMEM((ROWS, EDGE), BF16),
            pltpu.VMEM((2, NB, 128), BF16),
            pltpu.VMEM((2, ROWS, 640), BF16),
            pltpu.VMEM((2, CHIPS, ROWS, COLS), BF16),
            pltpu.VMEM((NY, 2, ROWS, ROWS), F32),
            pltpu.VMEM((NY, 2, HALFROWS, ROWS), BF16),
            pltpu.VMEM((NY, 2, HALFROWS, ROWS), BF16),
            pltpu.VMEM((NY, 2, HALFROWS, ROWS), BF16),
            pltpu.VMEM((XL * ZL - 1, 2, quarter, ROWS), BF16),
            pltpu.VMEM((2, quarter, ROWS), BF16),
            pltpu.VMEM((ZL - 1, 2, quarter, ROWS), BF16),
            pltpu.VMEM((2, quarter, ROWS), BF16),
            pltpu.VMEM((4, CHIPS, ROWS), F32),
            pltpu.VMEM((15, CHIPS, ROWS), F32),
            pltpu.VMEM((HALFROWS, BANDS), BF16),
            pltpu.VMEM((2, HALFROWS, COLS), F32),
            pltpu.VMEM((2, HALFROWS, COLS), BF16),
            *[pltpu.SMEM((2 * NE,), jnp.int32)] * 4,
            *[pltpu.SemaphoreType.REGULAR] * 3,
            dma((8,)),
            dma((9,)),
            dma((9,)),
            dma((22,)),
            dma((22,)),
            dma((30,)),
            dma((30,)),
            dma((15,)),
            dma((15,)),
        ],
        compiler_params=pltpu.CompilerParams(
            collective_id=0, has_side_effects=True, vmem_limit_bytes=67043328
        ),
        name="filter_step",
    )(basis_sizes, coupling_pattern, h_diag, h_couple, bands)
    return jnp.concatenate(halves, axis=1)


def solution(mesh):
    in_specs = (
        P("elem"),
        P("elem"),
        P("elem", None, None),
        P("elem", None, None),
        P("band", "elem"),
    )
    out_specs = P("band", "elem")
    return jax.shard_map(shards, mesh=mesh, in_specs=in_specs, out_specs=out_specs, check_vma=False)
```

```python
import functools
import math

import jax
import jax.numpy as jnp
from jax import lax
from jax.experimental import pallas as pl
from jax.experimental.pallas import tpu as pltpu
from jax.sharding import PartitionSpec as P

MESH = pl.DeviceIdType.MESH
DEGREE = 6
CENTER = 0.4
HALF = 2.8
EPS = 1e-06
F32 = jnp.float32
BF16 = jnp.bfloat16

NB = 160
PAD = 256
NE = 8
ROWS = 128
HALFROWS = 64
COLS = NE * NB
DEEP = 3
EDGE = 512
REST = NB - 128
ZL = 4
ZN = 16
XL = 2
NY = 4
CHIPS = 8
BANDS = ROWS * CHIPS


def nt_dot(a, b):
    return lax.dot_general(a, b, (((1,), (1,)), ((), ())), preferred_element_type=F32)


def kernel(
    total_rows,
    sizes_hbm,
    pattern_hbm,
    hd,
    hc,
    bands,
    out,
    wts,
    buf,
    dbuf,
    cbuf,
    raw,
    edges,
    tails,
    packed,
    fall,
    strip,
    s1,
    r1,
    s2,
    r2,
    s3,
    r3,
    s4,
    sqs,
    sqr,
    wfull,
    halfsum,
    sizes,
    pattern,
    sizes_out,
    pattern_out,
    round1,
    round2,
    round3,
    local_sem,
    ext_send,
    ext_recv,
    gat_send,
    gat_recv,
    red_send,
    red_recv,
    sq_send,
    sq_recv,
):
    e = lax.axis_index("elem")
    b = lax.axis_index("band")
    ne = lax.axis_size("elem")
    core = b % 2
    other = 1 - core
    chip = b // 2
    xh = chip // NY
    y = chip % NY
    xl = e // ZN
    z = e % ZN
    zh = z // ZL
    zl = z % ZL

    def at(e_, b_):
        return (e_, b_)

    partner = at(e, chip * 2 + other)
    first = core == 0
    across_chip = at((e + jnp.where(first, ne - 1, 1)) % ne, chip * 2 + other)
    xpeer = at(e, ((1 - xh) * NY + y) * 2 + core)
    yup = at(e, (xh * NY + (y + 1) % NY) * 2 + core)
    ydn = at(e, (xh * NY + (y + NY - 1) % NY) * 2 + core)
    places = [((xl + j // ZL) % XL) * ZN + zh * ZL + (zl + j) % ZL for j in range(XL * ZL)]
    near = [at(p, b) for p in places[1:]]
    across = [at(p, xpeer[1]) for p in places]
    far = [at(xl * ZN + ((zh + j) % ZL) * ZL + zl, b) for j in range(1, ZL)]

    barrier = pltpu.get_barrier_semaphore()
    zs = [at(xl * ZN + (z + d) % ZN, b) for d in (1, ZN - 1, 2, ZN - 2)]
    links = zs + [xpeer, at((1 - xl) * ZN + z, b), yup, ydn]
    friends = [partner, across_chip] + links
    yfar = at(e, (xh * NY + (y + 2) % NY) * 2 + core)

    def tell(sem, whom):
        for who in whom:
            pl.semaphore_signal(sem, inc=1, device_id=who, device_id_type=MESH)

    tell(barrier, friends)

    def remote(src, dst, ss, rs, who):
        return pltpu.make_async_remote_copy(
            src_ref=src, dst_ref=dst, send_sem=ss, recv_sem=rs, device_id=who, device_id_type=MESH
        )

    def aligned(x, n):
        return pl.multiple_of(x, n)

    my_rows = pl.ds(aligned(core * HALFROWS, HALFROWS), HALFROWS)
    other_rows = pl.ds(aligned(other * HALFROWS, HALFROWS), HALFROWS)

    n_c, n_d = NE + DEEP, NE + DEEP - 1
    c_at, d_at = jnp.where(first, DEEP, 0), jnp.where(first, DEEP - 1, 0)
    load_c = pltpu.make_async_copy(
        hc.at[pl.ds(core * (NE - DEEP), n_c)], cbuf.at[pl.ds(c_at, n_c)], local_sem.at[0]
    )
    load_d = pltpu.make_async_copy(
        hd.at[pl.ds(core * (NE - DEEP + 1), n_d)], dbuf.at[pl.ds(d_at, n_d)], local_sem.at[1]
    )
    wide = COLS + EDGE
    base = aligned(core * EDGE, 128)
    mine = pl.ds(aligned(core * (COLS - EDGE), 128), wide)
    theirs = pl.ds(aligned(other * (COLS - EDGE), 128), wide)
    load_v = pltpu.make_async_copy(bands.at[:, mine], raw.at[my_rows], local_sem.at[2])
    load_s = pltpu.make_async_copy(sizes_hbm, sizes, local_sem.at[5])
    load_p = pltpu.make_async_copy(pattern_hbm, pattern, local_sem.at[6])
    for load in (load_s, load_p, load_c, load_d, load_v):
        load.start()

    pl.semaphore_wait(barrier, len(friends))

    tell(round1, links)

    def outer(k, src, dst, who):
        return remote(src, dst, ext_send.at[k], ext_recv.at[k], who)

    swap = remote(bands.at[:, theirs], raw.at[my_rows], gat_send.at[13], gat_recv.at[13], partner)
    swap.start()
    head, n_e = slice(0, 128), DEEP - 1
    c_out = jnp.where(first, 0, 2 * NE - DEEP)
    d_out = jnp.where(first, 0, 2 * NE - DEEP + 1)
    c_in, d_in = jnp.where(first, DEEP + NE, 0), jnp.where(first, DEEP - 1 + NE, 0)
    blocks = [
        outer(0, sizes_hbm, sizes_out, across_chip),
        outer(1, pattern_hbm, pattern_out, across_chip),
        outer(2, hc.at[pl.ds(c_out, DEEP), :, head], cbuf.at[pl.ds(c_in, DEEP), :, head], across_chip),
        outer(3, hd.at[pl.ds(d_out, n_e), :, head], dbuf.at[pl.ds(d_in, n_e), :, head], across_chip),
    ]
    for copy in blocks:
        copy.start()
    for load in (load_s, load_p, load_c, load_d):
        load.wait()
    c_from = jnp.where(first, DEEP, NE)
    d_from = jnp.where(first, DEEP - 1, NE)
    for k in range(DEEP):
        tails[0, :, REST * k : REST * (k + 1)] = cbuf[c_from + k, :, 128:NB]
    for k in range(n_e):
        tails[0, REST * k : REST * (k + 1), REST * DEEP : 128] = dbuf[d_from + k, 128:NB, 128:NB]
    blocks.append(outer(5, tails.at[0], tails.at[1], across_chip))
    blocks[-1].start()

    wts[...] = jnp.zeros_like(wts)
    load_v.wait()
    swap.wait_recv()
    edge_out = pl.ds(aligned(core * COLS, 128), EDGE)
    vectors = outer(4, raw.at[:, edge_out], edges, across_chip)
    vectors.start()

    ICI, CHIP = 0, 1

    def on_side(side, j):
        return jnp.where(first, j, NE - 1 - j) if side == ICI else jnp.where(first, NE - 1 - j, j)

    def number(table, table_out, side, j):
        if side == ICI and j < 0:
            return table_out[jnp.where(first, 2 * NE + j, -1 - j)]
        if side == ICI:
            return table[jnp.where(first, j, 2 * NE - 1 - j)]
        return table[jnp.where(first, NE - 1 - j, NE + j)]

    lanes_nb = lax.broadcasted_iota(jnp.int32, (NB, NB), 1)
    eye = (lax.broadcasted_iota(jnp.int32, (NB, NB), 0) == lanes_nb).astype(BF16)

    def coupled(i, on):
        gate = jnp.full((NB, NB), on, jnp.int32) != 0
        return jnp.where(gate, cbuf[i + DEEP].astype(F32), 0.0)

    def put_weights(i, row, value, size):
        at_row = slice(row * PAD, row * PAD + NB)
        keep = lanes_nb < size
        wts[i + DEEP - 1, at_row, 0:NB] = jnp.where(keep, value, 0.0).astype(BF16)

    own_size = [sizes[core * NE + i] for i in range(NE)]
    for i in range(NE):
        put_weights(i, 1, dbuf[i + DEEP - 1].astype(F32), own_size[i])
        if i + 1 < NE:
            pc = coupled(i, pattern[core * NE + i])
            put_weights(i, 2, nt_dot(eye, pc.astype(BF16)), own_size[i])
            put_weights(i + 1, 0, pc, own_size[i + 1])

    def side_weights(side):
        left_side = first if side == ICI else jnp.logical_not(first)
        count = number

        for j in range(-1, -DEEP, -1):
            i = on_side(side, j)
            size = count(sizes, sizes_out, side, j)
            put_weights(i, 1, dbuf[i + DEEP - 1].astype(F32), size)
        for j in range(0, -DEEP, -1):
            low = jnp.where(left_side, on_side(side, j - 1), on_side(side, j))
            on = jnp.where(
                left_side,
                count(pattern, pattern_out, side, j - 1),
                count(pattern, pattern_out, side, j),
            )
            pc = coupled(low, on)
            turned = nt_dot(eye, pc.astype(BF16))
            inner, outer_ = on_side(side, j), on_side(side, j - 1)
            size = count(sizes, sizes_out, side, j)
            value = jnp.where(left_side, pc, turned)
            put_weights_at(inner, jnp.where(left_side, 0, 2), value, size)
            if j > 1 - DEEP:
                size = count(sizes, sizes_out, side, j - 1)
                value = jnp.where(left_side, turned, pc)
                put_weights_at(outer_, jnp.where(left_side, 2, 0), value, size)

    def put_weights_at(i, row, value, size):
        keep = lanes_nb < size
        rows = pl.ds(aligned(row * PAD, PAD), NB)
        wts[i + DEEP - 1, rows, 0:NB] = jnp.where(keep, value, 0.0).astype(BF16)

    def slot(i, n=1):
        if isinstance(i, int):
            return slice(PAD * (i + DEEP), PAD * (i + DEEP + n))
        return pl.ds(aligned(PAD * (i + DEEP), PAD), PAD * n)

    lanes_pad = lax.broadcasted_iota(jnp.int32, (ROWS, PAD), 1)

    def expand(i, size, ref, column):
        off = column % 128
        x = ref[:, pl.ds(aligned(column - off, 128), PAD)].astype(F32)
        x = pltpu.roll(x, (PAD - off) % PAD, 1)
        buf[0, :, slot(i)] = jnp.where(lanes_pad < size, x, 0.0).astype(BF16)

    for i in range(NE):
        start = NB * i // 128 * 128
        x = raw[:, pl.ds(aligned(base + start, 128), PAD)].astype(F32)
        if NB * i > start:
            x = pltpu.roll(x, PAD - (NB * i - start), 1)
        buf[0, :, slot(i)] = jnp.where(lanes_pad < own_size[i], x, 0.0).astype(BF16)
    for j in range(-1, -DEEP - 1, -1):
        column = jnp.where(first, COLS + NB * (-1 - j), EDGE + NB * j)
        expand(on_side(CHIP, j), number(sizes, sizes_out, CHIP, j), raw, column)

    plan = [
        (0, None, [1]),
        (1, 0, [0, 2]),
        (0, 1, [1, 3]),
        (3, 2, [2]),
        (2, 3, [3]),
        (3, 2, [2]),
    ]

    def element(t, i, own):
        store(t, i, own, stepped(t, i))

    def stepped(t, i):
        now, prior, _ = plan[t]
        acc = jnp.dot(
            buf[now, :, slot(i - 1, 3)], wts[i + DEEP - 1], preferred_element_type=F32
        )
        shifted = acc - CENTER * buf[now, :, slot(i)].astype(F32)
        if t == 0:
            nxt = shifted * (1.0 / HALF)
        else:
            nxt = shifted * (2.0 / HALF) - buf[prior, :, slot(i)].astype(F32)
        return nxt.astype(BF16)

    def store(t, i, own, nxt):
        for target in plan[t][2]:
            if own or target < 2 or t >= DEEP:
                buf[target, :, slot(i)] = nxt

    def inside(t0):
        for k in range(DEEP):
            for i in range(k + 1, NE - k - 1):
                element(t0 + k, i, True)

    def side_steps(t0, side, k):
        level = range(k + 1 - DEEP, k + 1)
        made = [stepped(t0 + k, on_side(side, j)) for j in level]
        for j, nxt in zip(level, made):
            store(t0 + k, on_side(side, j), j >= 0 or k == DEEP - 2, nxt)

    def pass_on(k, source, target, skip, n):
        v, w = buf.at[source], buf.at[target]
        src = slot(jnp.where(first, NE - n - skip, skip), n)
        dst = slot(jnp.where(first, -n - skip, NE + skip), n)
        return outer(k, v.at[:, src], w.at[:, dst], partner)

    second = pass_on(6, 0, 2, DEEP - 2, 1)
    third = pass_on(7, 1, 3, 0, DEEP)
    packed_copy = outer(8, packed.at[0], packed.at[1], across_chip)
    sent = [(1, j) for j in range(DEEP)] + [(0, DEEP - 2)]

    def pack():
        for k, (source, j) in enumerate(sent):
            at_slot = on_side(ICI, j)
            start = aligned(PAD * (at_slot + DEEP), PAD)
            packed[0, :, 128 * k : 128 * (k + 1)] = buf[source, :, pl.ds(start, 128)]
            x = buf[source, :, pl.ds(aligned(start + 128, 128), 128)].astype(F32)
            if k:
                x = pltpu.roll(x, REST * k, 1)
            rest = x if k == 0 else rest + x
        packed[0, :, 512:640] = rest.astype(BF16)

    def unpack():
        rest = packed[1, :, 512:640].astype(F32)
        for k, (source, j) in enumerate(sent):
            start = aligned(PAD * (on_side(ICI, -1 - j) + DEEP), PAD)
            buf[source + 2, :, pl.ds(start, 128)] = packed[1, :, 128 * k : 128 * (k + 1)]
            x = pltpu.roll(rest, 128 - REST * k, 1) if k else rest
            x = jnp.where(lanes_pad[:, 0:128] < REST, x, 0.0).astype(BF16)
            buf[source + 2, :, pl.ds(aligned(start + 128, 128), 128)] = x

    def first_steps(side):
        for k in range(DEEP):
            side_steps(0, side, k)
        if side == CHIP:
            second.start()
            third.start()
        else:
            pack()
            packed_copy.start()

    pl.semaphore_wait(round1, len(links))
    tell(round2, links + [far[0], far[ZL - 2]])
    side_weights(CHIP)
    inside(0)
    first_steps(CHIP)
    pl.semaphore_wait(round2, len(links) + 2)
    tell(round3, links)
    for copy in blocks:
        copy.wait_recv()
    c_got, d_got = jnp.where(first, 0, DEEP + NE), jnp.where(first, 0, DEEP - 1 + NE)
    for k in range(DEEP):
        cbuf[c_got + k, :, 128:NB] = tails[1, :, REST * k : REST * (k + 1)]
    for k in range(n_e):
        turned = nt_dot(eye[0:128, 0:128], dbuf[d_got + k, 128:NB, 0:128])
        dbuf[d_got + k, 0:128, 128:NB] = turned.astype(BF16)
        corner = tails[1, REST * k : REST * (k + 1), REST * DEEP : 128]
        dbuf[d_got + k, 128:NB, 128:NB] = corner
    side_weights(ICI)
    vectors.wait_recv()
    for j in range(-1, -DEEP - 1, -1):
        column = jnp.where(first, EDGE + NB * j, NB * (-1 - j))
        expand(on_side(ICI, j), number(sizes, sizes_out, ICI, j), edges, column)
    first_steps(ICI)
    inside(DEEP)
    second.wait_recv()
    third.wait_recv()
    for k in range(DEEP):
        side_steps(DEEP, CHIP, k)
    packed_copy.wait_recv()
    unpack()
    for k in range(DEEP):
        side_steps(DEEP, ICI, k)

    pl.semaphore_wait(round3, len(links))

    final = 2
    chunks = {}
    for i in range(NE):
        start = (NB * i) // 128
        off = NB * i - 128 * start
        x = buf[final, :, slot(i)].astype(F32)
        if off:
            x = pltpu.roll(x, off, 1)
        for k in range(2):
            part = x[:, 128 * k : 128 * (k + 1)]
            at_chunk = start + k
            chunks[at_chunk] = chunks[at_chunk] + part if at_chunk in chunks else part
        done_to = COLS // 128 if i == NE - 1 else (NB * (i + 1)) // 128
        for c in sorted(chunks):
            if c < done_to:
                fall[core, chip, :, 128 * c : 128 * (c + 1)] = chunks.pop(c).astype(BF16)

    y_up, y_dn, y_far = (y + 1) % NY, (y + NY - 1) % NY, (y + 2) % NY
    peer_chip = (1 - xh) * NY + y
    side, far_side = xh * NY, (1 - xh) * NY
    low, high = slice(0, HALFROWS), slice(HALFROWS, ROWS)

    held = fall.at[core]

    def gather(k, g, rows, who):
        part = held.at[g] if rows is None else held.at[g, rows]
        copy = remote(part, part, gat_send.at[k], gat_recv.at[k], who)
        copy.start()
        sends.append(copy)
        return copy

    def share(k, g):
        copy = gather(14 + k, g, None, partner)
        shared.append(copy)

    sends, shared = [], []
    from_dn = [gather(1, chip, low, yup)]
    from_up = [gather(3, chip, high, ydn)]
    from_x = gather(0, chip, None, xpeer)
    from_dn.append(gather(2, chip, high, yup))
    from_up.append(gather(4, chip, low, ydn))

    r128 = lax.broadcasted_iota(jnp.int32, (ROWS, ROWS), 0)
    c128 = lax.broadcasted_iota(jnp.int32, (ROWS, ROWS), 1)

    def gram(which, g, o):
        strip[o, which] = nt_dot(held[g], held[side + (y + o) % NY])

    def squares(k, s, who):
        copy = remote(sqs.at[s], sqr.at[k], sq_send.at[k], sq_recv.at[k], who)
        copy.start()
        sends.append(copy)
        return copy

    def stage(k, src, dst, who):
        return remote(src, dst, red_send.at[k], red_recv.at[k], who)

    quarter = HALFROWS // XL
    row0 = pl.multiple_of(core * HALFROWS + xl * quarter, quarter)
    piece_rows = pl.ds(row0, quarter)

    def over_cores(offsets):
        copies = []
        for o in offsets:
            s1[o] = strip[o, :, other_rows, :].astype(BF16)
            copies.append(stage(o, s1.at[o], r1.at[o], partner))
            copies[-1].start()
        sends.extend(copies)
        return copies

    def to_owner(o, dx):
        col = (y + o) % NY
        j = dx * ZL + (col + ZL - zl) % ZL
        xl_ = (xl + dx) % XL
        rows = pl.ds(pl.multiple_of(xl_ * quarter, quarter), quarter)
        who = at(xl_ * ZN + zh * ZL + col, b)
        copy = remote(
            s2.at[o, :, rows], r2.at[j - 1], red_send.at[j + 4], red_recv.at[j + 4], who
        )
        return copy, col != zl

    def to_owners(offsets, copies):
        for o, copy in zip(offsets, copies):
            copy.wait_recv()
            half = strip[o, :, my_rows, :] + r1[o].astype(F32)
            strip[o, :, my_rows, :] = half
            s2[o] = half.astype(BF16)
            crossing, _ = to_owner(o, 1)
            crossing.start()
            along, away = to_owner(o, 0)

            @pl.when(away)
            def _():
                along.start()

    gram(0, chip, 0)
    norm = jnp.sum(jnp.where(r128 == c128, strip[0, 0], 0.0), axis=0, keepdims=True)
    sqs[0] = jnp.broadcast_to(norm, (CHIPS, ROWS))
    of_core = squares(0, 0, partner)
    from_dn[0].wait_recv()
    on_up = gather(5, side + y_dn, low, yup)
    from_up[0].wait_recv()
    on_dn = gather(6, side + y_up, high, ydn)
    of_core.wait_recv()
    sqs[1] = sqs[0] + sqr[0]
    of_near = [squares(j, 1, near[j - 1]) for j in range(1, XL * ZL)]
    from_dn[1].wait_recv()
    gram(0, chip, 3)
    from_up[1].wait_recv()
    gram(0, chip, 1)
    from_x.wait_recv()
    late_dn = [gather(7, peer_chip, low, yup)]
    late_up = [gather(9, peer_chip, high, ydn)]
    late_dn.append(gather(8, peer_chip, high, yup))
    late_up.append(gather(10, peer_chip, low, ydn))
    early, last = (0, 3, 1), (2,)
    for o in early:
        gram(1, peer_chip, o)
    first_sums = over_cores(early)
    to_owners(early, first_sums)
    for copy in of_near:
        copy.wait_recv()
    norm = sqs[1]
    for j in range(1, XL * ZL):
        norm = norm + sqr[j]
    sqs[2] = norm
    of_far = [squares(7 + j, 2, far[j - 1]) for j in range(1, ZL)]
    on_up.wait_recv()
    on_dn.wait_recv()
    gram(0, chip, 2)
    gram(1, peer_chip, 2)
    last_sums = over_cores(last)
    to_owners(last, last_sums)
    share(0, chip)
    share(1, side + y_dn)
    share(2, side + y_up)
    share(3, side + y_far)
    share(4, peer_chip)

    copies = [stage(4 + j, r2.at[j - 1], r2.at[j - 1], near[j - 1]) for j in range(1, XL * ZL)]
    for copy in copies:
        copy.wait_recv()
    total = strip[(zl + NY - y) % NY, :, piece_rows, :]
    for j in range(1, XL * ZL):
        total = total + r2[j - 1].astype(F32)
    s3[...] = total.astype(BF16)
    copies = [stage(11 + j, s3, r3.at[j - 1], far[j - 1]) for j in range(1, ZL)]
    for copy in copies:
        copy.start()
    sends.extend(copies)

    for copy in of_far:
        copy.wait_recv()
    norm = sqs[2]
    for j in range(1, ZL):
        norm = norm + sqr[7 + j]
    sqs[3] = norm
    norms = [squares(11 + k, 3, who) for k, who in enumerate((yup, ydn, yfar, xpeer))]
    late_dn[0].wait_recv()
    late_on_up = gather(11, far_side + y_dn, low, yup)
    late_up[0].wait_recv()
    late_on_dn = gather(12, far_side + y_up, high, ydn)
    late_dn[1].wait_recv()
    share(5, far_side + y_dn)
    late_up[1].wait_recv()
    share(6, far_side + y_up)
    for copy in norms:
        copy.wait_recv()
    for copy in copies:
        copy.wait_recv()
    for j in range(1, ZL):
        total = total + r3[j - 1].astype(F32)

    ri = lax.broadcasted_iota(jnp.int32, (quarter, ROWS), 0) + row0
    ci = lax.broadcasted_iota(jnp.int32, (quarter, ROWS), 1)
    same = ri == ci
    g = side + zl
    by_offset = [sqs[3, 0:1], sqr[12, 0:1], sqr[13, 0:1], sqr[11, 0:1]]
    sq_row = by_offset[0]
    for o in range(1, NY):
        here = jnp.full((1, ROWS), (zl + NY - y) % NY, jnp.int32) == o
        sq_row = jnp.where(here, by_offset[o], sq_row)
    scale_row = lax.rsqrt(sq_row + EPS)
    for rows_of in range(2):
        lanes = lax.rsqrt((sqs[3, 0:1] if rows_of == 0 else sqr[14, 0:1]) + EPS)
        row_scale = jnp.sum(jnp.where(same, lanes, 0.0), axis=1, keepdims=True)
        value = total[rows_of]
        ident = jnp.zeros_like(value)
        if rows_of == 0:
            unit = jnp.logical_and(same, jnp.full(same.shape, zl - y, jnp.int32) == 0)
            value = jnp.where(unit, sq_row, value)
            ident = jnp.where(unit, 1.5, 0.0)
        normed = row_scale * value * scale_row
        w = math.sqrt(total_rows) * scale_row * (ident - 0.5 * normed)
        s4[rows_of] = w.astype(BF16)

    g_cols = pl.ds(pl.multiple_of(g * ROWS, ROWS), ROWS)
    place = wfull.at[pl.ds(pl.multiple_of(xl * quarter, quarter), quarter), g_cols]
    put = pltpu.make_async_copy(s4.at[0], place, local_sem.at[4])
    put.start()
    copies = [stage(14 + j, s4.at[0], place, near[j - 1]) for j in range(1, XL * ZL)]
    copies += [stage(22 + j, s4.at[1], place, across[j]) for j in range(XL * ZL)]
    for copy in copies:
        copy.start()
    late_on_up.wait_recv()
    late_on_dn.wait_recv()
    share(7, far_side + y_far)
    for copy in shared:
        copy.wait_recv()
    near_cols = pl.ds(pl.multiple_of(side * ROWS, 128), NY * ROWS)
    far_cols = pl.ds(pl.multiple_of(far_side * ROWS, 128), NY * ROWS)
    for copy in copies[: XL * ZL - 1]:
        copy.wait_recv()
    put.wait()
    for h in range(2):
        whole = fall.at[h].reshape(BANDS, COLS)
        for k in range(COLS // PAD):
            halfsum[h, :, PAD * k : PAD * (k + 1)] = jnp.dot(
                wfull[:, near_cols],
                whole[near_cols, PAD * k : PAD * (k + 1)],
                preferred_element_type=F32,
            )
    for copy in copies[XL * ZL - 1 :]:
        copy.wait_recv()
    sends += copies

    for h in range(2):
        whole = fall.at[h].reshape(BANDS, COLS)
        for k in range(COLS // PAD):
            more = jnp.dot(
                wfull[:, far_cols],
                whole[far_cols, PAD * k : PAD * (k + 1)],
                preferred_element_type=F32,
            )
            out[:, COLS * h + PAD * k : COLS * h + PAD * (k + 1)] = (
                halfsum[h, :, PAD * k : PAD * (k + 1)] + more
            ).astype(BF16)
    for o in range(NY):
        crossing, _ = to_owner(o, 1)
        crossing.wait_send()
        along, away = to_owner(o, 0)

        @pl.when(away)
        def _():
            along.wait_send()

    for copy in sends + blocks + [vectors, swap, second, third, packed_copy]:
        copy.wait_send()


def shards(basis_sizes, coupling_pattern, h_diag, h_couple, bands):
    total_rows = h_diag.shape[0] * lax.axis_size("elem") * h_diag.shape[1]
    hbm = pl.BlockSpec(memory_space=pltpu.HBM)
    dma = pltpu.SemaphoreType.DMA
    quarter = HALFROWS // XL
    return pl.pallas_call(
        functools.partial(kernel, total_rows),
        out_shape=pltpu.VMEM(bands.shape, BF16),
        in_specs=[hbm] * 5,
        out_specs=pl.BlockSpec(memory_space=pltpu.VMEM),
        scratch_shapes=[
            pltpu.VMEM((NE + 2 * DEEP - 2, 3 * PAD, PAD), BF16),
            pltpu.VMEM((4, ROWS, PAD * (NE + 2 * DEEP)), BF16),
            pltpu.VMEM((NE + 2 * DEEP - 2, NB, NB), BF16),
            pltpu.VMEM((NE + 2 * DEEP, NB, NB), BF16),
            pltpu.VMEM((ROWS, COLS + EDGE), BF16),
            pltpu.VMEM((ROWS, EDGE), BF16),
            pltpu.VMEM((2, NB, 128), BF16),
            pltpu.VMEM((2, ROWS, 640), BF16),
            pltpu.VMEM((2, CHIPS, ROWS, COLS), BF16),
            pltpu.VMEM((NY, 2, ROWS, ROWS), F32),
            pltpu.VMEM((NY, 2, HALFROWS, ROWS), BF16),
            pltpu.VMEM((NY, 2, HALFROWS, ROWS), BF16),
            pltpu.VMEM((NY, 2, HALFROWS, ROWS), BF16),
            pltpu.VMEM((XL * ZL - 1, 2, quarter, ROWS), BF16),
            pltpu.VMEM((2, quarter, ROWS), BF16),
            pltpu.VMEM((ZL - 1, 2, quarter, ROWS), BF16),
            pltpu.VMEM((2, quarter, ROWS), BF16),
            pltpu.VMEM((4, CHIPS, ROWS), F32),
            pltpu.VMEM((15, CHIPS, ROWS), F32),
            pltpu.VMEM((HALFROWS, BANDS), BF16),
            pltpu.VMEM((2, HALFROWS, COLS), F32),
            *[pltpu.SMEM((2 * NE,), jnp.int32)] * 4,
            *[pltpu.SemaphoreType.REGULAR] * 3,
            dma((8,)),
            dma((9,)),
            dma((9,)),
            dma((22,)),
            dma((22,)),
            dma((30,)),
            dma((30,)),
            dma((15,)),
            dma((15,)),
        ],
        compiler_params=pltpu.CompilerParams(
            collective_id=0, has_side_effects=True, vmem_limit_bytes=62000000
        ),
        name="filter_step",
    )(basis_sizes, coupling_pattern, h_diag, h_couple, bands)


def solution(mesh):
    in_specs = (
        P("elem"),
        P("elem"),
        P("elem", None, None),
        P("elem", None, None),
        P("band", "elem"),
    )
    out_specs = P("band", "elem")
    return jax.shard_map(shards, mesh=mesh, in_specs=in_specs, out_specs=out_specs, check_vma=False)
```

```python
import functools
import math

import jax
import jax.numpy as jnp
from jax import lax
from jax.experimental import pallas as pl
from jax.experimental.pallas import tpu as pltpu
from jax.sharding import PartitionSpec as P

MESH = pl.DeviceIdType.MESH
DEGREE = 6
CENTER = 0.4
HALF = 2.8
EPS = 1e-06
F32 = jnp.float32
BF16 = jnp.bfloat16

NB = 160
PAD = 256
NE = 8
ROWS = 128
HALFROWS = 64
COLS = NE * NB
DEEP = 3
EDGE = 512
REST = NB - 128
ZL = 4
ZN = 16
XL = 2
NY = 4
CHIPS = 8
BANDS = ROWS * CHIPS


def nt_dot(a, b):
    return lax.dot_general(a, b, (((1,), (1,)), ((), ())), preferred_element_type=F32)


def kernel(
    total_rows,
    sizes_hbm,
    pattern_hbm,
    hd,
    hc,
    bands,
    out,
    wts,
    buf,
    dbuf,
    cbuf,
    raw,
    edges,
    tails,
    packed,
    fall,
    strip,
    s1,
    r1,
    s2,
    r2,
    s3,
    r3,
    s4,
    sqs,
    sqr,
    wfull,
    halfsum,
    sizes,
    pattern,
    sizes_out,
    pattern_out,
    round1,
    round2,
    round3,
    local_sem,
    ext_send,
    ext_recv,
    gat_send,
    gat_recv,
    red_send,
    red_recv,
    sq_send,
    sq_recv,
):
    e = lax.axis_index("elem")
    b = lax.axis_index("band")
    ne = lax.axis_size("elem")
    core = b % 2
    other = 1 - core
    chip = b // 2
    xh = chip // NY
    y = chip % NY
    xl = e // ZN
    z = e % ZN
    zh = z // ZL
    zl = z % ZL

    def at(e_, b_):
        return (e_, b_)

    partner = at(e, chip * 2 + other)
    first = core == 0
    across_chip = at((e + jnp.where(first, ne - 1, 1)) % ne, chip * 2 + other)
    xpeer = at(e, ((1 - xh) * NY + y) * 2 + core)
    yup = at(e, (xh * NY + (y + 1) % NY) * 2 + core)
    ydn = at(e, (xh * NY + (y + NY - 1) % NY) * 2 + core)
    places = [((xl + j // ZL) % XL) * ZN + zh * ZL + (zl + j) % ZL for j in range(XL * ZL)]
    near = [at(p, b) for p in places[1:]]
    across = [at(p, xpeer[1]) for p in places]
    far = [at(xl * ZN + ((zh + j) % ZL) * ZL + zl, b) for j in range(1, ZL)]

    barrier = pltpu.get_barrier_semaphore()
    zs = [at(xl * ZN + (z + d) % ZN, b) for d in (1, ZN - 1, 2, ZN - 2)]
    links = zs + [xpeer, at((1 - xl) * ZN + z, b), yup, ydn]
    friends = [partner, across_chip] + links
    yfar = at(e, (xh * NY + (y + 2) % NY) * 2 + core)

    def tell(sem, whom):
        for who in whom:
            pl.semaphore_signal(sem, inc=1, device_id=who, device_id_type=MESH)

    tell(barrier, friends)

    def remote(src, dst, ss, rs, who):
        return pltpu.make_async_remote_copy(
            src_ref=src, dst_ref=dst, send_sem=ss, recv_sem=rs, device_id=who, device_id_type=MESH
        )

    def aligned(x, n):
        return pl.multiple_of(x, n)

    my_rows = pl.ds(aligned(core * HALFROWS, HALFROWS), HALFROWS)
    other_rows = pl.ds(aligned(other * HALFROWS, HALFROWS), HALFROWS)

    n_c, n_d = NE + DEEP, NE + DEEP - 1
    c_at, d_at = jnp.where(first, DEEP, 0), jnp.where(first, DEEP - 1, 0)
    load_c = pltpu.make_async_copy(
        hc.at[pl.ds(core * (NE - DEEP), n_c)], cbuf.at[pl.ds(c_at, n_c)], local_sem.at[0]
    )
    load_d = pltpu.make_async_copy(
        hd.at[pl.ds(core * (NE - DEEP + 1), n_d)], dbuf.at[pl.ds(d_at, n_d)], local_sem.at[1]
    )
    wide = COLS + EDGE
    base = aligned(core * EDGE, 128)
    mine = pl.ds(aligned(core * (COLS - EDGE), 128), wide)
    theirs = pl.ds(aligned(other * (COLS - EDGE), 128), wide)
    load_v = pltpu.make_async_copy(bands.at[:, mine], raw.at[my_rows], local_sem.at[2])
    load_s = pltpu.make_async_copy(sizes_hbm, sizes, local_sem.at[5])
    load_p = pltpu.make_async_copy(pattern_hbm, pattern, local_sem.at[6])
    for load in (load_s, load_p, load_c, load_d, load_v):
        load.start()

    pl.semaphore_wait(barrier, len(friends))

    tell(round1, links)

    def outer(k, src, dst, who):
        return remote(src, dst, ext_send.at[k], ext_recv.at[k], who)

    swap = remote(bands.at[:, theirs], raw.at[my_rows], gat_send.at[13], gat_recv.at[13], partner)
    swap.start()
    head, n_e = slice(0, 128), DEEP - 1
    c_out = jnp.where(first, 0, 2 * NE - DEEP)
    d_out = jnp.where(first, 0, 2 * NE - DEEP + 1)
    c_in, d_in = jnp.where(first, DEEP + NE, 0), jnp.where(first, DEEP - 1 + NE, 0)
    blocks = [
        outer(0, sizes_hbm, sizes_out, across_chip),
        outer(1, pattern_hbm, pattern_out, across_chip),
        outer(2, hc.at[pl.ds(c_out, DEEP), :, head], cbuf.at[pl.ds(c_in, DEEP), :, head], across_chip),
        outer(3, hd.at[pl.ds(d_out, n_e), :, head], dbuf.at[pl.ds(d_in, n_e), :, head], across_chip),
    ]
    for copy in blocks:
        copy.start()
    for load in (load_s, load_p, load_c, load_d):
        load.wait()
    c_from = jnp.where(first, DEEP, NE)
    d_from = jnp.where(first, DEEP - 1, NE)
    for k in range(DEEP):
        tails[0, :, REST * k : REST * (k + 1)] = cbuf[c_from + k, :, 128:NB]
    for k in range(n_e):
        tails[0, REST * k : REST * (k + 1), REST * DEEP : 128] = dbuf[d_from + k, 128:NB, 128:NB]
    blocks.append(outer(5, tails.at[0], tails.at[1], across_chip))
    blocks[-1].start()

    wts[...] = jnp.zeros_like(wts)
    load_v.wait()
    swap.wait_recv()
    edge_out = pl.ds(aligned(core * COLS, 128), EDGE)
    vectors = outer(4, raw.at[:, edge_out], edges, across_chip)
    vectors.start()

    ICI, CHIP = 0, 1

    def on_side(side, j):
        return jnp.where(first, j, NE - 1 - j) if side == ICI else jnp.where(first, NE - 1 - j, j)

    def number(table, table_out, side, j):
        if side == ICI and j < 0:
            return table_out[jnp.where(first, 2 * NE + j, -1 - j)]
        if side == ICI:
            return table[jnp.where(first, j, 2 * NE - 1 - j)]
        return table[jnp.where(first, NE - 1 - j, NE + j)]

    lanes_nb = lax.broadcasted_iota(jnp.int32, (NB, NB), 1)
    eye = (lax.broadcasted_iota(jnp.int32, (NB, NB), 0) == lanes_nb).astype(BF16)

    def coupled(i, on):
        gate = jnp.full((NB, NB), on, jnp.int32) != 0
        return jnp.where(gate, cbuf[i + DEEP].astype(F32), 0.0)

    def put_weights(i, row, value, size):
        at_row = slice(row * PAD, row * PAD + NB)
        keep = lanes_nb < size
        wts[i + DEEP - 1, at_row, 0:NB] = jnp.where(keep, value, 0.0).astype(BF16)

    own_size = [sizes[core * NE + i] for i in range(NE)]
    for i in range(NE):
        put_weights(i, 1, dbuf[i + DEEP - 1].astype(F32), own_size[i])
        if i + 1 < NE:
            pc = coupled(i, pattern[core * NE + i])
            put_weights(i, 2, nt_dot(eye, pc.astype(BF16)), own_size[i])
            put_weights(i + 1, 0, pc, own_size[i + 1])

    def side_weights(side):
        left_side = first if side == ICI else jnp.logical_not(first)
        count = number

        for j in range(-1, -DEEP, -1):
            i = on_side(side, j)
            size = count(sizes, sizes_out, side, j)
            put_weights(i, 1, dbuf[i + DEEP - 1].astype(F32), size)
        for j in range(0, -DEEP, -1):
            low = jnp.where(left_side, on_side(side, j - 1), on_side(side, j))
            on = jnp.where(
                left_side,
                count(pattern, pattern_out, side, j - 1),
                count(pattern, pattern_out, side, j),
            )
            pc = coupled(low, on)
            turned = nt_dot(eye, pc.astype(BF16))
            inner, outer_ = on_side(side, j), on_side(side, j - 1)
            size = count(sizes, sizes_out, side, j)
            value = jnp.where(left_side, pc, turned)
            put_weights_at(inner, jnp.where(left_side, 0, 2), value, size)
            if j > 1 - DEEP:
                size = count(sizes, sizes_out, side, j - 1)
                value = jnp.where(left_side, turned, pc)
                put_weights_at(outer_, jnp.where(left_side, 2, 0), value, size)

    def put_weights_at(i, row, value, size):
        keep = lanes_nb < size
        rows = pl.ds(aligned(row * PAD, PAD), NB)
        wts[i + DEEP - 1, rows, 0:NB] = jnp.where(keep, value, 0.0).astype(BF16)

    def slot(i, n=1):
        if isinstance(i, int):
            return slice(PAD * (i + DEEP), PAD * (i + DEEP + n))
        return pl.ds(aligned(PAD * (i + DEEP), PAD), PAD * n)

    lanes_pad = lax.broadcasted_iota(jnp.int32, (ROWS, PAD), 1)

    def expand(i, size, ref, column):
        off = column % 128
        x = ref[:, pl.ds(aligned(column - off, 128), PAD)].astype(F32)
        x = pltpu.roll(x, (PAD - off) % PAD, 1)
        buf[0, :, slot(i)] = jnp.where(lanes_pad < size, x, 0.0).astype(BF16)

    for i in range(NE):
        start = NB * i // 128 * 128
        x = raw[:, pl.ds(aligned(base + start, 128), PAD)].astype(F32)
        if NB * i > start:
            x = pltpu.roll(x, PAD - (NB * i - start), 1)
        buf[0, :, slot(i)] = jnp.where(lanes_pad < own_size[i], x, 0.0).astype(BF16)
    for j in range(-1, -DEEP - 1, -1):
        column = jnp.where(first, COLS + NB * (-1 - j), EDGE + NB * j)
        expand(on_side(CHIP, j), number(sizes, sizes_out, CHIP, j), raw, column)

    plan = [
        (0, None, [1]),
        (1, 0, [0, 2]),
        (0, 1, [1, 3]),
        (3, 2, [2]),
        (2, 3, [3]),
        (3, 2, [2]),
    ]

    def element(t, i, own):
        store(t, i, own, stepped(t, i))

    def stepped(t, i):
        now, prior, _ = plan[t]
        acc = jnp.dot(
            buf[now, :, slot(i - 1, 3)], wts[i + DEEP - 1], preferred_element_type=F32
        )
        shifted = acc - CENTER * buf[now, :, slot(i)].astype(F32)
        if t == 0:
            nxt = shifted * (1.0 / HALF)
        else:
            nxt = shifted * (2.0 / HALF) - buf[prior, :, slot(i)].astype(F32)
        return nxt.astype(BF16)

    def store(t, i, own, nxt):
        for target in plan[t][2]:
            if own or target < 2 or t >= DEEP:
                buf[target, :, slot(i)] = nxt

    def inside(t0):
        for k in range(DEEP):
            for i in range(k + 1, NE - k - 1):
                element(t0 + k, i, True)

    def side_steps(t0, side, k):
        level = range(k + 1 - DEEP, k + 1)
        made = [stepped(t0 + k, on_side(side, j)) for j in level]
        for j, nxt in zip(level, made):
            store(t0 + k, on_side(side, j), j >= 0 or k == DEEP - 2, nxt)

    def pass_on(k, source, target, skip, n):
        v, w = buf.at[source], buf.at[target]
        src = slot(jnp.where(first, NE - n - skip, skip), n)
        dst = slot(jnp.where(first, -n - skip, NE + skip), n)
        return outer(k, v.at[:, src], w.at[:, dst], partner)

    second = pass_on(6, 0, 2, DEEP - 2, 1)
    third = pass_on(7, 1, 3, 0, DEEP)
    packed_copy = outer(8, packed.at[0], packed.at[1], across_chip)
    sent = [(1, j) for j in range(DEEP)] + [(0, DEEP - 2)]

    def pack():
        for k, (source, j) in enumerate(sent):
            at_slot = on_side(ICI, j)
            start = aligned(PAD * (at_slot + DEEP), PAD)
            packed[0, :, 128 * k : 128 * (k + 1)] = buf[source, :, pl.ds(start, 128)]
            x = buf[source, :, pl.ds(aligned(start + 128, 128), 128)].astype(F32)
            if k:
                x = pltpu.roll(x, REST * k, 1)
            rest = x if k == 0 else rest + x
        packed[0, :, 512:640] = rest.astype(BF16)

    def unpack():
        rest = packed[1, :, 512:640].astype(F32)
        for k, (source, j) in enumerate(sent):
            start = aligned(PAD * (on_side(ICI, -1 - j) + DEEP), PAD)
            buf[source + 2, :, pl.ds(start, 128)] = packed[1, :, 128 * k : 128 * (k + 1)]
            x = pltpu.roll(rest, 128 - REST * k, 1) if k else rest
            x = jnp.where(lanes_pad[:, 0:128] < REST, x, 0.0).astype(BF16)
            buf[source + 2, :, pl.ds(aligned(start + 128, 128), 128)] = x

    def first_steps(side):
        for k in range(DEEP):
            side_steps(0, side, k)
        if side == CHIP:
            second.start()
            third.start()
        else:
            pack()
            packed_copy.start()

    pl.semaphore_wait(round1, len(links))
    tell(round2, links + [far[0], far[ZL - 2]])
    side_weights(CHIP)
    inside(0)
    first_steps(CHIP)
    pl.semaphore_wait(round2, len(links) + 2)
    tell(round3, links)
    for copy in blocks:
        copy.wait_recv()
    c_got, d_got = jnp.where(first, 0, DEEP + NE), jnp.where(first, 0, DEEP - 1 + NE)
    for k in range(DEEP):
        cbuf[c_got + k, :, 128:NB] = tails[1, :, REST * k : REST * (k + 1)]
    for k in range(n_e):
        turned = nt_dot(eye[0:128, 0:128], dbuf[d_got + k, 128:NB, 0:128])
        dbuf[d_got + k, 0:128, 128:NB] = turned.astype(BF16)
        corner = tails[1, REST * k : REST * (k + 1), REST * DEEP : 128]
        dbuf[d_got + k, 128:NB, 128:NB] = corner
    side_weights(ICI)
    vectors.wait_recv()
    for j in range(-1, -DEEP - 1, -1):
        column = jnp.where(first, EDGE + NB * j, NB * (-1 - j))
        expand(on_side(ICI, j), number(sizes, sizes_out, ICI, j), edges, column)
    first_steps(ICI)
    inside(DEEP)
    second.wait_recv()
    third.wait_recv()
    for k in range(DEEP):
        side_steps(DEEP, CHIP, k)
    packed_copy.wait_recv()
    unpack()
    for k in range(DEEP):
        side_steps(DEEP, ICI, k)

    pl.semaphore_wait(round3, len(links))

    final = 2
    chunks = {}
    for i in range(NE):
        start = (NB * i) // 128
        off = NB * i - 128 * start
        x = buf[final, :, slot(i)].astype(F32)
        if off:
            x = pltpu.roll(x, off, 1)
        for k in range(2):
            part = x[:, 128 * k : 128 * (k + 1)]
            at_chunk = start + k
            chunks[at_chunk] = chunks[at_chunk] + part if at_chunk in chunks else part
        done_to = COLS // 128 if i == NE - 1 else (NB * (i + 1)) // 128
        for c in sorted(chunks):
            if c < done_to:
                fall[core, chip, :, 128 * c : 128 * (c + 1)] = chunks.pop(c).astype(BF16)

    y_up, y_dn, y_far = (y + 1) % NY, (y + NY - 1) % NY, (y + 2) % NY
    peer_chip = (1 - xh) * NY + y
    side, far_side = xh * NY, (1 - xh) * NY
    low, high = slice(0, HALFROWS), slice(HALFROWS, ROWS)

    held = fall.at[core]

    def gather(k, g, rows, who):
        part = held.at[g] if rows is None else held.at[g, rows]
        copy = remote(part, part, gat_send.at[k], gat_recv.at[k], who)
        copy.start()
        sends.append(copy)
        return copy

    def share(k, g):
        copy = gather(14 + k, g, None, partner)
        shared.append(copy)

    sends, shared = [], []
    from_dn = [gather(1, chip, low, yup)]
    from_up = [gather(3, chip, high, ydn)]
    from_x = gather(0, chip, None, xpeer)
    from_dn.append(gather(2, chip, high, yup))
    from_up.append(gather(4, chip, low, ydn))

    r128 = lax.broadcasted_iota(jnp.int32, (ROWS, ROWS), 0)
    c128 = lax.broadcasted_iota(jnp.int32, (ROWS, ROWS), 1)

    def gram(which, g, o):
        strip[o, which] = nt_dot(held[g], held[side + (y + o) % NY])

    def squares(k, s, who):
        copy = remote(sqs.at[s], sqr.at[k], sq_send.at[k], sq_recv.at[k], who)
        copy.start()
        sends.append(copy)
        return copy

    def stage(k, src, dst, who):
        return remote(src, dst, red_send.at[k], red_recv.at[k], who)

    quarter = HALFROWS // XL
    row0 = pl.multiple_of(core * HALFROWS + xl * quarter, quarter)
    piece_rows = pl.ds(row0, quarter)

    def over_cores(offsets):
        copies = []
        for o in offsets:
            s1[o] = strip[o, :, other_rows, :].astype(BF16)
            copies.append(stage(o, s1.at[o], r1.at[o], partner))
            copies[-1].start()
        sends.extend(copies)
        return copies

    def to_owner(o, dx):
        col = (y + o) % NY
        j = dx * ZL + (col + ZL - zl) % ZL
        xl_ = (xl + dx) % XL
        rows = pl.ds(pl.multiple_of(xl_ * quarter, quarter), quarter)
        who = at(xl_ * ZN + zh * ZL + col, b)
        copy = remote(
            s2.at[o, :, rows], r2.at[j], red_send.at[j + 4], red_recv.at[j + 4], who
        )
        return copy, col != zl

    def to_owners(offsets, copies):
        for o, copy in zip(offsets, copies):
            copy.wait_recv()
            half = strip[o, :, my_rows, :] + r1[o].astype(F32)
            strip[o, :, my_rows, :] = half
            s2[o] = half.astype(BF16)
            crossing, _ = to_owner(o, 1)
            crossing.start()
            along, away = to_owner(o, 0)

            @pl.when(away)
            def _():
                along.start()

    gram(0, chip, 0)
    norm = jnp.sum(jnp.where(r128 == c128, strip[0, 0], 0.0), axis=0, keepdims=True)
    sqs[0] = jnp.broadcast_to(norm, (CHIPS, ROWS))
    of_core = squares(0, 0, partner)
    from_dn[0].wait_recv()
    on_up = gather(5, side + y_dn, low, yup)
    from_up[0].wait_recv()
    on_dn = gather(6, side + y_up, high, ydn)
    of_core.wait_recv()
    sqs[1] = sqs[0] + sqr[0]
    of_near = [squares(j, 1, near[j - 1]) for j in range(1, XL * ZL)]
    from_dn[1].wait_recv()
    gram(0, chip, 3)
    from_up[1].wait_recv()
    gram(0, chip, 1)
    from_x.wait_recv()
    late_dn = [gather(7, peer_chip, low, yup)]
    late_up = [gather(9, peer_chip, high, ydn)]
    late_dn.append(gather(8, peer_chip, high, yup))
    late_up.append(gather(10, peer_chip, low, ydn))
    early, last = (0, 3, 1), (2,)
    for o in early:
        gram(1, peer_chip, o)
    first_sums = over_cores(early)
    to_owners(early, first_sums)
    for copy in of_near:
        copy.wait_recv()
    norm = sqs[1]
    for j in range(1, XL * ZL):
        norm = norm + sqr[j]
    sqs[2] = norm
    of_far = [squares(7 + j, 2, far[j - 1]) for j in range(1, ZL)]
    on_up.wait_recv()
    on_dn.wait_recv()
    gram(0, chip, 2)
    gram(1, peer_chip, 2)
    last_sums = over_cores(last)
    to_owners(last, last_sums)
    share(0, chip)
    share(1, side + y_dn)
    share(2, side + y_up)
    share(3, side + y_far)
    share(4, peer_chip)

    copies = [stage(4 + j, r2.at[j], r2.at[j], near[j - 1]) for j in range(1, XL * ZL)]
    for copy in copies:
        copy.wait_recv()
    total = strip[(zl + NY - y) % NY, :, piece_rows, :]
    for j in range(1, XL * ZL):
        total = total + r2[j].astype(F32)
    s3[...] = total.astype(BF16)
    copies = [stage(11 + j, s3, r3.at[j - 1], far[j - 1]) for j in range(1, ZL)]
    for copy in copies:
        copy.start()
    sends.extend(copies)

    for copy in of_far:
        copy.wait_recv()
    norm = sqs[2]
    for j in range(1, ZL):
        norm = norm + sqr[7 + j]
    sqs[3] = norm
    norms = [squares(11 + k, 3, who) for k, who in enumerate((yup, ydn, yfar, xpeer))]
    late_dn[0].wait_recv()
    late_on_up = gather(11, far_side + y_dn, low, yup)
    late_up[0].wait_recv()
    late_on_dn = gather(12, far_side + y_up, high, ydn)
    late_dn[1].wait_recv()
    share(5, far_side + y_dn)
    late_up[1].wait_recv()
    share(6, far_side + y_up)
    for copy in norms:
        copy.wait_recv()
    for copy in copies:
        copy.wait_recv()
    for j in range(1, ZL):
        total = total + r3[j - 1].astype(F32)

    ri = lax.broadcasted_iota(jnp.int32, (quarter, ROWS), 0) + row0
    ci = lax.broadcasted_iota(jnp.int32, (quarter, ROWS), 1)
    same = ri == ci
    g = side + zl
    by_offset = [sqs[3, 0:1], sqr[12, 0:1], sqr[13, 0:1], sqr[11, 0:1]]
    sq_row = by_offset[0]
    for o in range(1, NY):
        here = jnp.full((1, ROWS), (zl + NY - y) % NY, jnp.int32) == o
        sq_row = jnp.where(here, by_offset[o], sq_row)
    scale_row = lax.rsqrt(sq_row + EPS)
    for rows_of in range(2):
        lanes = lax.rsqrt((sqs[3, 0:1] if rows_of == 0 else sqr[14, 0:1]) + EPS)
        row_scale = jnp.sum(jnp.where(same, lanes, 0.0), axis=1, keepdims=True)
        value = total[rows_of]
        ident = jnp.zeros_like(value)
        if rows_of == 0:
            unit = jnp.logical_and(same, jnp.full(same.shape, zl - y, jnp.int32) == 0)
            value = jnp.where(unit, sq_row, value)
            ident = jnp.where(unit, 1.5, 0.0)
        normed = row_scale * value * scale_row
        w = math.sqrt(total_rows) * scale_row * (ident - 0.5 * normed)
        s4[rows_of] = w.astype(BF16)

    g_cols = pl.ds(pl.multiple_of(g * ROWS, ROWS), ROWS)
    place = wfull.at[pl.ds(pl.multiple_of(xl * quarter, quarter), quarter), g_cols]
    put = pltpu.make_async_copy(s4.at[0], place, local_sem.at[4])
    put.start()
    copies = [stage(14 + j, s4.at[0], place, near[j - 1]) for j in range(1, XL * ZL)]
    copies += [stage(22 + j, s4.at[1], place, across[j]) for j in range(XL * ZL)]
    for copy in copies:
        copy.start()
    late_on_up.wait_recv()
    late_on_dn.wait_recv()
    share(7, far_side + y_far)
    for copy in shared:
        copy.wait_recv()
    near_cols = pl.ds(pl.multiple_of(side * ROWS, 128), NY * ROWS)
    far_cols = pl.ds(pl.multiple_of(far_side * ROWS, 128), NY * ROWS)
    for copy in copies[: XL * ZL - 1]:
        copy.wait_recv()
    put.wait()
    for h in range(2):
        whole = fall.at[h].reshape(BANDS, COLS)
        for k in range(COLS // PAD):
            halfsum[h, :, PAD * k : PAD * (k + 1)] = jnp.dot(
                wfull[:, near_cols],
                whole[near_cols, PAD * k : PAD * (k + 1)],
                preferred_element_type=F32,
            )
    for copy in copies[XL * ZL - 1 :]:
        copy.wait_recv()
    sends += copies

    for h in range(2):
        whole = fall.at[h].reshape(BANDS, COLS)
        for k in range(COLS // PAD):
            more = jnp.dot(
                wfull[:, far_cols],
                whole[far_cols, PAD * k : PAD * (k + 1)],
                preferred_element_type=F32,
            )
            out[:, COLS * h + PAD * k : COLS * h + PAD * (k + 1)] = (
                halfsum[h, :, PAD * k : PAD * (k + 1)] + more
            ).astype(BF16)
    for o in range(NY):
        crossing, _ = to_owner(o, 1)
        crossing.wait_send()
        along, away = to_owner(o, 0)

        @pl.when(away)
        def _():
            along.wait_send()

    for copy in sends + blocks + [vectors, swap, second, third, packed_copy]:
        copy.wait_send()


def shards(basis_sizes, coupling_pattern, h_diag, h_couple, bands):
    total_rows = h_diag.shape[0] * lax.axis_size("elem") * h_diag.shape[1]
    hbm = pl.BlockSpec(memory_space=pltpu.HBM)
    dma = pltpu.SemaphoreType.DMA
    quarter = HALFROWS // XL
    return pl.pallas_call(
        functools.partial(kernel, total_rows),
        out_shape=pltpu.VMEM(bands.shape, BF16),
        in_specs=[hbm] * 5,
        out_specs=pl.BlockSpec(memory_space=pltpu.VMEM),
        scratch_shapes=[
            pltpu.VMEM((NE + 2 * DEEP - 2, 3 * PAD, PAD), BF16),
            pltpu.VMEM((4, ROWS, PAD * (NE + 2 * DEEP)), BF16),
            pltpu.VMEM((NE + 2 * DEEP - 2, NB, NB), BF16),
            pltpu.VMEM((NE + 2 * DEEP, NB, NB), BF16),
            pltpu.VMEM((ROWS, COLS + EDGE), BF16),
            pltpu.VMEM((ROWS, EDGE), BF16),
            pltpu.VMEM((2, NB, 128), BF16),
            pltpu.VMEM((2, ROWS, 640), BF16),
            pltpu.VMEM((2, CHIPS, ROWS, COLS), BF16),
            pltpu.VMEM((NY, 2, ROWS, ROWS), F32),
            pltpu.VMEM((NY, 2, HALFROWS, ROWS), BF16),
            pltpu.VMEM((NY, 2, HALFROWS, ROWS), BF16),
            pltpu.VMEM((NY, 2, HALFROWS, ROWS), BF16),
            pltpu.VMEM((XL * ZL, 2, quarter, ROWS), BF16),
            pltpu.VMEM((2, quarter, ROWS), BF16),
            pltpu.VMEM((ZL - 1, 2, quarter, ROWS), BF16),
            pltpu.VMEM((2, quarter, ROWS), BF16),
            pltpu.VMEM((4, CHIPS, ROWS), F32),
            pltpu.VMEM((15, CHIPS, ROWS), F32),
            pltpu.VMEM((HALFROWS, BANDS), BF16),
            pltpu.VMEM((2, HALFROWS, COLS), F32),
            *[pltpu.SMEM((2 * NE,), jnp.int32)] * 4,
            *[pltpu.SemaphoreType.REGULAR] * 3,
            dma((8,)),
            dma((9,)),
            dma((9,)),
            dma((22,)),
            dma((22,)),
            dma((30,)),
            dma((30,)),
            dma((15,)),
            dma((15,)),
        ],
        compiler_params=pltpu.CompilerParams(
            collective_id=0, has_side_effects=True, vmem_limit_bytes=62000000
        ),
        name="filter_step",
    )(basis_sizes, coupling_pattern, h_diag, h_couple, bands)


def solution(mesh):
    in_specs = (
        P("elem"),
        P("elem"),
        P("elem", None, None),
        P("elem", None, None),
        P("band", "elem"),
    )
    out_specs = P("band", "elem")
    return jax.shard_map(shards, mesh=mesh, in_specs=in_specs, out_specs=out_specs, check_vma=False)
```

```python
import functools
import math

import jax
import jax.numpy as jnp
from jax import lax
from jax.experimental import pallas as pl
from jax.experimental.pallas import tpu as pltpu
from jax.sharding import PartitionSpec as P

MESH = pl.DeviceIdType.MESH
DEGREE = 6
CENTER = 0.4
HALF = 2.8
EPS = 1e-06
F32 = jnp.float32
BF16 = jnp.bfloat16

NB = 160
PAD = 256
NE = 8
ROWS = 128
HALFROWS = 64
COLS = NE * NB
DEEP = 3
EDGE = 512
REST = NB - 128
ZL = 4
ZN = 16
XL = 2
NY = 4
CHIPS = 8
BANDS = ROWS * CHIPS


def nt_dot(a, b):
    return lax.dot_general(a, b, (((1,), (1,)), ((), ())), preferred_element_type=F32)


def kernel(
    total_rows,
    sizes_hbm,
    pattern_hbm,
    hd,
    hc,
    bands,
    out,
    wts,
    buf,
    dbuf,
    cbuf,
    raw,
    edges,
    tails,
    packed,
    fall,
    strip,
    s1,
    r1,
    s2,
    r2,
    s3,
    r3,
    s4,
    sqs,
    sqr,
    wfull,
    halfsum,
    sizes,
    pattern,
    sizes_out,
    pattern_out,
    round1,
    round2,
    round3,
    local_sem,
    ext_send,
    ext_recv,
    gat_send,
    gat_recv,
    red_send,
    red_recv,
    sq_send,
    sq_recv,
):
    e = lax.axis_index("elem")
    b = lax.axis_index("band")
    ne = lax.axis_size("elem")
    core = b % 2
    other = 1 - core
    chip = b // 2
    xh = chip // NY
    y = chip % NY
    xl = e // ZN
    z = e % ZN
    zh = z // ZL
    zl = z % ZL

    def at(e_, b_):
        return (e_, b_)

    partner = at(e, chip * 2 + other)
    first = core == 0
    across_chip = at((e + jnp.where(first, ne - 1, 1)) % ne, chip * 2 + other)
    xpeer = at(e, ((1 - xh) * NY + y) * 2 + core)
    yup = at(e, (xh * NY + (y + 1) % NY) * 2 + core)
    ydn = at(e, (xh * NY + (y + NY - 1) % NY) * 2 + core)
    places = [((xl + j // ZL) % XL) * ZN + zh * ZL + (zl + j) % ZL for j in range(XL * ZL)]
    near = [at(p, b) for p in places[1:]]
    across = [at(p, xpeer[1]) for p in places]
    far = [at(xl * ZN + ((zh + j) % ZL) * ZL + zl, b) for j in range(1, ZL)]

    barrier = pltpu.get_barrier_semaphore()
    zs = [at(xl * ZN + (z + d) % ZN, b) for d in (1, ZN - 1, 2, ZN - 2)]
    links = zs + [xpeer, at((1 - xl) * ZN + z, b), yup, ydn]
    friends = [partner, across_chip] + links
    yfar = at(e, (xh * NY + (y + 2) % NY) * 2 + core)

    def tell(sem, whom):
        for who in whom:
            pl.semaphore_signal(sem, inc=1, device_id=who, device_id_type=MESH)

    tell(barrier, friends)

    def remote(src, dst, ss, rs, who):
        return pltpu.make_async_remote_copy(
            src_ref=src, dst_ref=dst, send_sem=ss, recv_sem=rs, device_id=who, device_id_type=MESH
        )

    def aligned(x, n):
        return pl.multiple_of(x, n)

    my_rows = pl.ds(aligned(core * HALFROWS, HALFROWS), HALFROWS)
    other_rows = pl.ds(aligned(other * HALFROWS, HALFROWS), HALFROWS)

    n_c, n_d = NE + DEEP, NE + DEEP - 1
    c_at, d_at = jnp.where(first, DEEP, 0), jnp.where(first, DEEP - 1, 0)
    load_c = pltpu.make_async_copy(
        hc.at[pl.ds(core * (NE - DEEP), n_c)], cbuf.at[pl.ds(c_at, n_c)], local_sem.at[0]
    )
    load_d = pltpu.make_async_copy(
        hd.at[pl.ds(core * (NE - DEEP + 1), n_d)], dbuf.at[pl.ds(d_at, n_d)], local_sem.at[1]
    )
    wide = COLS + EDGE
    base = aligned(core * EDGE, 128)
    mine = pl.ds(aligned(core * (COLS - EDGE), 128), wide)
    theirs = pl.ds(aligned(other * (COLS - EDGE), 128), wide)
    load_v = pltpu.make_async_copy(bands.at[:, mine], raw.at[my_rows], local_sem.at[2])
    load_s = pltpu.make_async_copy(sizes_hbm, sizes, local_sem.at[5])
    load_p = pltpu.make_async_copy(pattern_hbm, pattern, local_sem.at[6])
    for load in (load_s, load_p, load_c, load_d, load_v):
        load.start()

    pl.semaphore_wait(barrier, len(friends))

    tell(round1, links)

    def outer(k, src, dst, who):
        return remote(src, dst, ext_send.at[k], ext_recv.at[k], who)

    swap = remote(bands.at[:, theirs], raw.at[my_rows], gat_send.at[13], gat_recv.at[13], partner)
    swap.start()
    head, n_e = slice(0, 128), DEEP - 1
    c_out = jnp.where(first, 0, 2 * NE - DEEP)
    d_out = jnp.where(first, 0, 2 * NE - DEEP + 1)
    c_in, d_in = jnp.where(first, DEEP + NE, 0), jnp.where(first, DEEP - 1 + NE, 0)
    blocks = [
        outer(0, sizes_hbm, sizes_out, across_chip),
        outer(1, pattern_hbm, pattern_out, across_chip),
        outer(2, hc.at[pl.ds(c_out, DEEP), :, head], cbuf.at[pl.ds(c_in, DEEP), :, head], across_chip),
        outer(3, hd.at[pl.ds(d_out, n_e), :, head], dbuf.at[pl.ds(d_in, n_e), :, head], across_chip),
    ]
    for copy in blocks:
        copy.start()
    for load in (load_s, load_p, load_c, load_d):
        load.wait()
    c_from = jnp.where(first, DEEP, NE)
    d_from = jnp.where(first, DEEP - 1, NE)
    for k in range(DEEP):
        tails[0, :, REST * k : REST * (k + 1)] = cbuf[c_from + k, :, 128:NB]
    for k in range(n_e):
        tails[0, REST * k : REST * (k + 1), REST * DEEP : 128] = dbuf[d_from + k, 128:NB, 128:NB]
    blocks.append(outer(5, tails.at[0], tails.at[1], across_chip))
    blocks[-1].start()

    wts[...] = jnp.zeros_like(wts)
    load_v.wait()
    swap.wait_recv()
    edge_out = pl.ds(aligned(core * COLS, 128), EDGE)
    vectors = outer(4, raw.at[:, edge_out], edges, across_chip)
    vectors.start()

    ICI, CHIP = 0, 1

    def on_side(side, j):
        return jnp.where(first, j, NE - 1 - j) if side == ICI else jnp.where(first, NE - 1 - j, j)

    def number(table, table_out, side, j):
        if side == ICI and j < 0:
            return table_out[jnp.where(first, 2 * NE + j, -1 - j)]
        if side == ICI:
            return table[jnp.where(first, j, 2 * NE - 1 - j)]
        return table[jnp.where(first, NE - 1 - j, NE + j)]

    lanes_nb = lax.broadcasted_iota(jnp.int32, (NB, NB), 1)
    eye = (lax.broadcasted_iota(jnp.int32, (NB, NB), 0) == lanes_nb).astype(BF16)

    def coupled(i, on):
        gate = jnp.full((NB, NB), on, jnp.int32) != 0
        return jnp.where(gate, cbuf[i + DEEP].astype(F32), 0.0)

    def put_weights(i, row, value, size):
        at_row = slice(row * PAD, row * PAD + NB)
        keep = lanes_nb < size
        wts[i + DEEP - 1, at_row, 0:NB] = jnp.where(keep, value, 0.0).astype(BF16)

    own_size = [sizes[core * NE + i] for i in range(NE)]
    for i in range(NE):
        put_weights(i, 1, dbuf[i + DEEP - 1].astype(F32), own_size[i])
        if i + 1 < NE:
            pc = coupled(i, pattern[core * NE + i])
            put_weights(i, 2, nt_dot(eye, pc.astype(BF16)), own_size[i])
            put_weights(i + 1, 0, pc, own_size[i + 1])

    def side_weights(side):
        left_side = first if side == ICI else jnp.logical_not(first)
        count = number

        for j in range(-1, -DEEP, -1):
            i = on_side(side, j)
            size = count(sizes, sizes_out, side, j)
            put_weights(i, 1, dbuf[i + DEEP - 1].astype(F32), size)
        for j in range(0, -DEEP, -1):
            low = jnp.where(left_side, on_side(side, j - 1), on_side(side, j))
            on = jnp.where(
                left_side,
                count(pattern, pattern_out, side, j - 1),
                count(pattern, pattern_out, side, j),
            )
            pc = coupled(low, on)
            turned = nt_dot(eye, pc.astype(BF16))
            inner, outer_ = on_side(side, j), on_side(side, j - 1)
            size = count(sizes, sizes_out, side, j)
            value = jnp.where(left_side, pc, turned)
            put_weights_at(inner, jnp.where(left_side, 0, 2), value, size)
            if j > 1 - DEEP:
                size = count(sizes, sizes_out, side, j - 1)
                value = jnp.where(left_side, turned, pc)
                put_weights_at(outer_, jnp.where(left_side, 2, 0), value, size)

    def put_weights_at(i, row, value, size):
        keep = lanes_nb < size
        rows = pl.ds(aligned(row * PAD, PAD), NB)
        wts[i + DEEP - 1, rows, 0:NB] = jnp.where(keep, value, 0.0).astype(BF16)

    def slot(i, n=1):
        if isinstance(i, int):
            return slice(PAD * (i + DEEP), PAD * (i + DEEP + n))
        return pl.ds(aligned(PAD * (i + DEEP), PAD), PAD * n)

    lanes_pad = lax.broadcasted_iota(jnp.int32, (ROWS, PAD), 1)

    def expand(i, size, ref, column):
        off = column % 128
        x = ref[:, pl.ds(aligned(column - off, 128), PAD)].astype(F32)
        x = pltpu.roll(x, (PAD - off) % PAD, 1)
        buf[0, :, slot(i)] = jnp.where(lanes_pad < size, x, 0.0).astype(BF16)

    for i in range(NE):
        start = NB * i // 128 * 128
        x = raw[:, pl.ds(aligned(base + start, 128), PAD)].astype(F32)
        if NB * i > start:
            x = pltpu.roll(x, PAD - (NB * i - start), 1)
        buf[0, :, slot(i)] = jnp.where(lanes_pad < own_size[i], x, 0.0).astype(BF16)
    for j in range(-1, -DEEP - 1, -1):
        column = jnp.where(first, COLS + NB * (-1 - j), EDGE + NB * j)
        expand(on_side(CHIP, j), number(sizes, sizes_out, CHIP, j), raw, column)

    plan = [
        (0, None, [1]),
        (1, 0, [0, 2]),
        (0, 1, [1, 3]),
        (3, 2, [2]),
        (2, 3, [3]),
        (3, 2, [2]),
    ]

    def element(t, i, own):
        store(t, i, own, stepped(t, i))

    def stepped(t, i):
        now, prior, _ = plan[t]
        acc = jnp.dot(
            buf[now, :, slot(i - 1, 3)], wts[i + DEEP - 1], preferred_element_type=F32
        )
        shifted = acc - CENTER * buf[now, :, slot(i)].astype(F32)
        if t == 0:
            nxt = shifted * (1.0 / HALF)
        else:
            nxt = shifted * (2.0 / HALF) - buf[prior, :, slot(i)].astype(F32)
        return nxt.astype(BF16)

    def store(t, i, own, nxt):
        for target in plan[t][2]:
            if own or target < 2 or t >= DEEP:
                buf[target, :, slot(i)] = nxt

    def inside(t0):
        for k in range(DEEP):
            for i in range(k + 1, NE - k - 1):
                element(t0 + k, i, True)

    def side_steps(t0, side, k):
        level = range(k + 1 - DEEP, k + 1)
        made = [stepped(t0 + k, on_side(side, j)) for j in level]
        for j, nxt in zip(level, made):
            store(t0 + k, on_side(side, j), j >= 0 or k == DEEP - 2, nxt)

    def pass_on(k, source, target, skip, n):
        v, w = buf.at[source], buf.at[target]
        src = slot(jnp.where(first, NE - n - skip, skip), n)
        dst = slot(jnp.where(first, -n - skip, NE + skip), n)
        return outer(k, v.at[:, src], w.at[:, dst], partner)

    second = pass_on(6, 0, 2, DEEP - 2, 1)
    third = pass_on(7, 1, 3, 0, DEEP)
    packed_copy = outer(8, packed.at[0], packed.at[1], across_chip)
    sent = [(1, j) for j in range(DEEP)] + [(0, DEEP - 2)]

    def pack():
        for k, (source, j) in enumerate(sent):
            at_slot = on_side(ICI, j)
            start = aligned(PAD * (at_slot + DEEP), PAD)
            packed[0, :, 128 * k : 128 * (k + 1)] = buf[source, :, pl.ds(start, 128)]
            x = buf[source, :, pl.ds(aligned(start + 128, 128), 128)].astype(F32)
            if k:
                x = pltpu.roll(x, REST * k, 1)
            rest = x if k == 0 else rest + x
        packed[0, :, 512:640] = rest.astype(BF16)

    def unpack():
        rest = packed[1, :, 512:640].astype(F32)
        for k, (source, j) in enumerate(sent):
            start = aligned(PAD * (on_side(ICI, -1 - j) + DEEP), PAD)
            buf[source + 2, :, pl.ds(start, 128)] = packed[1, :, 128 * k : 128 * (k + 1)]
            x = pltpu.roll(rest, 128 - REST * k, 1) if k else rest
            x = jnp.where(lanes_pad[:, 0:128] < REST, x, 0.0).astype(BF16)
            buf[source + 2, :, pl.ds(aligned(start + 128, 128), 128)] = x

    def first_steps(side):
        for k in range(DEEP):
            side_steps(0, side, k)
        if side == CHIP:
            second.start()
            third.start()
        else:
            pack()
            packed_copy.start()

    pl.semaphore_wait(round1, len(links))
    tell(round2, links + [far[0], far[ZL - 2]])
    side_weights(CHIP)
    inside(0)
    first_steps(CHIP)
    pl.semaphore_wait(round2, len(links) + 2)
    tell(round3, links)
    for copy in blocks:
        copy.wait_recv()
    c_got, d_got = jnp.where(first, 0, DEEP + NE), jnp.where(first, 0, DEEP - 1 + NE)
    for k in range(DEEP):
        cbuf[c_got + k, :, 128:NB] = tails[1, :, REST * k : REST * (k + 1)]
    for k in range(n_e):
        turned = nt_dot(eye[0:128, 0:128], dbuf[d_got + k, 128:NB, 0:128])
        dbuf[d_got + k, 0:128, 128:NB] = turned.astype(BF16)
        corner = tails[1, REST * k : REST * (k + 1), REST * DEEP : 128]
        dbuf[d_got + k, 128:NB, 128:NB] = corner
    side_weights(ICI)
    vectors.wait_recv()
    for j in range(-1, -DEEP - 1, -1):
        column = jnp.where(first, EDGE + NB * j, NB * (-1 - j))
        expand(on_side(ICI, j), number(sizes, sizes_out, ICI, j), edges, column)
    first_steps(ICI)
    inside(DEEP)
    second.wait_recv()
    third.wait_recv()
    for k in range(DEEP):
        side_steps(DEEP, CHIP, k)
    packed_copy.wait_recv()
    unpack()
    for k in range(DEEP):
        side_steps(DEEP, ICI, k)

    pl.semaphore_wait(round3, len(links))

    def compact(rows):
        final = 2
        chunks = {}
        for i in range(NE):
            start = (NB * i) // 128
            off = NB * i - 128 * start
            x = buf[final, rows, slot(i)].astype(F32)
            if off:
                x = pltpu.roll(x, off, 1)
            for k in range(2):
                part = x[:, 128 * k : 128 * (k + 1)]
                at_chunk = start + k
                chunks[at_chunk] = chunks[at_chunk] + part if at_chunk in chunks else part
            done_to = COLS // 128 if i == NE - 1 else (NB * (i + 1)) // 128
            for c in sorted(chunks):
                if c < done_to:
                    fall[core, chip, rows, 128 * c : 128 * (c + 1)] = chunks.pop(c).astype(BF16)

    y_up, y_dn, y_far = (y + 1) % NY, (y + NY - 1) % NY, (y + 2) % NY
    peer_chip = (1 - xh) * NY + y
    side, far_side = xh * NY, (1 - xh) * NY
    low, high = slice(0, HALFROWS), slice(HALFROWS, ROWS)

    held = fall.at[core]

    def gather(k, g, rows, who):
        part = held.at[g] if rows is None else held.at[g, rows]
        copy = remote(part, part, gat_send.at[k], gat_recv.at[k], who)
        copy.start()
        sends.append(copy)
        return copy

    def share(k, g):
        copy = gather(14 + k, g, None, partner)
        shared.append(copy)

    sends, shared = [], []
    compact(low)
    from_dn = [gather(1, chip, low, yup)]
    compact(high)
    from_up = [gather(3, chip, high, ydn)]
    from_x = gather(0, chip, None, xpeer)
    from_dn.append(gather(2, chip, high, yup))
    from_up.append(gather(4, chip, low, ydn))

    r128 = lax.broadcasted_iota(jnp.int32, (ROWS, ROWS), 0)
    c128 = lax.broadcasted_iota(jnp.int32, (ROWS, ROWS), 1)

    def gram(which, g, o):
        strip[o, which] = nt_dot(held[g], held[side + (y + o) % NY])

    def squares(k, s, who):
        copy = remote(sqs.at[s], sqr.at[k], sq_send.at[k], sq_recv.at[k], who)
        copy.start()
        sends.append(copy)
        return copy

    def stage(k, src, dst, who):
        return remote(src, dst, red_send.at[k], red_recv.at[k], who)

    quarter = HALFROWS // XL
    row0 = pl.multiple_of(core * HALFROWS + xl * quarter, quarter)
    piece_rows = pl.ds(row0, quarter)

    def over_cores(offsets):
        copies = []
        for o in offsets:
            s1[o] = strip[o, :, other_rows, :].astype(BF16)
            copies.append(stage(o, s1.at[o], r1.at[o], partner))
            copies[-1].start()
        sends.extend(copies)
        return copies

    def to_owner(o, dx):
        col = (y + o) % NY
        j = dx * ZL + (col + ZL - zl) % ZL
        xl_ = (xl + dx) % XL
        rows = pl.ds(pl.multiple_of(xl_ * quarter, quarter), quarter)
        who = at(xl_ * ZN + zh * ZL + col, b)
        copy = remote(
            s2.at[o, :, rows], r2.at[j], red_send.at[j + 4], red_recv.at[j + 4], who
        )
        return copy, col != zl

    def to_owners(offsets, copies):
        for o, copy in zip(offsets, copies):
            copy.wait_recv()
            half = strip[o, :, my_rows, :] + r1[o].astype(F32)
            strip[o, :, my_rows, :] = half
            s2[o] = half.astype(BF16)
            crossing, _ = to_owner(o, 1)
            crossing.start()
            along, away = to_owner(o, 0)

            @pl.when(away)
            def _():
                along.start()

    gram(0, chip, 0)
    norm = jnp.sum(jnp.where(r128 == c128, strip[0, 0], 0.0), axis=0, keepdims=True)
    sqs[0] = jnp.broadcast_to(norm, (CHIPS, ROWS))
    of_core = squares(0, 0, partner)
    from_dn[0].wait_recv()
    on_up = gather(5, side + y_dn, low, yup)
    from_up[0].wait_recv()
    on_dn = gather(6, side + y_up, high, ydn)
    of_core.wait_recv()
    sqs[1] = sqs[0] + sqr[0]
    of_near = [squares(j, 1, near[j - 1]) for j in range(1, XL * ZL)]
    from_dn[1].wait_recv()
    gram(0, chip, 3)
    from_up[1].wait_recv()
    gram(0, chip, 1)
    from_x.wait_recv()
    late_dn = [gather(7, peer_chip, low, yup)]
    late_up = [gather(9, peer_chip, high, ydn)]
    late_dn.append(gather(8, peer_chip, high, yup))
    late_up.append(gather(10, peer_chip, low, ydn))
    early, last = (0, 3, 1), (2,)
    for o in early:
        gram(1, peer_chip, o)
    first_sums = over_cores(early)
    to_owners(early, first_sums)
    for copy in of_near:
        copy.wait_recv()
    norm = sqs[1]
    for j in range(1, XL * ZL):
        norm = norm + sqr[j]
    sqs[2] = norm
    of_far = [squares(7 + j, 2, far[j - 1]) for j in range(1, ZL)]
    on_up.wait_recv()
    on_dn.wait_recv()
    gram(0, chip, 2)
    gram(1, peer_chip, 2)
    last_sums = over_cores(last)
    to_owners(last, last_sums)
    share(0, chip)
    share(1, side + y_dn)
    share(2, side + y_up)
    share(3, side + y_far)
    share(4, peer_chip)

    copies = [stage(4 + j, r2.at[j], r2.at[j], near[j - 1]) for j in range(1, XL * ZL)]
    for copy in copies:
        copy.wait_recv()
    total = strip[(zl + NY - y) % NY, :, piece_rows, :]
    for j in range(1, XL * ZL):
        total = total + r2[j].astype(F32)
    s3[...] = total.astype(BF16)
    copies = [stage(11 + j, s3, r3.at[j - 1], far[j - 1]) for j in range(1, ZL)]
    for copy in copies:
        copy.start()
    sends.extend(copies)

    for copy in of_far:
        copy.wait_recv()
    norm = sqs[2]
    for j in range(1, ZL):
        norm = norm + sqr[7 + j]
    sqs[3] = norm
    norms = [squares(11 + k, 3, who) for k, who in enumerate((yup, ydn, yfar, xpeer))]
    late_dn[0].wait_recv()
    late_on_up = gather(11, far_side + y_dn, low, yup)
    late_up[0].wait_recv()
    late_on_dn = gather(12, far_side + y_up, high, ydn)
    late_dn[1].wait_recv()
    share(5, far_side + y_dn)
    late_up[1].wait_recv()
    share(6, far_side + y_up)
    for copy in norms:
        copy.wait_recv()
    for copy in copies:
        copy.wait_recv()
    for j in range(1, ZL):
        total = total + r3[j - 1].astype(F32)

    ri = lax.broadcasted_iota(jnp.int32, (quarter, ROWS), 0) + row0
    ci = lax.broadcasted_iota(jnp.int32, (quarter, ROWS), 1)
    same = ri == ci
    g = side + zl
    by_offset = [sqs[3, 0:1], sqr[12, 0:1], sqr[13, 0:1], sqr[11, 0:1]]
    sq_row = by_offset[0]
    for o in range(1, NY):
        here = jnp.full((1, ROWS), (zl + NY - y) % NY, jnp.int32) == o
        sq_row = jnp.where(here, by_offset[o], sq_row)
    scale_row = lax.rsqrt(sq_row + EPS)
    for rows_of in range(2):
        lanes = lax.rsqrt((sqs[3, 0:1] if rows_of == 0 else sqr[14, 0:1]) + EPS)
        row_scale = jnp.sum(jnp.where(same, lanes, 0.0), axis=1, keepdims=True)
        value = total[rows_of]
        ident = jnp.zeros_like(value)
        if rows_of == 0:
            unit = jnp.logical_and(same, jnp.full(same.shape, zl - y, jnp.int32) == 0)
            value = jnp.where(unit, sq_row, value)
            ident = jnp.where(unit, 1.5, 0.0)
        normed = row_scale * value * scale_row
        w = math.sqrt(total_rows) * scale_row * (ident - 0.5 * normed)
        s4[rows_of] = w.astype(BF16)

    g_cols = pl.ds(pl.multiple_of(g * ROWS, ROWS), ROWS)
    place = wfull.at[pl.ds(pl.multiple_of(xl * quarter, quarter), quarter), g_cols]
    put = pltpu.make_async_copy(s4.at[0], place, local_sem.at[4])
    put.start()
    copies = [stage(14 + j, s4.at[0], place, near[j - 1]) for j in range(1, XL * ZL)]
    copies += [stage(22 + j, s4.at[1], place, across[j]) for j in range(XL * ZL)]
    for copy in copies:
        copy.start()
    late_on_up.wait_recv()
    late_on_dn.wait_recv()
    share(7, far_side + y_far)
    for copy in shared:
        copy.wait_recv()
    near_cols = pl.ds(pl.multiple_of(side * ROWS, 128), NY * ROWS)
    far_cols = pl.ds(pl.multiple_of(far_side * ROWS, 128), NY * ROWS)
    for copy in copies[: XL * ZL - 1]:
        copy.wait_recv()
    put.wait()
    for h in range(2):
        whole = fall.at[h].reshape(BANDS, COLS)
        for k in range(COLS // PAD):
            halfsum[h, :, PAD * k : PAD * (k + 1)] = jnp.dot(
                wfull[:, near_cols],
                whole[near_cols, PAD * k : PAD * (k + 1)],
                preferred_element_type=F32,
            )
    for copy in copies[XL * ZL - 1 :]:
        copy.wait_recv()
    sends += copies

    for h in range(2):
        whole = fall.at[h].reshape(BANDS, COLS)
        for k in range(COLS // PAD):
            more = jnp.dot(
                wfull[:, far_cols],
                whole[far_cols, PAD * k : PAD * (k + 1)],
                preferred_element_type=F32,
            )
            out[:, COLS * h + PAD * k : COLS * h + PAD * (k + 1)] = (
                halfsum[h, :, PAD * k : PAD * (k + 1)] + more
            ).astype(BF16)
    for o in range(NY):
        crossing, _ = to_owner(o, 1)
        crossing.wait_send()
        along, away = to_owner(o, 0)

        @pl.when(away)
        def _():
            along.wait_send()

    for copy in sends + blocks + [vectors, swap, second, third, packed_copy]:
        copy.wait_send()


def shards(basis_sizes, coupling_pattern, h_diag, h_couple, bands):
    total_rows = h_diag.shape[0] * lax.axis_size("elem") * h_diag.shape[1]
    hbm = pl.BlockSpec(memory_space=pltpu.HBM)
    dma = pltpu.SemaphoreType.DMA
    quarter = HALFROWS // XL
    return pl.pallas_call(
        functools.partial(kernel, total_rows),
        out_shape=pltpu.VMEM(bands.shape, BF16),
        in_specs=[hbm] * 5,
        out_specs=pl.BlockSpec(memory_space=pltpu.VMEM),
        scratch_shapes=[
            pltpu.VMEM((NE + 2 * DEEP - 2, 3 * PAD, PAD), BF16),
            pltpu.VMEM((4, ROWS, PAD * (NE + 2 * DEEP)), BF16),
            pltpu.VMEM((NE + 2 * DEEP - 2, NB, NB), BF16),
            pltpu.VMEM((NE + 2 * DEEP, NB, NB), BF16),
            pltpu.VMEM((ROWS, COLS + EDGE), BF16),
            pltpu.VMEM((ROWS, EDGE), BF16),
            pltpu.VMEM((2, NB, 128), BF16),
            pltpu.VMEM((2, ROWS, 640), BF16),
            pltpu.VMEM((2, CHIPS, ROWS, COLS), BF16),
            pltpu.VMEM((NY, 2, ROWS, ROWS), F32),
            pltpu.VMEM((NY, 2, HALFROWS, ROWS), BF16),
            pltpu.VMEM((NY, 2, HALFROWS, ROWS), BF16),
            pltpu.VMEM((NY, 2, HALFROWS, ROWS), BF16),
            pltpu.VMEM((XL * ZL, 2, quarter, ROWS), BF16),
            pltpu.VMEM((2, quarter, ROWS), BF16),
            pltpu.VMEM((ZL - 1, 2, quarter, ROWS), BF16),
            pltpu.VMEM((2, quarter, ROWS), BF16),
            pltpu.VMEM((4, CHIPS, ROWS), F32),
            pltpu.VMEM((15, CHIPS, ROWS), F32),
            pltpu.VMEM((HALFROWS, BANDS), BF16),
            pltpu.VMEM((2, HALFROWS, COLS), F32),
            *[pltpu.SMEM((2 * NE,), jnp.int32)] * 4,
            *[pltpu.SemaphoreType.REGULAR] * 3,
            dma((8,)),
            dma((9,)),
            dma((9,)),
            dma((22,)),
            dma((22,)),
            dma((30,)),
            dma((30,)),
            dma((15,)),
            dma((15,)),
        ],
        compiler_params=pltpu.CompilerParams(
            collective_id=0, has_side_effects=True, vmem_limit_bytes=62000000
        ),
        name="filter_step",
    )(basis_sizes, coupling_pattern, h_diag, h_couple, bands)


def solution(mesh):
    in_specs = (
        P("elem"),
        P("elem"),
        P("elem", None, None),
        P("elem", None, None),
        P("band", "elem"),
    )
    out_specs = P("band", "elem")
    return jax.shard_map(shards, mesh=mesh, in_specs=in_specs, out_specs=out_specs, check_vma=False)
```
